32 devices in a mesh: ctx: 8 (over z, y), wsh: 4 (over x, core).
Axes of the slice: x: 2, y: 2, z: 4, core: 2. Of those that a mesh axis runs over, the one named last changes fastest.
Arguments:
- tokens: bfloat16 [4, 8192, 768], P('wsh', 'ctx'), may hold values from -6 to 6
- cotangent: bfloat16 [4, 8192, 768], P('wsh', 'ctx'), may hold values from -6 to 6
- random_blocks: int32 [4, 128, 3], P('wsh'), may hold values from 16 to 111, as said below
- query_weight: bfloat16 [768, 768], P('wsh'), may hold values from -0.21875 to 0.21875
- query_bias: bfloat16 [768], P('wsh'), may hold values from -3 to 3
- key_weight: bfloat16 [768, 768], P('wsh'), may hold values from -0.21875 to 0.21875
- value_weight: bfloat16 [768, 768], P('wsh'), may hold values from -0.21875 to 0.21875
- value_bias: bfloat16 [768], P('wsh'), may hold values from -1.1953125 to 1.1953125
- output_weight: bfloat16 [768, 768], P('wsh'), may hold values from -1.75 to 1.75
- output_bias: bfloat16 [768], P('wsh'), may hold values from -1.796875 to 1.796875
- first_gain: bfloat16 [768], P('wsh'), may hold values from 0.5 to 1.5
- first_shift: bfloat16 [768], P('wsh'), may hold values from -1.1953125 to 1.1953125
- inner_weight: bfloat16 [768, 3072], P('wsh'), may hold values from -0.21875 to 0.21875
- inner_bias: bfloat16 [3072], P('wsh'), may hold values from -1.796875 to 1.796875
- outer_weight: bfloat16 [3072, 768], P('wsh'), may hold values from -0.109375 to 0.109375
- outer_bias: bfloat16 [768], P('wsh'), may hold values from -1.796875 to 1.796875
- second_gain: bfloat16 [768], P('wsh'), may hold values from 0.5 to 1.5
- second_shift: bfloat16 [768], P('wsh'), may hold values from -1.1953125 to 1.1953125
Outputs:
- layer_output: bfloat16 [4, 8192, 768], P('wsh', 'ctx')
- tokens_grad: bfloat16 [4, 8192, 768], P('wsh', 'ctx')
- query_weight_grad: float32 [768, 768], P('wsh')
- query_bias_grad: float32 [768], P('wsh')
- key_weight_grad: float32 [768, 768], P('wsh')
- value_weight_grad: float32 [768, 768], P('wsh')
- value_bias_grad: float32 [768], P('wsh')
- output_weight_grad: float32 [768, 768], P('wsh')
- output_bias_grad: float32 [768], P('wsh')
- first_gain_grad: float32 [768], P('wsh')
- first_shift_grad: float32 [768], P('wsh')
- inner_weight_grad: float32 [768, 3072], P('wsh')
- inner_bias_grad: float32 [3072], P('wsh')
- outer_weight_grad: float32 [3072, 768], P('wsh')
- outer_bias_grad: float32 [768], P('wsh')
- second_gain_grad: float32 [768], P('wsh')
- second_shift_grad: float32 [768], P('wsh')
- stream_rms: float32 [2], replicated
The draws below stay inside these ranges and needn't reach their ends.
Inputs may be any that keep to these rules, and one draw needn't show every extreme that they name: `random_blocks`: of the 48 random blocks of one device's 16 query blocks, at most 8 lie in the 1024 tokens of any one index of ctx, and exactly 8 for some; none lies in the first or the last 1024 tokens of the sequence.
All inputs are finite; a program needn't handle non-finite values.
Results may differ from the reference program's by a relative error of at most 0.018.
Values may be sent and summed in bfloat16 or wider, within the bound.
A program may use at most 576 MiB of HBM per device.

```python
import jax
import jax.numpy as jnp
from jax import lax

D = 768
HD = 64
FF = 3072
BLK = 64
SEQS = 4
SEQ_LEN = 8192
BPD = 16
N_CTX = 8


def draw_tokens(key, part):
    position = jnp.arange(SEQ_LEN, dtype=jnp.float32) / (SEQ_LEN - 1)
    base = jax.random.truncated_normal(key, -4.0, 4.0, (SEQS, SEQ_LEN, D), jnp.float32)
    scale = (0.5 + position)[None, :, None]
    return (base * scale).astype(jnp.bfloat16)


def draw_random_blocks(key, part):
    middle = N_CTX - 2
    slots = 3 * BPD
    rows = SEQS * N_CTX
    keys = jax.random.split(key, rows + 1)
    orders = jax.vmap(lambda item: jax.random.permutation(item, middle))(keys[1:])
    columns = jnp.arange(slots, dtype=jnp.int32) % middle
    source = 1 + orders[:, columns]
    within = jax.random.randint(keys[0], (rows, slots), 0, BPD)
    blocks = source * BPD + within
    return blocks.reshape(SEQS, N_CTX * BPD, 3).astype(jnp.int32)


def block_levels(own_key, dims, shards, low, high):
    level = 1.0
    for axis_at, parts in shards:
        steps = jax.random.uniform(jax.random.fold_in(jax.random.fold_in(own_key, 6), axis_at), (parts,), jnp.float32, low / len(shards), high / len(shards))
        level = level * jnp.repeat(jnp.exp(steps), dims[axis_at] // parts).reshape((-1,) + (1,) * (len(dims) - 1 - axis_at))
    return level


def scatter_about(key, shape, spread, bound, shards=(), kind=jnp.bfloat16):
    array = jax.random.normal(key, shape, jnp.float32) * spread
    if len(shards) > 0:
        array = block_levels(key, shape, shards, -0.22, 0.18) * array
    return jnp.clip(array, min=-bound, max=bound).astype(kind)


def setup_inputs(seed: int = 0) -> dict:
    key_list = jax.random.split(jax.random.key(seed), 19)
    return {
        "tokens": draw_tokens(jax.random.fold_in(key_list[18], 71), 0),
        "cotangent": scatter_about(key_list[1], (SEQS, SEQ_LEN, D), 1.0, 6.0, ((0, 4), (1, 8))),
        "random_blocks": draw_random_blocks(jax.random.fold_in(key_list[18], 71), 0),
        "query_weight": scatter_about(key_list[3], (D, D), D ** -0.5, 0.21875, ((0, 4),)),
        "query_bias": scatter_about(key_list[4], (D,), 0.5, 3.0, ((0, 4),)),
        "key_weight": scatter_about(key_list[5], (D, D), D ** -0.5, 0.21875, ((0, 4),)),
        "value_weight": scatter_about(key_list[6], (D, D), D ** -0.5, 0.21875, ((0, 4),)),
        "value_bias": scatter_about(key_list[7], (D,), 0.2, 1.1953125, ((0, 4),)),
        "output_weight": scatter_about(key_list[8], (D, D), (D // 64) ** -0.5, 1.75, ((0, 4),)),
        "output_bias": scatter_about(key_list[9], (D,), 0.3, 1.796875, ((0, 4),)),
        "first_gain": jnp.clip(1.0 + 0.1 * jax.random.normal(key_list[10], (D,), jnp.float32), 0.5, 1.5).astype(jnp.bfloat16),
        "first_shift": scatter_about(key_list[11], (D,), 0.2, 1.1953125, ((0, 4),)),
        "inner_weight": scatter_about(key_list[12], (D, FF), D ** -0.5, 0.21875, ((0, 4),)),
        "inner_bias": scatter_about(key_list[13], (FF,), 0.3, 1.796875, ((0, 4),)),
        "outer_weight": scatter_about(key_list[14], (FF, D), FF ** -0.5, 0.109375, ((0, 4),)),
        "outer_bias": scatter_about(key_list[15], (D,), 0.3, 1.796875, ((0, 4),)),
        "second_gain": jnp.clip(1.0 + 0.1 * jax.random.normal(key_list[16], (D,), jnp.float32), 0.5, 1.5).astype(jnp.bfloat16),
        "second_shift": scatter_about(key_list[17], (D,), 0.2, 1.1953125, ((0, 4),)),
    }


EPSILON = 1e-06
NEG_FILL = -1e+30
HIGHEST_PREC = lax.Precision.HIGHEST

@jax.custom_vjp
def low(v):
    return lax.optimization_barrier(v.astype(jnp.bfloat16)).astype(jnp.float32)

@jax.custom_vjp
def low_back(v):
    return v

def low_keep(v):
    return (low(v), None)

def low_pass(kept, grad):
    return (grad,)

def back_keep(v):
    return (v, None)

def back_low(kept, grad):
    return (low(grad),)
low.defvjp(low_keep, low_pass)
low_back.defvjp(back_keep, back_low)

def matmul(left, right):
    return jnp.dot(left, right, precision=HIGHEST_PREC, preferred_element_type=jnp.float32)

def layer_norm(hidden, gain, shift):
    center = hidden - lax.optimization_barrier(jnp.mean(hidden, axis=-1, keepdims=True))
    inverse = lax.rsqrt(lax.optimization_barrier(jnp.mean(center * center, axis=-1, keepdims=True)) + EPSILON)
    return center * inverse * gain + shift

def key_table(random_rows):
    count = random_rows.shape[0]
    blocks = jnp.arange(count, dtype=jnp.int32)
    lower = jnp.maximum(blocks - 1, 0).astype(jnp.int32)
    upper = jnp.minimum(blocks + 1, count - 1).astype(jnp.int32)
    first = jnp.zeros_like(blocks)
    final = jnp.full_like(blocks, count - 1)
    table = jnp.stack([lower, blocks, upper, first, final, random_rows[:, 0], random_rows[:, 1], random_rows[:, 2]], axis=1).astype(jnp.int32)
    always = jnp.ones((count,), bool)
    usable = jnp.stack([blocks > 0, always, blocks < count - 1, always, always, always, always, always], axis=1)
    return (table, usable)

def group_attend(query_group, table_group, usable_group, key_blocks, value_blocks):
    picked_keys = key_blocks[table_group]
    picked_values = value_blocks[table_group]
    scores = jnp.einsum('gihd,gjthd->ghijt', query_group, picked_keys, precision=HIGHEST_PREC) * HD ** (-0.5)
    scores = low_back(scores)
    scores = jnp.where(usable_group[:, None, None, :, None], scores, NEG_FILL)
    flat = scores.reshape(scores.shape[:3] + (scores.shape[3] * scores.shape[4],))
    probs = low(jax.nn.softmax(flat, axis=-1)).reshape(scores.shape)
    return jnp.einsum('ghijt,gjthd->gihd', probs, picked_values, precision=HIGHEST_PREC)

def attend(queries, key_rows, value_rows, random_rows):
    length, features = queries.shape
    count = length // BLK
    head_count = features // HD
    groups = count // BPD
    table, usable = key_table(random_rows)
    key_blocks = key_rows.reshape(count, BLK, head_count, HD)
    value_blocks = value_rows.reshape(count, BLK, head_count, HD)
    stepper = jax.checkpoint(group_attend)
    query_groups = queries.reshape(groups, BPD, BLK, head_count, HD)

    def one_group(item):
        return stepper(item[0], item[1], item[2], key_blocks, value_blocks)
    outputs = lax.map(one_group, (query_groups, table.reshape(groups, BPD, 8), usable.reshape(groups, BPD, 8)))
    return outputs.reshape(length, features)

def layer(token_rows, query_weight, query_bias, key_weight, value_weight, value_bias, output_weight, output_bias, first_gain, first_shift, inner_weight, inner_bias, outer_weight, outer_bias, second_gain, second_shift, random_rows):
    queries = low(low_back(matmul(token_rows, query_weight) + query_bias))
    key_rows = low(low_back(matmul(token_rows, key_weight)))
    value_rows = low(low_back(matmul(token_rows, value_weight) + value_bias))
    mixed = low(low_back(attend(queries, key_rows, value_rows, random_rows)))
    attention = matmul(mixed, output_weight) + output_bias
    stream = token_rows + low_back(attention)
    normed = layer_norm(stream, first_gain, first_shift)
    inner = low_back(matmul(low(normed), inner_weight) + inner_bias)
    activated = low(jax.nn.gelu(inner, approximate=False))
    outer = matmul(activated, outer_weight) + outer_bias
    final = layer_norm(normed + low_back(outer), second_gain, second_shift)
    squares = jnp.stack([jnp.sum(stream * stream), jnp.sum(attention * attention)])
    return (final, squares)

def reference(tokens, cotangent, random_blocks, query_weight, query_bias, key_weight, value_weight, value_bias, output_weight, output_bias, first_gain, first_shift, inner_weight, inner_bias, outer_weight, outer_bias, second_gain, second_shift):
    weights = tuple((member.astype(jnp.float32) for member in (query_weight, query_bias, key_weight, value_weight, value_bias, output_weight, output_bias, first_gain, first_shift, inner_weight, inner_bias, outer_weight, outer_bias, second_gain, second_shift)))

    def one_sequence(carry, item):
        seq_rows, seq_grad, random_rows = item

        def forward(inputs, *params):
            return layer(inputs, *params, random_rows)
        final, pullback, squares = jax.vjp(forward, seq_rows.astype(jnp.float32), *weights, has_aux=True)
        grads = pullback(seq_grad.astype(jnp.float32))
        totals = tuple((left + right for left, right in zip(carry[0], grads[1:])))
        return ((totals, carry[1] + squares), (final.astype(jnp.bfloat16), grads[0].astype(jnp.bfloat16)))
    start = (tuple((jnp.zeros(member.shape, jnp.float32) for member in weights)), jnp.zeros((2,), jnp.float32))
    (totals, squares), (outputs, input_grads) = lax.scan(one_sequence, start, (tokens, cotangent, random_blocks))
    stream_rms = jnp.sqrt(squares / tokens.size)
    return (outputs, input_grads, totals[0], totals[1], totals[2], totals[3], totals[4], totals[5], totals[6], totals[7], totals[8], totals[9], totals[10], totals[11], totals[12], totals[13], totals[14], stream_rms)
```

```python
import functools
import math

import jax
import jax.numpy as jnp
from jax import lax
from jax.experimental import pallas as pl
from jax.experimental.pallas import tpu as pltpu
from jax.sharding import PartitionSpec as P

HD = 64
BLK = 64
PACKED = 4
LANES = PACKED * HD
LISTED = 8
EXTRA = 4

EPSILON = 1e-06
NEG_FILL = -1e30
MESH = pl.DeviceIdType.MESH
MIB = 1 << 20


def request_tables(random_rows, cycle_size, blocks_here):
    wanted = random_rows.reshape(cycle_size, 3 * blocks_here)
    source = wanted // blocks_here
    within = wanted % blocks_here
    positions = jnp.arange(wanted.shape[1])
    earlier = positions[None, :] < positions[:, None]
    same_source = source[:, :, None] == source[:, None, :]
    ranking = jnp.sum(same_source & earlier[None], axis=2, dtype=jnp.int32)
    return (source, within, ranking)


def send_slots(source, within, ranking, own_index, capacity):
    slot_ids = jnp.arange(capacity, dtype=jnp.int32)
    selected = (source[:, None, :] == own_index) & (ranking[:, None, :] == slot_ids[None, :, None])
    filled = jnp.any(selected, axis=2)
    picked = jnp.sum(jnp.where(selected, within[:, None, :], 0), axis=2, dtype=jnp.int32)
    return (filled.astype(jnp.int32), picked)


def key_slots(own_source, own_rank, blocks_here, capacity):
    block = jnp.arange(blocks_here, dtype=jnp.int32)
    left = jnp.where(block == 0, blocks_here, block - 1)
    right = jnp.where(block == blocks_here - 1, blocks_here + 1, block + 1)
    drawn = (blocks_here + EXTRA + (own_source - 1) * capacity + own_rank).reshape(blocks_here, 3)
    fixed = jnp.stack(
        [
            left,
            block,
            right,
            jnp.full_like(block, blocks_here + 2),
            jnp.full_like(block, blocks_here + 3),
        ],
        axis=1,
    )
    return jnp.concatenate([fixed, drawn], axis=1).astype(jnp.int32)


def pack_kernel(picked_ref, rows_ref, out_ref, sems):
    slots = out_ref.shape[0]

    def copy(i):
        return pltpu.make_async_copy(rows_ref.at[picked_ref[i]], out_ref.at[i], sems.at[i])

    @pl.loop(0, slots)
    def _(i):
        copy(i).start()

    @pl.loop(0, slots)
    def _(i):
        copy(i).wait()


def pack_blocks(rows, picked):
    slots = picked.shape[0]
    return pl.pallas_call(
        pack_kernel,
        out_shape=jax.ShapeDtypeStruct((slots,) + rows.shape[1:], rows.dtype),
        grid_spec=pltpu.PrefetchScalarGridSpec(
            num_scalar_prefetch=1,
            grid=(1,),
            in_specs=[pl.BlockSpec(rows.shape, lambda i, t: (0, 0, 0))],
            out_specs=pl.BlockSpec(memory_space=pl.ANY),
            scratch_shapes=[pltpu.SemaphoreType.DMA((slots,))],
        ),
        name="pack_blocks",
    )(picked, rows)


def spread_kernel(count, capacity, *refs):
    weights = (len(refs) - 2 - 1 - 9) // 2
    pack, rows = refs[:2]
    shards = refs[2 : 2 + weights]
    ext = refs[2 + weights]
    fulls = refs[3 + weights : 3 + 2 * weights]
    rand_s, rand_r, halo_s, halo_r, glob_s, glob_r, wgt_s, wgt_r, loc = refs[3 + 2 * weights :]
    blocks = rows.shape[0]
    base = blocks + EXTRA
    me = lax.axis_index("ctx")
    w = lax.axis_index("wsh")
    sib = w + 1 - 2 * (w % 2)
    far = (w + 2) % 4
    far_sib = (sib + 2) % 4
    last = count - 1
    is_source = jnp.logical_and(me >= 1, me <= last - 1)

    barrier = pltpu.get_barrier_semaphore()

    @pl.loop(1, count)
    def _(delta):
        pl.semaphore_signal(
            barrier, inc=1, device_id={"ctx": (me + delta) % count}, device_id_type=MESH
        )

    pl.semaphore_signal(barrier, inc=1, device_id={"wsh": sib}, device_id_type=MESH)
    pl.semaphore_signal(barrier, inc=1, device_id={"wsh": far}, device_id_type=MESH)
    pl.semaphore_wait(barrier, count + 1)

    def weight_copy(i, step):
        if step == 2:
            src, dst, target = fulls[i].at[far], fulls[i].at[far], sib
        else:
            src, dst, target = shards[i], fulls[i].at[w], (far, sib)[step]
        return pltpu.make_async_remote_copy(
            src_ref=src,
            dst_ref=dst,
            send_sem=wgt_s.at[i, step],
            recv_sem=wgt_r.at[i, step],
            device_id={"wsh": target},
            device_id_type=MESH,
        )

    def random_copy(dst):
        return pltpu.make_async_remote_copy(
            src_ref=pack.at[dst],
            dst_ref=ext.at[pl.ds(base + (me - 1) * capacity, capacity)],
            send_sem=rand_s.at[dst],
            recv_sem=rand_r.at[me],
            device_id={"ctx": dst},
            device_id_type=MESH,
        )

    def random_landed(source):
        return pltpu.make_async_remote_copy(
            src_ref=pack.at[source],
            dst_ref=ext.at[pl.ds(base + (source - 1) * capacity, capacity)],
            send_sem=rand_s.at[source],
            recv_sem=rand_r.at[source],
            device_id={"ctx": source},
            device_id_type=MESH,
        )

    def halo_copy(side):
        return pltpu.make_async_remote_copy(
            src_ref=rows.at[blocks - 1 if side == 0 else 0],
            dst_ref=ext.at[blocks + side],
            send_sem=halo_s.at[side],
            recv_sem=halo_r.at[side],
            device_id={"ctx": me + 1 if side == 0 else me - 1},
            device_id_type=MESH,
        )

    def global_copy(which, dst):
        return pltpu.make_async_remote_copy(
            src_ref=rows.at[0 if which == 0 else blocks - 1],
            dst_ref=ext.at[blocks + 2 + which],
            send_sem=glob_s.at[dst],
            recv_sem=glob_r.at[which],
            device_id={"ctx": dst},
            device_id_type=MESH,
        )

    for i in range(weights):
        weight_copy(i, 0).start()

    @pl.when(me < last)
    def _():
        halo_copy(0).start()

    @pl.when(me > 0)
    def _():
        halo_copy(1).start()

    @pl.when(is_source)
    def _():
        @pl.loop(1, count)
        def _(delta):
            random_copy((me + delta) % count).start()

    for which, owner in ((0, 0), (1, last)):

        @pl.when(me == owner)
        def _():
            @pl.loop(1, count)
            def _(delta):
                global_copy(which, (me + delta) % count).start()

    for i in range(weights):
        weight_copy(i, 1).start()

    def own_rows():
        return pltpu.make_async_copy(rows, ext.at[pl.ds(0, blocks)], loc.at[0])

    def own_weight(i):
        return pltpu.make_async_copy(shards[i], fulls[i].at[w], loc.at[5 + i])

    def own_random():
        return pltpu.make_async_copy(
            pack.at[me], ext.at[pl.ds(base + (me - 1) * capacity, capacity)], loc.at[1]
        )

    def own_rim(side):
        return pltpu.make_async_copy(rows.at[0], ext.at[blocks + side], loc.at[2])

    def own_global(which):
        return pltpu.make_async_copy(
            rows.at[0 if which == 0 else blocks - 1], ext.at[blocks + 2 + which], loc.at[3]
        )

    own_rows().start()
    for i in range(weights):
        own_weight(i).start()

    @pl.when(is_source)
    def _():
        own_random().start()

    for which, owner in ((0, 0), (1, last)):

        @pl.when(me == owner)
        def _():
            own_rim(which).start()
            own_global(which).start()

    for i in range(weights):
        weight_copy(i, 0).wait_recv()
        weight_copy(i, 2).start()

    own_rows().wait()
    for i in range(weights):
        own_weight(i).wait()

    @pl.when(is_source)
    def _():
        own_random().wait()

        @pl.loop(1, count)
        def _(delta):
            random_copy((me + delta) % count).wait_send()

    for which, owner in ((0, 0), (1, last)):

        @pl.when(me == owner)
        def _():
            own_rim(which).wait()
            own_global(which).wait()

            @pl.loop(1, count)
            def _(delta):
                global_copy(which, (me + delta) % count).wait_send()

        @pl.when(me != owner)
        def _():
            global_copy(which, owner).wait_recv()

    @pl.when(me < last)
    def _():
        halo_copy(0).wait_send()
        halo_copy(1).wait_recv()

    @pl.when(me > 0)
    def _():
        halo_copy(1).wait_send()
        halo_copy(0).wait_recv()

    @pl.loop(1, last)
    def _(source):
        @pl.when(source != me)
        def _():
            random_landed(source).wait_recv()

    for i in range(weights):
        for step in range(3):
            weight_copy(i, step).wait_send()
        weight_copy(i, 1).wait_recv()
        weight_copy(i, 2).wait_recv()


def spread(pack, rows, shards, count, capacity):
    blocks = rows.shape[0]
    weights = len(shards)
    slots = blocks + EXTRA + (count - 2) * capacity
    outs = pl.pallas_call(
        functools.partial(spread_kernel, count, capacity),
        out_shape=[jax.ShapeDtypeStruct((slots,) + rows.shape[1:], rows.dtype)]
        + [jax.ShapeDtypeStruct((4,) + shard.shape, shard.dtype) for shard in shards],
        in_specs=[pl.BlockSpec(memory_space=pl.ANY)] * (2 + weights),
        out_specs=[pl.BlockSpec(memory_space=pl.ANY)] * (1 + weights),
        scratch_shapes=[
            pltpu.SemaphoreType.DMA((count,)),
            pltpu.SemaphoreType.DMA((count,)),
            pltpu.SemaphoreType.DMA((2,)),
            pltpu.SemaphoreType.DMA((2,)),
            pltpu.SemaphoreType.DMA((count,)),
            pltpu.SemaphoreType.DMA((2,)),
            pltpu.SemaphoreType.DMA((weights, 3)),
            pltpu.SemaphoreType.DMA((weights, 3)),
            pltpu.SemaphoreType.DMA((5 + weights,)),
        ],
        compiler_params=pltpu.CompilerParams(collective_id=0, has_side_effects=True),
        name="spread_rows",
    )(pack, rows, *shards)
    return outs[0], outs[1:]


def return_kernel(
    count, capacity, far_grad, back, rim, glob, rand_s, rand_r, halo_s, halo_r, glob_s, glob_r, loc
):
    me = lax.axis_index("ctx")
    last = count - 1
    is_source = jnp.logical_and(me >= 1, me <= last - 1)
    barrier = pltpu.get_barrier_semaphore()

    @pl.loop(1, count)
    def _(delta):
        pl.semaphore_signal(
            barrier, inc=1, device_id={"ctx": (me + delta) % count}, device_id_type=MESH
        )

    pl.semaphore_wait(barrier, count - 1)

    def random_copy(owner, sender):
        return pltpu.make_async_remote_copy(
            src_ref=far_grad.at[pl.ds(EXTRA + (owner - 1) * capacity, capacity)],
            dst_ref=back.at[sender],
            send_sem=rand_s.at[owner],
            recv_sem=rand_r.at[sender],
            device_id={"ctx": owner},
            device_id_type=MESH,
        )

    def landed(sender):
        return pltpu.make_async_remote_copy(
            src_ref=far_grad.at[pl.ds(EXTRA, capacity)],
            dst_ref=back.at[sender],
            send_sem=rand_s.at[sender],
            recv_sem=rand_r.at[sender],
            device_id={"ctx": sender},
            device_id_type=MESH,
        )

    def halo_copy(side):
        return pltpu.make_async_remote_copy(
            src_ref=far_grad.at[side],
            dst_ref=rim.at[1 - side],
            send_sem=halo_s.at[side],
            recv_sem=halo_r.at[side],
            device_id={"ctx": me - 1 if side == 0 else me + 1},
            device_id_type=MESH,
        )

    def global_copy(which, sender):
        return pltpu.make_async_remote_copy(
            src_ref=far_grad.at[2 + which],
            dst_ref=glob.at[sender],
            send_sem=glob_s.at[which],
            recv_sem=glob_r.at[sender],
            device_id={"ctx": 0 if which == 0 else last},
            device_id_type=MESH,
        )

    @pl.when(me > 0)
    def _():
        halo_copy(0).start()
        global_copy(0, me).start()

    @pl.when(me < last)
    def _():
        halo_copy(1).start()
        global_copy(1, me).start()

    @pl.loop(1, count)
    def _(delta):
        owner = (me + delta) % count

        @pl.when(jnp.logical_and(owner >= 1, owner <= last - 1))
        def _():
            random_copy(owner, me).start()

    def own_random():
        return pltpu.make_async_copy(
            far_grad.at[pl.ds(EXTRA + (me - 1) * capacity, capacity)], back.at[me], loc.at[0]
        )

    def own_global(which):
        return pltpu.make_async_copy(far_grad.at[2 + which], glob.at[me], loc.at[1])

    @pl.when(is_source)
    def _():
        own_random().start()
        own_random().wait()

        @pl.loop(0, count)
        def _(sender):
            @pl.when(sender != me)
            def _():
                landed(sender).wait_recv()

    for which, owner in ((0, 0), (1, last)):

        @pl.when(me == owner)
        def _():
            own_global(which).start()
            own_global(which).wait()

            @pl.loop(0, count)
            def _(sender):
                @pl.when(sender != me)
                def _():
                    global_copy(which, sender).wait_recv()

    @pl.when(me > 0)
    def _():
        halo_copy(0).wait_send()
        halo_copy(1).wait_recv()
        global_copy(0, me).wait_send()

    @pl.when(me < last)
    def _():
        halo_copy(1).wait_send()
        halo_copy(0).wait_recv()
        global_copy(1, me).wait_send()

    @pl.loop(1, count)
    def _(delta):
        owner = (me + delta) % count

        @pl.when(jnp.logical_and(owner >= 1, owner <= last - 1))
        def _():
            random_copy(owner, me).wait_send()


def return_grads(far_grad, count, capacity):
    tail = far_grad.shape[1:]
    kind = far_grad.dtype
    return pl.pallas_call(
        functools.partial(return_kernel, count, capacity),
        out_shape=[
            jax.ShapeDtypeStruct((count, capacity) + tail, kind),
            jax.ShapeDtypeStruct((2,) + tail, kind),
            jax.ShapeDtypeStruct((count,) + tail, kind),
        ],
        in_specs=[pl.BlockSpec(memory_space=pl.ANY)],
        out_specs=[pl.BlockSpec(memory_space=pl.ANY)] * 3,
        scratch_shapes=[
            pltpu.SemaphoreType.DMA((count,)),
            pltpu.SemaphoreType.DMA((count,)),
            pltpu.SemaphoreType.DMA((2,)),
            pltpu.SemaphoreType.DMA((2,)),
            pltpu.SemaphoreType.DMA((2,)),
            pltpu.SemaphoreType.DMA((count,)),
            pltpu.SemaphoreType.DMA((2,)),
        ],
        compiler_params=pltpu.CompilerParams(collective_id=1, has_side_effects=True),
        name="return_grads",
    )(far_grad)


def unpack_kernel(
    capacity, picked_ref, filled_ref, edge_ref, base_ref, back_ref, rim_ref, glob_ref, out_ref, acc
):
    step = pl.program_id(0)
    blocks = base_ref.shape[0]

    @pl.when(step == 0)
    def _():
        acc[...] = base_ref[...]

        @pl.when(edge_ref[0] == 0)
        def _():
            acc[0] += rim_ref[0].astype(jnp.float32)

        @pl.when(edge_ref[1] == 0)
        def _():
            acc[blocks - 1] += rim_ref[1].astype(jnp.float32)

    for k in range(capacity):
        slot = step * capacity + k

        @pl.when(filled_ref[slot] == 1)
        def _():
            acc[picked_ref[slot]] += back_ref[0, k].astype(jnp.float32)

    for which, block in ((0, 0), (1, blocks - 1)):

        @pl.when(edge_ref[which] == 1)
        def _():
            acc[block] += glob_ref[0].astype(jnp.float32)

    @pl.when(step == pl.num_programs(0) - 1)
    def _():
        out_ref[...] = acc[...].astype(out_ref.dtype)


def unpack_grads(base, back, rim, glob, picked, filled, edge):
    count, capacity = back.shape[:2]
    blocks, block_rows, features = base.shape
    return pl.pallas_call(
        functools.partial(unpack_kernel, capacity),
        out_shape=jax.ShapeDtypeStruct(base.shape, jnp.bfloat16),
        grid_spec=pltpu.PrefetchScalarGridSpec(
            num_scalar_prefetch=3,
            grid=(count,),
            in_specs=[
                pl.BlockSpec(base.shape, lambda i, *t: (0, 0, 0)),
                pl.BlockSpec((1,) + back.shape[1:], lambda i, *t: (i, 0, 0, 0)),
                pl.BlockSpec(rim.shape, lambda i, *t: (0, 0, 0)),
                pl.BlockSpec((1, block_rows, features), lambda i, *t: (i, 0, 0)),
            ],
            out_specs=pl.BlockSpec(base.shape, lambda i, *t: (0, 0, 0)),
            scratch_shapes=[pltpu.VMEM(base.shape, jnp.float32)],
        ),
        compiler_params=pltpu.CompilerParams(vmem_limit_bytes=32 * MIB),
        name="unpack_grads",
    )(picked, filled, edge, base, back, rim, glob)


def head_mask():
    rows = lax.broadcasted_iota(jnp.int32, (LANES, LANES), 0) // HD
    columns = lax.broadcasted_iota(jnp.int32, (LANES, LANES), 1) // HD
    return rows == columns


def spread_heads(block, mask):
    tiled = jnp.concatenate([block] * PACKED, axis=0)
    return jnp.where(mask, tiled, jnp.zeros_like(tiled))


def fold_heads(square, mask):
    kept = jnp.where(mask, square, 0.0)
    total = kept[:BLK]
    for i in range(1, PACKED):
        total = total + kept[i * BLK : (i + 1) * BLK]
    return total


def listed_rows(ref, index_ref, b):
    return jnp.concatenate([ref[index_ref[b * LISTED + j]] for j in range(LISTED)], axis=0)


def nt(left, right):
    return lax.dot_general(
        left, right, (((1,), (1,)), ((), ())), preferred_element_type=jnp.float32
    )


def nn(left, right):
    return jnp.dot(left, right, preferred_element_type=jnp.float32)


def tn(left, right):
    return lax.dot_general(
        left, right, (((0,), (0,)), ((), ())), preferred_element_type=jnp.float32
    )


def mask_edges(scores, edge_ref, b, blocks):
    low = jnp.logical_and(b == 0, edge_ref[0] == 1)
    high = jnp.logical_and(b == blocks - 1, edge_ref[1] == 1)
    first = jnp.where(low, NEG_FILL, scores[:BLK])
    third = jnp.where(high, NEG_FILL, scores[2 * BLK : 3 * BLK])
    return jnp.concatenate([first, scores[BLK : 2 * BLK], third, scores[3 * BLK :]], axis=0)


def forward_kernel(index_ref, edge_ref, q_ref, k_ref, v_ref, o_ref, log_ref):
    blocks = q_ref.shape[0]
    mask = head_mask()

    @pl.loop(0, blocks)
    def _(b):
        query = spread_heads(q_ref[b] * HD**-0.5, mask)
        scores = mask_edges(nt(listed_rows(k_ref, index_ref, b), query), edge_ref, b, blocks)
        top = jnp.max(scores, axis=0, keepdims=True)
        raised = jnp.exp(scores - top)
        total = jnp.sum(raised, axis=0, keepdims=True)
        probs = (raised * (1.0 / total)).astype(jnp.bfloat16)
        log_ref[b] = top + jnp.log(total)
        mixed = tn(probs, listed_rows(v_ref, index_ref, b))
        o_ref[b] = fold_heads(mixed, mask).astype(o_ref.dtype)


def attend(queries, keys, values, index, edge):
    blocks, block_rows, features = queries.shape
    slots = keys.shape[0]
    groups = features // LANES
    column = lambda g, *t: (0, 0, g)
    return pl.pallas_call(
        forward_kernel,
        out_shape=[
            jax.ShapeDtypeStruct(queries.shape, jnp.bfloat16),
            jax.ShapeDtypeStruct((blocks, 1, features), jnp.float32),
        ],
        grid_spec=pltpu.PrefetchScalarGridSpec(
            num_scalar_prefetch=2,
            grid=(groups,),
            in_specs=[
                pl.BlockSpec((blocks, block_rows, LANES), column),
                pl.BlockSpec((slots, block_rows, LANES), column),
                pl.BlockSpec((slots, block_rows, LANES), column),
            ],
            out_specs=[
                pl.BlockSpec((blocks, block_rows, LANES), column),
                pl.BlockSpec((blocks, 1, LANES), column),
            ],
        ),
        compiler_params=pltpu.CompilerParams(vmem_limit_bytes=40 * MIB),
        name="attend",
    )(index, edge, queries, keys, values)


def backward_kernel(
    index_ref,
    edge_ref,
    q_ref,
    g_ref,
    k_ref,
    v_ref,
    log_ref,
    dq_ref,
    dk_ref,
    dv_ref,
    key_sum,
    value_sum,
):
    blocks = q_ref.shape[0]
    near = blocks + EXTRA
    mask = head_mask()
    key_sum[...] = jnp.zeros_like(key_sum)
    value_sum[...] = jnp.zeros_like(value_sum)
    dk_ref[...] = jnp.zeros_like(dk_ref)
    dv_ref[...] = jnp.zeros_like(dv_ref)

    @pl.loop(0, blocks)
    def _(b):
        query = spread_heads(q_ref[b] * HD**-0.5, mask)
        upstream = spread_heads(g_ref[b], mask)
        key_rows = listed_rows(k_ref, index_ref, b)
        scores = mask_edges(nt(key_rows, query), edge_ref, b, blocks)
        probs = jnp.exp(scores - log_ref[b])
        prob_grad = nt(listed_rows(v_ref, index_ref, b), upstream)
        delta = jnp.sum(probs * prob_grad, axis=0, keepdims=True)
        score_grad = (probs * (prob_grad - delta)).astype(jnp.bfloat16)
        value_grad = nn(probs.astype(jnp.bfloat16), upstream)
        key_grad = nn(score_grad, query)
        query_grad = fold_heads(tn(score_grad, key_rows), mask) * HD**-0.5
        dq_ref[b] = query_grad.astype(dq_ref.dtype)
        for j in range(LISTED):
            slot = index_ref[b * LISTED + j]
            piece = slice(j * BLK, (j + 1) * BLK)
            if j < 5:
                key_sum[slot] += key_grad[piece]
                value_sum[slot] += value_grad[piece]
            else:
                dk_ref[slot] = key_grad[piece].astype(dk_ref.dtype)
                dv_ref[slot] = value_grad[piece].astype(dv_ref.dtype)

    dk_ref[:near] = key_sum[...].astype(dk_ref.dtype)
    dv_ref[:near] = value_sum[...].astype(dv_ref.dtype)


def attend_back(queries, upstream, keys, values, log_total, index, edge):
    blocks, block_rows, features = queries.shape
    slots = keys.shape[0]
    groups = features // LANES
    column = lambda g, *t: (0, 0, g)
    few = pl.BlockSpec((blocks, block_rows, LANES), column)
    many = pl.BlockSpec((slots, block_rows, LANES), column)
    return pl.pallas_call(
        backward_kernel,
        out_shape=[
            jax.ShapeDtypeStruct(queries.shape, jnp.bfloat16),
            jax.ShapeDtypeStruct(keys.shape, jnp.bfloat16),
            jax.ShapeDtypeStruct(keys.shape, jnp.bfloat16),
        ],
        grid_spec=pltpu.PrefetchScalarGridSpec(
            num_scalar_prefetch=2,
            grid=(groups,),
            in_specs=[few, few, many, many, pl.BlockSpec((blocks, 1, LANES), column)],
            out_specs=[few, many, many],
            scratch_shapes=[
                pltpu.VMEM((blocks + EXTRA, block_rows, LANES), jnp.float32),
                pltpu.VMEM((blocks + EXTRA, block_rows, LANES), jnp.float32),
            ],
        ),
        compiler_params=pltpu.CompilerParams(vmem_limit_bytes=48 * MIB),
        name="attend_back",
    )(index, edge, queries, upstream, keys, values, log_total)


def layer_norm(hidden, gain, shift):
    center = hidden - jnp.mean(hidden, axis=-1, keepdims=True)
    inverse = lax.rsqrt(jnp.mean(center * center, axis=-1, keepdims=True) + EPSILON)
    normal = center * inverse
    return (normal * gain + shift, normal, inverse)


def norm_back(upstream, normal, inverse, gain):
    scaled = upstream * gain
    hidden_grad = inverse * (
        scaled
        - jnp.mean(scaled, axis=-1, keepdims=True)
        - normal * jnp.mean(scaled * normal, axis=-1, keepdims=True)
    )
    return (hidden_grad, jnp.sum(upstream * normal, axis=0), jnp.sum(upstream, axis=0))


def gelu_slope(inner):
    cumulative = 0.5 * (1.0 + jax.scipy.special.erf(inner * (1.0 / math.sqrt(2.0))))
    density = jnp.exp(-0.5 * inner * inner) * (1.0 / math.sqrt(2.0 * math.pi))
    return cumulative + inner * density


def outer_product(left, right):
    return jnp.einsum("ta,tb->ab", left, right, preferred_element_type=jnp.float32)


def back_product(upstream, weight):
    return jnp.einsum("tb,ab->ta", upstream, weight, preferred_element_type=jnp.float32)


def column_sum(upstream):
    return jnp.sum(upstream.astype(jnp.float32), axis=0)


def shards(
    tokens,
    cotangent,
    random_blocks,
    query_weight,
    query_bias,
    key_weight,
    value_weight,
    value_bias,
    output_weight,
    output_bias,
    first_gain,
    first_shift,
    inner_weight,
    inner_bias,
    outer_weight,
    outer_bias,
    second_gain,
    second_shift,
):
    token_rows = tokens[0]
    length, features = token_rows.shape
    blocks_here = length // BLK
    count = lax.axis_size("ctx")
    groups = lax.axis_size("wsh")
    own_index = lax.axis_index("ctx")
    own_group = lax.axis_index("wsh")
    capacity = (3 * blocks_here + count - 3) // (count - 2)
    part = features // groups
    inner_parts = inner_bias.shape[0] // part

    small = jnp.concatenate(
        [
            vector.reshape(-1, part)
            for vector in (
                query_bias,
                value_bias,
                output_bias,
                first_gain,
                first_shift,
                outer_bias,
                second_gain,
                second_shift,
                inner_bias,
            )
        ],
        axis=0,
    )
    small = jnp.pad(small, ((0, (-small.shape[0]) % 16), (0, (-part) % 128)))

    source, within, ranking = request_tables(random_blocks[0], count, blocks_here)
    filled, picked = send_slots(source, within, ranking, own_index, capacity)
    filled, picked = filled.reshape(-1), picked.reshape(-1)
    own_source = lax.dynamic_index_in_dim(source, own_index, 0, keepdims=False)
    own_rank = lax.dynamic_index_in_dim(ranking, own_index, 0, keepdims=False)
    index = key_slots(own_source, own_rank, blocks_here, capacity).reshape(-1)
    edge = jnp.stack([own_index == 0, own_index == count - 1]).astype(jnp.int32)

    row_blocks = token_rows.reshape(blocks_here, BLK, features)
    pack = pack_blocks(row_blocks, picked).reshape(count, capacity, BLK, features)
    ext_rows, fulls = spread(
        pack,
        row_blocks,
        (
            query_weight,
            key_weight,
            value_weight,
            output_weight,
            inner_weight,
            outer_weight,
            small,
        ),
        count,
        capacity,
    )
    full_query, full_key, full_value, full_output, full_inner, full_outer = (
        full.reshape(-1, full.shape[-1]) for full in fulls[:6]
    )
    vectors = [fulls[6][:, i, :part].reshape(-1) for i in range(8)]
    (
        full_query_bias,
        full_value_bias,
        full_output_bias,
        full_first_gain,
        full_first_shift,
        full_outer_bias,
        full_second_gain,
        full_second_shift,
    ) = vectors
    full_inner_bias = fulls[6][:, 8 : 8 + inner_parts, :part].reshape(-1)
    first_gain_f = full_first_gain.astype(jnp.float32)
    second_gain_f = full_second_gain.astype(jnp.float32)

    slots = ext_rows.shape[0]
    ext_flat = ext_rows.reshape(slots * BLK, features)
    queries_bf = (
        jnp.dot(token_rows, full_query, preferred_element_type=jnp.float32) + full_query_bias
    ).astype(jnp.bfloat16)
    keys_bf = jnp.dot(ext_flat, full_key, preferred_element_type=jnp.float32).astype(jnp.bfloat16)
    values_bf = (
        jnp.dot(ext_flat, full_value, preferred_element_type=jnp.float32) + full_value_bias
    ).astype(jnp.bfloat16)
    query_blocks = queries_bf.reshape(blocks_here, BLK, features)
    key_blocks = keys_bf.reshape(slots, BLK, features)
    value_blocks = values_bf.reshape(slots, BLK, features)
    mixed_blocks, log_total = attend(query_blocks, key_blocks, value_blocks, index, edge)
    mixed_bf = mixed_blocks.reshape(length, features)

    attention = (
        jnp.dot(mixed_bf, full_output, preferred_element_type=jnp.float32) + full_output_bias
    )
    stream = token_rows.astype(jnp.float32) + attention
    normed, first_normal, first_inverse = layer_norm(
        stream, first_gain_f, full_first_shift.astype(jnp.float32)
    )
    normed_bf = normed.astype(jnp.bfloat16)
    inner = jnp.dot(normed_bf, full_inner, preferred_element_type=jnp.float32) + full_inner_bias
    activated_bf = jax.nn.gelu(inner, approximate=False).astype(jnp.bfloat16)
    outer = jnp.dot(activated_bf, full_outer, preferred_element_type=jnp.float32) + full_outer_bias
    final, second_normal, second_inverse = layer_norm(
        normed + outer, second_gain_f, full_second_shift.astype(jnp.float32)
    )
    square_sums = jnp.stack([jnp.sum(stream * stream), jnp.sum(attention * attention)])

    output_grad = cotangent[0].astype(jnp.float32)
    second_stream_grad, second_gain_grad, second_shift_grad = norm_back(
        output_grad, second_normal, second_inverse, second_gain_f
    )
    outer_grad_bf = second_stream_grad.astype(jnp.bfloat16)
    outer_bias_grad = column_sum(outer_grad_bf)
    outer_weight_grad = outer_product(activated_bf, outer_grad_bf)
    inner_grad_bf = (back_product(outer_grad_bf, full_outer) * gelu_slope(inner)).astype(
        jnp.bfloat16
    )
    inner_bias_grad = column_sum(inner_grad_bf)
    inner_weight_grad = outer_product(normed_bf, inner_grad_bf)
    normed_grad = second_stream_grad + back_product(inner_grad_bf, full_inner)
    stream_grad, first_gain_grad, first_shift_grad = norm_back(
        normed_grad, first_normal, first_inverse, first_gain_f
    )
    attention_grad_bf = stream_grad.astype(jnp.bfloat16)
    output_bias_grad = column_sum(attention_grad_bf)
    output_weight_grad = outer_product(mixed_bf, attention_grad_bf)
    mixed_grad_bf = back_product(attention_grad_bf, full_output).astype(jnp.bfloat16)

    dq_blocks, dk_blocks, dv_blocks = attend_back(
        query_blocks,
        mixed_grad_bf.reshape(blocks_here, BLK, features),
        key_blocks,
        value_blocks,
        log_total,
        index,
        edge,
    )
    dq = dq_blocks.reshape(length, features)
    dk = dk_blocks.reshape(slots * BLK, features)
    dv = dv_blocks.reshape(slots * BLK, features)
    far_grad = (
        (back_product(dk[length:], full_key) + back_product(dv[length:], full_value))
        .astype(jnp.bfloat16)
        .reshape(slots - blocks_here, BLK, features)
    )
    back, rim, glob = return_grads(far_grad, count, capacity)
    near_grad = (
        stream_grad
        + back_product(dq, full_query)
        + back_product(dk[:length], full_key)
        + back_product(dv[:length], full_value)
    ).reshape(blocks_here, BLK, features)
    tokens_grad = unpack_grads(near_grad, back, rim, glob, picked, filled, edge)

    query_bias_grad = column_sum(dq)
    value_bias_grad = column_sum(dv)
    query_weight_grad = outer_product(token_rows, dq)
    key_weight_grad = outer_product(ext_flat, dk)
    value_weight_grad = outer_product(ext_flat, dv)

    def shared(grad):
        scattered = lax.psum_scatter(
            grad.astype(jnp.bfloat16), "wsh", scatter_dimension=0, tiled=True
        )
        return lax.psum(scattered, "ctx").astype(jnp.float32)

    vector_grads = (
        query_bias_grad,
        value_bias_grad,
        output_bias_grad,
        first_gain_grad,
        first_shift_grad,
        outer_bias_grad,
        second_gain_grad,
        second_shift_grad,
    )
    small_grads = jnp.concatenate(vector_grads + (inner_bias_grad, square_sums))
    small_sums = lax.psum(small_grads, ("ctx", "wsh"))
    element_count = count * groups * length * features
    stream_rms = jnp.sqrt(small_sums[-2:] / element_count)
    (
        query_bias_grad,
        value_bias_grad,
        output_bias_grad,
        first_gain_grad,
        first_shift_grad,
        outer_bias_grad,
        second_gain_grad,
        second_shift_grad,
    ) = (
        lax.dynamic_slice_in_dim(small_sums, i * features + own_group * part, part)
        for i in range(8)
    )
    inner_bias_grad = lax.dynamic_slice_in_dim(
        small_sums, 8 * features + own_group * inner_parts * part, inner_parts * part
    )
    return (
        final.astype(jnp.bfloat16)[None],
        tokens_grad.reshape(1, length, features),
        shared(query_weight_grad),
        query_bias_grad,
        shared(key_weight_grad),
        shared(value_weight_grad),
        value_bias_grad,
        shared(output_weight_grad),
        output_bias_grad,
        first_gain_grad,
        first_shift_grad,
        shared(inner_weight_grad),
        inner_bias_grad,
        shared(outer_weight_grad),
        outer_bias_grad,
        second_gain_grad,
        second_shift_grad,
        stream_rms,
    )


def solution(mesh):
    in_specs = (
        P("wsh", "ctx", None),
        P("wsh", "ctx", None),
        P("wsh", None, None),
        P("wsh", None),
        P("wsh"),
        P("wsh", None),
        P("wsh", None),
        P("wsh"),
        P("wsh", None),
        P("wsh"),
        P("wsh"),
        P("wsh"),
        P("wsh", None),
        P("wsh"),
        P("wsh", None),
        P("wsh"),
        P("wsh"),
        P("wsh"),
    )
    out_specs = (
        P("wsh", "ctx", None),
        P("wsh", "ctx", None),
        P("wsh", None),
        P("wsh"),
        P("wsh", None),
        P("wsh", None),
        P("wsh"),
        P("wsh", None),
        P("wsh"),
        P("wsh"),
        P("wsh"),
        P("wsh", None),
        P("wsh"),
        P("wsh", None),
        P("wsh"),
        P("wsh"),
        P("wsh"),
        P(),
    )
    return jax.shard_map(shards, mesh=mesh, in_specs=in_specs, out_specs=out_specs, check_vma=False)
```

```python
import functools
import math

import jax
import jax.numpy as jnp
from jax import lax
from jax.experimental import pallas as pl
from jax.experimental.pallas import tpu as pltpu
from jax.sharding import PartitionSpec as P

HD = 64
BLK = 64
PACKED = 4
LANES = PACKED * HD
LISTED = 8
EXTRA = 4

EPSILON = 1e-06
NEG_FILL = -1e30
MESH = pl.DeviceIdType.MESH
MIB = 1 << 20


def lasting(microseconds):
    return pl.CostEstimate(
        flops=int(microseconds * 1e9), bytes_accessed=int(microseconds * 1e6), transcendentals=0
    )


def request_tables(random_rows, cycle_size, blocks_here):
    wanted = random_rows.reshape(cycle_size, 3 * blocks_here)
    source = wanted // blocks_here
    within = wanted % blocks_here
    positions = jnp.arange(wanted.shape[1])
    earlier = positions[None, :] < positions[:, None]
    same_source = source[:, :, None] == source[:, None, :]
    ranking = jnp.sum(same_source & earlier[None], axis=2, dtype=jnp.int32)
    return (source, within, ranking)


def send_slots(source, within, ranking, own_index, capacity):
    slot_ids = jnp.arange(capacity, dtype=jnp.int32)
    selected = (source[:, None, :] == own_index) & (ranking[:, None, :] == slot_ids[None, :, None])
    filled = jnp.any(selected, axis=2)
    picked = jnp.sum(jnp.where(selected, within[:, None, :], 0), axis=2, dtype=jnp.int32)
    return (filled.astype(jnp.int32), picked)


def key_slots(own_source, own_rank, blocks_here, capacity):
    block = jnp.arange(blocks_here, dtype=jnp.int32)
    left = jnp.where(block == 0, blocks_here, block - 1)
    right = jnp.where(block == blocks_here - 1, blocks_here + 1, block + 1)
    drawn = (blocks_here + EXTRA + (own_source - 1) * capacity + own_rank).reshape(blocks_here, 3)
    fixed = jnp.stack(
        [
            left,
            block,
            right,
            jnp.full_like(block, blocks_here + 2),
            jnp.full_like(block, blocks_here + 3),
        ],
        axis=1,
    )
    return jnp.concatenate([fixed, drawn], axis=1).astype(jnp.int32)


def pack_kernel(picked_ref, rows_ref, out_ref, sems):
    slots = out_ref.shape[0]

    def copy(i):
        return pltpu.make_async_copy(rows_ref.at[picked_ref[i]], out_ref.at[i], sems.at[i])

    @pl.loop(0, slots)
    def _(i):
        copy(i).start()

    @pl.loop(0, slots)
    def _(i):
        copy(i).wait()


def pack_blocks(rows, picked):
    slots = picked.shape[0]
    return pl.pallas_call(
        pack_kernel,
        out_shape=jax.ShapeDtypeStruct((slots,) + rows.shape[1:], rows.dtype),
        grid_spec=pltpu.PrefetchScalarGridSpec(
            num_scalar_prefetch=1,
            grid=(1,),
            in_specs=[pl.BlockSpec(rows.shape, lambda i, t: (0, 0, 0))],
            out_specs=pl.BlockSpec(memory_space=pl.ANY),
            scratch_shapes=[pltpu.SemaphoreType.DMA((slots,))],
        ),
        name="pack_blocks",
    )(picked, rows)


def greet(count, groups):
    barrier = pltpu.get_barrier_semaphore()
    me = lax.axis_index("ctx")
    w = lax.axis_index("wsh")

    @pl.loop(1, count)
    def _(delta):
        pl.semaphore_signal(
            barrier, inc=1, device_id={"ctx": (me + delta) % count}, device_id_type=MESH
        )

    for delta in range(1, groups):
        pl.semaphore_signal(
            barrier, inc=1, device_id={"wsh": (w + delta) % groups}, device_id_type=MESH
        )
    pl.semaphore_wait(barrier, count + groups - 2)


def relays(count):
    return ((3, 2, (4, 6)), (4, 5, (3, 1))) if count == 8 else ()


def spread_kernel(count, capacity, *refs):
    weights = (len(refs) - 2 - 2 - 14) // 3
    pack, rows = refs[:2]
    shards = refs[2 : 2 + weights]
    ext, passing = refs[2 + weights : 4 + weights]
    fulls = refs[4 + weights : 4 + 2 * weights]
    rest = refs[4 + 2 * weights :]
    held = rest[:weights]
    rand_s, rand_r, halo_s, halo_r, glob_s, glob_r, wgt_s, wgt_r = rest[weights : weights + 8]
    pass_s, pass_r, loc_in, loc_out, own_pack, own_row = rest[weights + 8 :]
    blocks = rows.shape[0]
    base = blocks + EXTRA
    me = lax.axis_index("ctx")
    w = lax.axis_index("wsh")
    sib = w + 1 - 2 * (w % 2)
    far = (w + 2) % 4
    last = count - 1
    is_source = jnp.logical_and(me >= 1, me <= last - 1)
    routes = relays(count)
    greet(count, 4)

    def relayed(dst):
        found = me < 0
        for source, _, targets in routes:
            for target in targets:
                found = jnp.logical_or(found, jnp.logical_and(me == source, dst == target))
        return found

    def weight_copy(i, step):
        if step == 2:
            src, dst, target = fulls[i].at[far], fulls[i].at[far], sib
        else:
            src, dst, target = shards[i], fulls[i].at[w], (far, sib)[step]
        return pltpu.make_async_remote_copy(
            src_ref=src,
            dst_ref=dst,
            send_sem=wgt_s.at[i, step],
            recv_sem=wgt_r.at[i, step],
            device_id={"wsh": target},
            device_id_type=MESH,
        )

    def random_copy(dst, k):
        return pltpu.make_async_remote_copy(
            src_ref=pack.at[dst, k],
            dst_ref=ext.at[base + (me - 1) * capacity + k],
            send_sem=rand_s.at[dst, k],
            recv_sem=rand_r.at[me, k],
            device_id={"ctx": dst},
            device_id_type=MESH,
        )

    def random_landed(source, k):
        return pltpu.make_async_remote_copy(
            src_ref=pack.at[source, k],
            dst_ref=ext.at[base + (source - 1) * capacity + k],
            send_sem=rand_s.at[source, k],
            recv_sem=rand_r.at[source, k],
            device_id={"ctx": source},
            device_id_type=MESH,
        )

    def to_relay(via, r, dst, k):
        return pltpu.make_async_remote_copy(
            src_ref=pack.at[dst, k],
            dst_ref=passing.at[r, k],
            send_sem=rand_s.at[dst, k],
            recv_sem=pass_r.at[r, k],
            device_id={"ctx": via},
            device_id_type=MESH,
        )

    def from_relay(source, r, dst, k):
        return pltpu.make_async_remote_copy(
            src_ref=passing.at[r, k],
            dst_ref=ext.at[base + (source - 1) * capacity + k],
            send_sem=pass_s.at[r, k],
            recv_sem=rand_r.at[source, k],
            device_id={"ctx": dst},
            device_id_type=MESH,
        )

    def halo_copy(side):
        return pltpu.make_async_remote_copy(
            src_ref=rows.at[blocks - 1 if side == 0 else 0],
            dst_ref=ext.at[blocks + side],
            send_sem=halo_s.at[side],
            recv_sem=halo_r.at[side],
            device_id={"ctx": me + 1 if side == 0 else me - 1},
            device_id_type=MESH,
        )

    def global_copy(which, dst):
        return pltpu.make_async_remote_copy(
            src_ref=rows.at[0 if which == 0 else blocks - 1],
            dst_ref=ext.at[blocks + 2 + which],
            send_sem=glob_s.at[dst],
            recv_sem=glob_r.at[which],
            device_id={"ctx": dst},
            device_id_type=MESH,
        )

    def held_in(i):
        return pltpu.make_async_copy(shards[i], held[i], loc_in.at[2 + i])

    def held_out(i):
        return pltpu.make_async_copy(held[i], fulls[i].at[w], loc_out.at[2 + i])

    def rows_in():
        return pltpu.make_async_copy(rows, own_row, loc_in.at[0])

    def rows_out():
        return pltpu.make_async_copy(own_row, ext.at[pl.ds(0, blocks)], loc_out.at[0])

    def pack_in():
        return pltpu.make_async_copy(pack.at[me], own_pack, loc_in.at[1])

    def pack_out():
        return pltpu.make_async_copy(
            own_pack, ext.at[pl.ds(base + (me - 1) * capacity, capacity)], loc_out.at[1]
        )

    def rim_out(side):
        return pltpu.make_async_copy(own_row.at[0], ext.at[blocks + side], loc_out.at[2 + weights])

    def global_out(which):
        return pltpu.make_async_copy(
            own_row.at[0 if which == 0 else blocks - 1],
            ext.at[blocks + 2 + which],
            loc_out.at[3 + weights],
        )

    for i in range(weights):
        weight_copy(i, 0).start()
        weight_copy(i, 1).start()

    @pl.when(me < last)
    def _():
        halo_copy(0).start()

    @pl.when(me > 0)
    def _():
        halo_copy(1).start()

    for which, owner in ((0, 0), (1, last)):

        @pl.when(me == owner)
        def _():
            @pl.loop(1, count)
            def _(delta):
                global_copy(which, (me + delta) % count).start()

    for k in range(capacity):
        for source, via, targets in routes:

            @pl.when(me == source)
            def _():
                for r, target in enumerate(targets):
                    to_relay(via, r, target, k).start()

        @pl.when(is_source)
        def _():
            @pl.loop(1, count)
            def _(delta):
                dst = (me + delta) % count

                @pl.when(jnp.logical_not(relayed(dst)))
                def _():
                    random_copy(dst, k).start()

    rows_in().start()
    for i in range(weights):
        held_in(i).start()

    @pl.when(is_source)
    def _():
        pack_in().start()
        pack_in().wait()
        pack_out().start()

    rows_in().wait()
    rows_out().start()
    for which, owner in ((0, 0), (1, last)):

        @pl.when(me == owner)
        def _():
            rim_out(which).start()
            global_out(which).start()

    for i in range(weights):
        held_in(i).wait()
        held_out(i).start()

    for step in range(max(capacity, weights)):
        if step < capacity:
            for source, via, targets in routes:

                @pl.when(me == via)
                def _():
                    for r, target in enumerate(targets):
                        to_relay(via, r, target, step).wait_recv()
                        from_relay(source, r, target, step).start()

        if step < weights:
            weight_copy(step, 0).wait_recv()
            weight_copy(step, 2).start()

    rows_out().wait()
    for i in range(weights):
        held_out(i).wait()

    @pl.when(is_source)
    def _():
        pack_out().wait()

        for k in range(capacity):

            @pl.loop(1, count)
            def _(delta):
                random_copy((me + delta) % count, k).wait_send()

    for source, via, targets in routes:

        @pl.when(me == via)
        def _():
            for r, target in enumerate(targets):
                for k in range(capacity):
                    from_relay(source, r, target, k).wait_send()

    for which, owner in ((0, 0), (1, last)):

        @pl.when(me == owner)
        def _():
            rim_out(which).wait()
            global_out(which).wait()

            @pl.loop(1, count)
            def _(delta):
                global_copy(which, (me + delta) % count).wait_send()

        @pl.when(me != owner)
        def _():
            global_copy(which, owner).wait_recv()

    @pl.when(me < last)
    def _():
        halo_copy(0).wait_send()
        halo_copy(1).wait_recv()

    @pl.when(me > 0)
    def _():
        halo_copy(1).wait_send()
        halo_copy(0).wait_recv()

    for k in range(capacity):

        @pl.loop(1, last)
        def _(source):
            @pl.when(source != me)
            def _():
                random_landed(source, k).wait_recv()

    for i in range(weights):
        for step in range(3):
            weight_copy(i, step).wait_send()
        weight_copy(i, 1).wait_recv()
        weight_copy(i, 2).wait_recv()


def spread(pack, rows, shards, count, capacity):
    blocks = rows.shape[0]
    tail = rows.shape[1:]
    weights = len(shards)
    slots = blocks + EXTRA + (count - 2) * capacity
    outs = pl.pallas_call(
        functools.partial(spread_kernel, count, capacity),
        out_shape=[
            jax.ShapeDtypeStruct((slots,) + tail, rows.dtype),
            jax.ShapeDtypeStruct((2, capacity) + tail, rows.dtype),
        ]
        + [jax.ShapeDtypeStruct((4,) + shard.shape, shard.dtype) for shard in shards],
        in_specs=[pl.BlockSpec(memory_space=pl.ANY)] * (2 + weights),
        out_specs=[pl.BlockSpec(memory_space=pl.ANY)] * (2 + weights),
        scratch_shapes=[pltpu.VMEM(shard.shape, shard.dtype) for shard in shards]
        + [
            pltpu.SemaphoreType.DMA((count, capacity)),
            pltpu.SemaphoreType.DMA((count, capacity)),
            pltpu.SemaphoreType.DMA((2,)),
            pltpu.SemaphoreType.DMA((2,)),
            pltpu.SemaphoreType.DMA((count,)),
            pltpu.SemaphoreType.DMA((2,)),
            pltpu.SemaphoreType.DMA((weights, 3)),
            pltpu.SemaphoreType.DMA((weights, 3)),
            pltpu.SemaphoreType.DMA((2, capacity)),
            pltpu.SemaphoreType.DMA((2, capacity)),
            pltpu.SemaphoreType.DMA((4 + weights,)),
            pltpu.SemaphoreType.DMA((4 + weights,)),
            pltpu.VMEM((capacity,) + tail, rows.dtype),
            pltpu.VMEM(rows.shape, rows.dtype),
        ],
        compiler_params=pltpu.CompilerParams(
            collective_id=0, has_side_effects=True, vmem_limit_bytes=16 * MIB
        ),
        cost_estimate=lasting(110),
        name="spread_rows",
    )(pack, rows, *shards)
    return outs[0], outs[2:]


class Reducer:
    def __init__(self, count, grads, out, scratch):
        self.grads = grads
        self.out = out
        (
            self.own,
            self.from_sib,
            self.from_far,
            self.from_pair,
            self.chain_in,
            self.load_sem,
            self.sib_s,
            self.sib_r,
            self.far_s,
            self.far_r,
            self.pair_s,
            self.pair_r,
            self.chain_s,
            self.chain_r,
            self.wide_s,
            self.wide_r,
            self.back_s,
            self.back_r,
        ) = scratch
        self.units = out.shape[0]
        self.top = count // 2 - 1
        me = lax.axis_index("ctx")
        w = lax.axis_index("wsh")
        self.w = w
        self.me = me
        self.sib = w + 1 - 2 * (w % 2)
        self.far = (w + 2) % 4
        self.sib_far = (self.sib + 2) % 4
        self.side = me % 2
        self.level = me // 2
        self.pair = me + 1 - 2 * self.side

    def unit(self, u, quarter):
        singles = len(self.grads) - 2
        inner, outer = self.grads[-2:]
        part, features = self.out.shape[1] * self.out.shape[2], self.out.shape[3]
        if u < singles:
            return self.grads[u].at[quarter]
        u -= singles
        across = inner.shape[2] // features
        if u < across:
            return inner.at[quarter, :, pl.ds(u * features, features)]
        return outer.at[quarter, pl.ds((u - across) * part, part)]

    def load(self, u, slot):
        return pltpu.make_async_copy(
            self.unit(u, (self.w, self.far)[slot]), self.own.at[u, slot], self.load_sem.at[u, slot]
        )

    def remote(self, src, dst, send, recv, **device):
        return pltpu.make_async_remote_copy(
            src_ref=src,
            dst_ref=dst,
            send_sem=send,
            recv_sem=recv,
            device_id=device,
            device_id_type=MESH,
        )

    def to_sib(self, u, slot):
        return self.remote(
            self.unit(u, (self.sib, self.sib_far)[slot]),
            self.from_sib.at[u, slot],
            self.sib_s.at[u, slot],
            self.sib_r.at[u, slot],
            wsh=self.sib,
        )

    def to_far(self, u):
        return self.remote(
            self.own.at[u, 1],
            self.from_far.at[u],
            self.far_s.at[u],
            self.far_r.at[u],
            wsh=self.far,
        )

    def half(self, u, side):
        rows = self.out.shape[2]
        return self.own.at[u, 0, pl.ds(pl.multiple_of(side * rows, rows), rows)]

    def to_pair(self, u):
        return self.remote(
            self.half(u, 1 - self.side),
            self.from_pair.at[u],
            self.pair_s.at[u],
            self.pair_r.at[u],
            ctx=self.pair,
        )

    def toward(self, u):
        return 2 if u % 2 == 0 else -2

    def place(self, u, hop):
        return hop if u % 2 == 0 else self.top - hop

    def along(self, u):
        return self.remote(
            self.from_pair.at[u],
            self.chain_in.at[u],
            self.chain_s.at[u],
            self.chain_r.at[u],
            ctx=self.me + self.toward(u),
        )

    def widen(self, u):
        place = self.out.at[u, self.side]
        return self.remote(
            place, place, self.wide_s.at[u], self.wide_r.at[u], ctx=self.me - self.toward(u)
        )

    def give_back(self, u, side):
        place = self.out.at[u, side]
        return self.remote(place, place, self.back_s.at[u], self.back_r.at[u], ctx=self.pair)


    def begin(self, u):
        for slot in (1, 0):
            self.to_sib(u, slot).start()
            self.load(u, slot).start()

    def join_sib(self, u):
        for slot in (1, 0):
            self.load(u, slot).wait()
            self.to_sib(u, slot).wait_recv()
            self.own[u, slot] = add_bf16(self.own[u, slot], self.from_sib[u, slot])
            if slot == 1:
                self.to_far(u).start()

    def join_far(self, u):
        self.to_far(u).wait_recv()
        self.own[u, 0] = add_bf16(self.own[u, 0], self.from_far[u])
        self.to_pair(u).start()

    def join_pair(self, u):
        self.to_pair(u).wait_recv()
        self.from_pair[u] = add_bf16(self.half(u, self.side)[...], self.from_pair[u])

    def gather(self, u, hop):
        @pl.when(self.level == self.place(u, hop))
        def _():
            if hop > 0:
                self.along(u).wait_recv()
                total = add_bf16(self.from_pair[u], self.chain_in[u])
                if hop < self.top:
                    self.from_pair[u] = total
                else:
                    self.out[u, self.side] = total
            if hop < self.top:
                self.along(u).start()
            else:
                self.widen(u).start()
                self.give_back(u, self.side).start()

    def spread_out(self, u, hop):
        @pl.when(self.level == self.place(u, hop))
        def _():
            self.widen(u).wait_recv()
            if hop > 0:
                self.widen(u).start()
            self.give_back(u, self.side).start()

    def steps(self):
        return self.units + 2 * self.top + 3

    def step(self, t):
        lag = 0

        def unit(lag):
            u = t - lag
            return u if 0 <= u < self.units else None

        for stage in (self.join_sib, self.join_far, self.join_pair):
            if unit(lag) is not None:
                stage(unit(lag))
            lag += 1
        lag -= 1
        for hop in range(self.top + 1):
            if unit(lag) is not None:
                self.gather(unit(lag), hop)
            lag += 1
        for hop in range(self.top - 1, -1, -1):
            if unit(lag) is not None:
                self.spread_out(unit(lag), hop)
            lag += 1

    def finish(self):
        for u in range(self.units):
            self.give_back(u, 1 - self.side).wait_recv()
            self.give_back(u, self.side).wait_send()

            @pl.when(self.level != self.place(u, self.top))
            def _():
                self.along(u).wait_send()

            @pl.when(self.level != self.place(u, 0))
            def _():
                self.widen(u).wait_send()

            for slot in range(2):
                self.to_sib(u, slot).wait_send()
            self.to_far(u).wait_send()
            self.to_pair(u).wait_send()


def add_bf16(left, right):
    return (left.astype(jnp.float32) + right.astype(jnp.float32)).astype(jnp.bfloat16)


def unit_count(grads):
    inner, outer = grads[-2:]
    features = outer.shape[2]
    return len(grads) - 2 + inner.shape[2] // features + outer.shape[1] // (features // 4)


def reducer_shapes(grads):
    units = unit_count(grads)
    features = grads[-1].shape[2]
    part = features // 4
    dma = pltpu.SemaphoreType.DMA
    kind = jnp.bfloat16
    out = jax.ShapeDtypeStruct((units, 2, part // 2, features), kind)
    scratch = [
        pltpu.VMEM((units, 2, part, features), kind),
        pltpu.VMEM((units, 2, part, features), kind),
        pltpu.VMEM((units, part, features), kind),
        pltpu.VMEM((units, part // 2, features), kind),
        pltpu.VMEM((units, part // 2, features), kind),
        dma((units, 2)),
        dma((units, 2)),
        dma((units, 2)),
        dma((units,)),
        dma((units,)),
        dma((units,)),
        dma((units,)),
        dma((units,)),
        dma((units,)),
        dma((units,)),
        dma((units,)),
        dma((units,)),
        dma((units,)),
    ]
    return out, scratch


def return_kernel(count, capacity, weights, far_grad, small, *refs):
    grads = refs[:weights]
    back, rim, glob, small_out = refs[weights : weights + 4]
    refs = refs[weights + 4 :]
    reducer = None
    if weights:
        reducer = Reducer(count, grads, refs[0], refs[1 + 15 :])
        refs = refs[1:]
    rand_s, rand_r, halo_s, halo_r, glob_s, glob_r, loc, own_far, own_glob = refs[:9]
    group_part, ring_part, group_s, group_r, ring_s, ring_r = refs[9:15]
    me = lax.axis_index("ctx")
    w = lax.axis_index("wsh")
    last = count - 1
    groups = small.shape[0]
    is_source = jnp.logical_and(me >= 1, me <= last - 1)
    greet(count, groups)

    def random_copy(owner, sender, k):
        return pltpu.make_async_remote_copy(
            src_ref=far_grad.at[EXTRA + (owner - 1) * capacity + k],
            dst_ref=back.at[sender, k],
            send_sem=rand_s.at[owner, k],
            recv_sem=rand_r.at[sender, k],
            device_id={"ctx": owner},
            device_id_type=MESH,
        )

    def landed(sender, k):
        return pltpu.make_async_remote_copy(
            src_ref=far_grad.at[EXTRA + k],
            dst_ref=back.at[sender, k],
            send_sem=rand_s.at[sender, k],
            recv_sem=rand_r.at[sender, k],
            device_id={"ctx": sender},
            device_id_type=MESH,
        )

    def send_random(k):
        @pl.loop(1, count)
        def _(delta):
            owner = (me + delta) % count

            @pl.when(jnp.logical_and(owner >= 1, owner <= last - 1))
            def _():
                random_copy(owner, me, k).start()

    def halo_copy(side):
        return pltpu.make_async_remote_copy(
            src_ref=far_grad.at[side],
            dst_ref=rim.at[1 - side],
            send_sem=halo_s.at[side],
            recv_sem=halo_r.at[side],
            device_id={"ctx": me - 1 if side == 0 else me + 1},
            device_id_type=MESH,
        )

    def global_copy(which, sender):
        return pltpu.make_async_remote_copy(
            src_ref=far_grad.at[2 + which],
            dst_ref=glob.at[sender],
            send_sem=glob_s.at[which],
            recv_sem=glob_r.at[sender],
            device_id={"ctx": 0 if which == 0 else last},
            device_id_type=MESH,
        )

    def group_copy(target, sender):
        return pltpu.make_async_remote_copy(
            src_ref=small.at[target],
            dst_ref=group_part.at[sender],
            send_sem=group_s.at[target],
            recv_sem=group_r.at[sender],
            device_id={"wsh": target},
            device_id_type=MESH,
        )

    def ring_copy(target, sender):
        return pltpu.make_async_remote_copy(
            src_ref=ring_part.at[me],
            dst_ref=ring_part.at[sender],
            send_sem=ring_s.at[target],
            recv_sem=ring_r.at[sender],
            device_id={"ctx": target},
            device_id_type=MESH,
        )

    for delta in range(1, groups):
        group_copy((w + delta) % groups, w).start()

    @pl.when(me > 0)
    def _():
        halo_copy(0).start()
        global_copy(0, me).start()

    @pl.when(me < last)
    def _():
        halo_copy(1).start()
        global_copy(1, me).start()

    if reducer:
        for u in range(reducer.units):
            reducer.begin(u)
    else:
        for k in range(capacity):
            send_random(k)

    total = small[w]
    for delta in range(1, groups):
        sender = (w + delta) % groups
        group_copy(w, sender).wait_recv()
        total = total + group_part[sender]
    ring_part[me] = total

    @pl.loop(1, count)
    def _(delta):
        ring_copy((me + delta) % count, me).start()

    def own_random_in():
        return pltpu.make_async_copy(
            far_grad.at[pl.ds(EXTRA + (me - 1) * capacity, capacity)], own_far, loc.at[0]
        )

    def own_random_out():
        return pltpu.make_async_copy(own_far, back.at[me], loc.at[1])

    def own_global_in(which):
        return pltpu.make_async_copy(far_grad.at[2 + which], own_glob, loc.at[2])

    def own_global_out():
        return pltpu.make_async_copy(own_glob, glob.at[me], loc.at[3])

    @pl.when(is_source)
    def _():
        own_random_in().start()
        own_random_in().wait()
        own_random_out().start()
        own_random_out().wait()

    for which, owner in ((0, 0), (1, last)):

        @pl.when(me == owner)
        def _():
            own_global_in(which).start()
            own_global_in(which).wait()
            own_global_out().start()
            own_global_out().wait()

    @pl.loop(1, count)
    def _(delta):
        ring_copy(me, (me + delta) % count).wait_recv()

    small_out[...] = jnp.sum(ring_part[...], axis=0)

    if reducer:
        for t in range(reducer.steps()):
            if t < capacity:
                send_random(t)
            reducer.step(t)
        reducer.finish()

    @pl.loop(1, count)
    def _(delta):
        ring_copy((me + delta) % count, me).wait_send()

    for delta in range(1, groups):
        group_copy((w + delta) % groups, w).wait_send()

    @pl.when(is_source)
    def _():
        @pl.loop(0, count)
        def _(sender):
            @pl.when(sender != me)
            def _():
                for k in range(capacity):
                    landed(sender, k).wait_recv()

    for which, owner in ((0, 0), (1, last)):

        @pl.when(me == owner)
        def _():
            @pl.loop(0, count)
            def _(sender):
                @pl.when(sender != me)
                def _():
                    global_copy(which, sender).wait_recv()

    @pl.when(me > 0)
    def _():
        halo_copy(0).wait_send()
        halo_copy(1).wait_recv()
        global_copy(0, me).wait_send()

    @pl.when(me < last)
    def _():
        halo_copy(1).wait_send()
        halo_copy(0).wait_recv()
        global_copy(1, me).wait_send()

    @pl.loop(1, count)
    def _(delta):
        owner = (me + delta) % count

        @pl.when(jnp.logical_and(owner >= 1, owner <= last - 1))
        def _():
            for k in range(capacity):
                random_copy(owner, me, k).wait_send()


def return_grads(far_grad, small, grads, count, capacity):
    tail = far_grad.shape[1:]
    kind = far_grad.dtype
    groups = small.shape[0]
    hbm = pl.BlockSpec(memory_space=pl.ANY)
    vmem = pl.BlockSpec(memory_space=pltpu.VMEM)
    sums, sum_scratch = reducer_shapes(grads) if grads else (None, [])
    dma = pltpu.SemaphoreType.DMA
    return pl.pallas_call(
        functools.partial(return_kernel, count, capacity, len(grads)),
        out_shape=[
            jax.ShapeDtypeStruct((count, capacity) + tail, kind),
            jax.ShapeDtypeStruct((2,) + tail, kind),
            jax.ShapeDtypeStruct((count,) + tail, kind),
            jax.ShapeDtypeStruct(small.shape[1:], jnp.float32),
        ]
        + ([sums] if grads else []),
        in_specs=[hbm, vmem] + [hbm] * len(grads),
        out_specs=[hbm, hbm, hbm, vmem] + ([vmem] if grads else []),
        scratch_shapes=[
            dma((count, capacity)),
            dma((count, capacity)),
            dma((2,)),
            dma((2,)),
            dma((2,)),
            dma((count,)),
            dma((4,)),
            pltpu.VMEM((capacity,) + tail, kind),
            pltpu.VMEM(tail, kind),
            pltpu.VMEM(small.shape, jnp.float32),
            pltpu.VMEM((count,) + small.shape[1:], jnp.float32),
            dma((groups,)),
            dma((groups,)),
            dma((count,)),
            dma((count,)),
        ]
        + sum_scratch,
        compiler_params=pltpu.CompilerParams(
            collective_id=1, has_side_effects=True, vmem_limit_bytes=48 * MIB
        ),
        cost_estimate=lasting(150),
        name="return_grads",
    )(far_grad, small, *grads)


def unpack_kernel(
    capacity, picked_ref, filled_ref, edge_ref, base_ref, back_ref, rim_ref, glob_ref, out_ref, acc
):
    step = pl.program_id(0)
    blocks = base_ref.shape[0]

    @pl.when(step == 0)
    def _():
        acc[...] = base_ref[...]

        @pl.when(edge_ref[0] == 0)
        def _():
            acc[0] += rim_ref[0].astype(jnp.float32)

        @pl.when(edge_ref[1] == 0)
        def _():
            acc[blocks - 1] += rim_ref[1].astype(jnp.float32)

    for k in range(capacity):
        slot = step * capacity + k

        @pl.when(filled_ref[slot] == 1)
        def _():
            acc[picked_ref[slot]] += back_ref[0, k].astype(jnp.float32)

    for which, block in ((0, 0), (1, blocks - 1)):

        @pl.when(edge_ref[which] == 1)
        def _():
            acc[block] += glob_ref[0].astype(jnp.float32)

    @pl.when(step == pl.num_programs(0) - 1)
    def _():
        out_ref[...] = acc[...].astype(out_ref.dtype)


def unpack_grads(base, back, rim, glob, picked, filled, edge):
    count, capacity = back.shape[:2]
    blocks, block_rows, features = base.shape
    return pl.pallas_call(
        functools.partial(unpack_kernel, capacity),
        out_shape=jax.ShapeDtypeStruct(base.shape, jnp.bfloat16),
        grid_spec=pltpu.PrefetchScalarGridSpec(
            num_scalar_prefetch=3,
            grid=(count,),
            in_specs=[
                pl.BlockSpec(base.shape, lambda i, *t: (0, 0, 0)),
                pl.BlockSpec((1,) + back.shape[1:], lambda i, *t: (i, 0, 0, 0)),
                pl.BlockSpec(rim.shape, lambda i, *t: (0, 0, 0)),
                pl.BlockSpec((1, block_rows, features), lambda i, *t: (i, 0, 0)),
            ],
            out_specs=pl.BlockSpec(base.shape, lambda i, *t: (0, 0, 0)),
            scratch_shapes=[pltpu.VMEM(base.shape, jnp.float32)],
        ),
        compiler_params=pltpu.CompilerParams(vmem_limit_bytes=32 * MIB),
        name="unpack_grads",
    )(picked, filled, edge, base, back, rim, glob)


def head_mask():
    rows = lax.broadcasted_iota(jnp.int32, (LANES, LANES), 0) // HD
    columns = lax.broadcasted_iota(jnp.int32, (LANES, LANES), 1) // HD
    return rows == columns


def spread_heads(block, mask):
    tiled = jnp.concatenate([block] * PACKED, axis=0)
    return jnp.where(mask, tiled, jnp.zeros_like(tiled))


def fold_heads(square, mask):
    kept = jnp.where(mask, square, 0.0)
    total = kept[:BLK]
    for i in range(1, PACKED):
        total = total + kept[i * BLK : (i + 1) * BLK]
    return total


def listed_rows(ref, index_ref, b):
    return jnp.concatenate([ref[index_ref[b * LISTED + j]] for j in range(LISTED)], axis=0)


def nt(left, right):
    return lax.dot_general(
        left, right, (((1,), (1,)), ((), ())), preferred_element_type=jnp.float32
    )


def nn(left, right):
    return jnp.dot(left, right, preferred_element_type=jnp.float32)


def tn(left, right):
    return lax.dot_general(
        left, right, (((0,), (0,)), ((), ())), preferred_element_type=jnp.float32
    )


def mask_edges(scores, edge_ref, b, blocks):
    low = jnp.logical_and(b == 0, edge_ref[0] == 1)
    high = jnp.logical_and(b == blocks - 1, edge_ref[1] == 1)
    first = jnp.where(low, NEG_FILL, scores[:BLK])
    third = jnp.where(high, NEG_FILL, scores[2 * BLK : 3 * BLK])
    return jnp.concatenate([first, scores[BLK : 2 * BLK], third, scores[3 * BLK :]], axis=0)


def forward_kernel(index_ref, edge_ref, q_ref, k_ref, v_ref, o_ref, log_ref):
    blocks = q_ref.shape[0]
    mask = head_mask()

    @pl.loop(0, blocks)
    def _(b):
        query = spread_heads(q_ref[b] * HD**-0.5, mask)
        scores = mask_edges(nt(listed_rows(k_ref, index_ref, b), query), edge_ref, b, blocks)
        top = jnp.max(scores, axis=0, keepdims=True)
        raised = jnp.exp(scores - top)
        total = jnp.sum(raised, axis=0, keepdims=True)
        probs = (raised * (1.0 / total)).astype(jnp.bfloat16)
        log_ref[b] = top + jnp.log(total)
        mixed = tn(probs, listed_rows(v_ref, index_ref, b))
        o_ref[b] = fold_heads(mixed, mask).astype(o_ref.dtype)


def attend(queries, keys, values, index, edge):
    blocks, block_rows, features = queries.shape
    slots = keys.shape[0]
    groups = features // LANES
    column = lambda g, *t: (0, 0, g)
    return pl.pallas_call(
        forward_kernel,
        out_shape=[
            jax.ShapeDtypeStruct(queries.shape, jnp.bfloat16),
            jax.ShapeDtypeStruct((blocks, 1, features), jnp.float32),
        ],
        grid_spec=pltpu.PrefetchScalarGridSpec(
            num_scalar_prefetch=2,
            grid=(groups,),
            in_specs=[
                pl.BlockSpec((blocks, block_rows, LANES), column),
                pl.BlockSpec((slots, block_rows, LANES), column),
                pl.BlockSpec((slots, block_rows, LANES), column),
            ],
            out_specs=[
                pl.BlockSpec((blocks, block_rows, LANES), column),
                pl.BlockSpec((blocks, 1, LANES), column),
            ],
        ),
        compiler_params=pltpu.CompilerParams(vmem_limit_bytes=40 * MIB),
        cost_estimate=lasting(37),
        name="attend",
    )(index, edge, queries, keys, values)


def backward_kernel(
    index_ref,
    edge_ref,
    q_ref,
    g_ref,
    k_ref,
    v_ref,
    log_ref,
    dq_ref,
    dk_ref,
    dv_ref,
    key_sum,
    value_sum,
):
    blocks = q_ref.shape[0]
    near = blocks + EXTRA
    mask = head_mask()
    key_sum[...] = jnp.zeros_like(key_sum)
    value_sum[...] = jnp.zeros_like(value_sum)
    dk_ref[...] = jnp.zeros_like(dk_ref)
    dv_ref[...] = jnp.zeros_like(dv_ref)

    @pl.loop(0, blocks)
    def _(b):
        query = spread_heads(q_ref[b] * HD**-0.5, mask)
        upstream = spread_heads(g_ref[b], mask)
        key_rows = listed_rows(k_ref, index_ref, b)
        scores = mask_edges(nt(key_rows, query), edge_ref, b, blocks)
        probs = jnp.exp(scores - log_ref[b])
        prob_grad = nt(listed_rows(v_ref, index_ref, b), upstream)
        delta = jnp.sum(probs * prob_grad, axis=0, keepdims=True)
        score_grad = (probs * (prob_grad - delta)).astype(jnp.bfloat16)
        value_grad = nn(probs.astype(jnp.bfloat16), upstream)
        key_grad = nn(score_grad, query)
        query_grad = fold_heads(tn(score_grad, key_rows), mask) * HD**-0.5
        dq_ref[b] = query_grad.astype(dq_ref.dtype)
        for j in range(LISTED):
            slot = index_ref[b * LISTED + j]
            piece = slice(j * BLK, (j + 1) * BLK)
            if j < 5:
                key_sum[slot] += key_grad[piece]
                value_sum[slot] += value_grad[piece]
            else:
                dk_ref[slot] = key_grad[piece].astype(dk_ref.dtype)
                dv_ref[slot] = value_grad[piece].astype(dv_ref.dtype)

    dk_ref[:near] = key_sum[...].astype(dk_ref.dtype)
    dv_ref[:near] = value_sum[...].astype(dv_ref.dtype)


def attend_back(queries, upstream, keys, values, log_total, index, edge):
    blocks, block_rows, features = queries.shape
    slots = keys.shape[0]
    groups = features // LANES
    column = lambda g, *t: (0, 0, g)
    few = pl.BlockSpec((blocks, block_rows, LANES), column)
    many = pl.BlockSpec((slots, block_rows, LANES), column)
    return pl.pallas_call(
        backward_kernel,
        out_shape=[
            jax.ShapeDtypeStruct(queries.shape, jnp.bfloat16),
            jax.ShapeDtypeStruct(keys.shape, jnp.bfloat16),
            jax.ShapeDtypeStruct(keys.shape, jnp.bfloat16),
        ],
        grid_spec=pltpu.PrefetchScalarGridSpec(
            num_scalar_prefetch=2,
            grid=(groups,),
            in_specs=[few, few, many, many, pl.BlockSpec((blocks, 1, LANES), column)],
            out_specs=[few, many, many],
            scratch_shapes=[
                pltpu.VMEM((blocks + EXTRA, block_rows, LANES), jnp.float32),
                pltpu.VMEM((blocks + EXTRA, block_rows, LANES), jnp.float32),
            ],
        ),
        compiler_params=pltpu.CompilerParams(vmem_limit_bytes=48 * MIB),
        cost_estimate=lasting(44),
        name="attend_back",
    )(index, edge, queries, upstream, keys, values, log_total)


def layer_norm(hidden, gain, shift):
    center = hidden - jnp.mean(hidden, axis=-1, keepdims=True)
    inverse = lax.rsqrt(jnp.mean(center * center, axis=-1, keepdims=True) + EPSILON)
    normal = center * inverse
    return (normal * gain + shift, normal, inverse)


def norm_back(upstream, normal, inverse, gain):
    scaled = upstream * gain
    hidden_grad = inverse * (
        scaled
        - jnp.mean(scaled, axis=-1, keepdims=True)
        - normal * jnp.mean(scaled * normal, axis=-1, keepdims=True)
    )
    return (hidden_grad, jnp.sum(upstream * normal, axis=0), jnp.sum(upstream, axis=0))


def gelu_slope(inner):
    cumulative = 0.5 * (1.0 + jax.scipy.special.erf(inner * (1.0 / math.sqrt(2.0))))
    density = jnp.exp(-0.5 * inner * inner) * (1.0 / math.sqrt(2.0 * math.pi))
    return cumulative + inner * density


def outer_product(left, right):
    return jnp.einsum("ta,tb->ab", left, right, preferred_element_type=jnp.float32)


def back_product(upstream, weight):
    return jnp.einsum("tb,ab->ta", upstream, weight, preferred_element_type=jnp.float32)


def column_sum(upstream):
    return jnp.sum(upstream.astype(jnp.float32), axis=0)


def shards(
    tokens,
    cotangent,
    random_blocks,
    query_weight,
    query_bias,
    key_weight,
    value_weight,
    value_bias,
    output_weight,
    output_bias,
    first_gain,
    first_shift,
    inner_weight,
    inner_bias,
    outer_weight,
    outer_bias,
    second_gain,
    second_shift,
):
    token_rows = tokens[0]
    length, features = token_rows.shape
    blocks_here = length // BLK
    count = lax.axis_size("ctx")
    groups = lax.axis_size("wsh")
    own_index = lax.axis_index("ctx")
    capacity = (3 * blocks_here + count - 3) // (count - 2)
    part = features // groups
    inner_parts = inner_bias.shape[0] // part

    small = jnp.concatenate(
        [
            vector.reshape(-1, part)
            for vector in (
                query_bias,
                value_bias,
                output_bias,
                first_gain,
                first_shift,
                outer_bias,
                second_gain,
                second_shift,
                inner_bias,
            )
        ],
        axis=0,
    )
    small = jnp.pad(small, ((0, (-small.shape[0]) % 16), (0, (-part) % 128)))

    source, within, ranking = request_tables(random_blocks[0], count, blocks_here)
    filled, picked = send_slots(source, within, ranking, own_index, capacity)
    filled, picked = filled.reshape(-1), picked.reshape(-1)
    own_source = lax.dynamic_index_in_dim(source, own_index, 0, keepdims=False)
    own_rank = lax.dynamic_index_in_dim(ranking, own_index, 0, keepdims=False)
    index = key_slots(own_source, own_rank, blocks_here, capacity).reshape(-1)
    edge = jnp.stack([own_index == 0, own_index == count - 1]).astype(jnp.int32)

    row_blocks = token_rows.reshape(blocks_here, BLK, features)
    pack = pack_blocks(row_blocks, picked).reshape(count, capacity, BLK, features)
    ext_rows, fulls = spread(
        pack,
        row_blocks,
        (
            query_weight,
            key_weight,
            value_weight,
            output_weight,
            inner_weight,
            outer_weight,
            small,
        ),
        count,
        capacity,
    )
    full_query, full_key, full_value, full_output, full_inner, full_outer = (
        full.reshape(-1, full.shape[-1]) for full in fulls[:6]
    )
    vectors = [fulls[6][:, i, :part].reshape(-1) for i in range(8)]
    (
        full_query_bias,
        full_value_bias,
        full_output_bias,
        full_first_gain,
        full_first_shift,
        full_outer_bias,
        full_second_gain,
        full_second_shift,
    ) = vectors
    full_inner_bias = fulls[6][:, 8 : 8 + inner_parts, :part].reshape(-1)
    first_gain_f = full_first_gain.astype(jnp.float32)
    second_gain_f = full_second_gain.astype(jnp.float32)

    slots = ext_rows.shape[0]
    ext_flat = ext_rows.reshape(slots * BLK, features)
    queries_bf = (
        jnp.dot(token_rows, full_query, preferred_element_type=jnp.float32) + full_query_bias
    ).astype(jnp.bfloat16)
    keys_bf = jnp.dot(ext_flat, full_key, preferred_element_type=jnp.float32).astype(jnp.bfloat16)
    values_bf = (
        jnp.dot(ext_flat, full_value, preferred_element_type=jnp.float32) + full_value_bias
    ).astype(jnp.bfloat16)
    query_blocks = queries_bf.reshape(blocks_here, BLK, features)
    key_blocks = keys_bf.reshape(slots, BLK, features)
    value_blocks = values_bf.reshape(slots, BLK, features)
    mixed_blocks, log_total = attend(query_blocks, key_blocks, value_blocks, index, edge)
    mixed_bf = mixed_blocks.reshape(length, features)

    attention = (
        jnp.dot(mixed_bf, full_output, preferred_element_type=jnp.float32) + full_output_bias
    )
    stream = token_rows.astype(jnp.float32) + attention
    normed, first_normal, first_inverse = layer_norm(
        stream, first_gain_f, full_first_shift.astype(jnp.float32)
    )
    normed_bf = normed.astype(jnp.bfloat16)
    inner = jnp.dot(normed_bf, full_inner, preferred_element_type=jnp.float32) + full_inner_bias
    activated_bf = jax.nn.gelu(inner, approximate=False).astype(jnp.bfloat16)
    outer = jnp.dot(activated_bf, full_outer, preferred_element_type=jnp.float32) + full_outer_bias
    final, second_normal, second_inverse = layer_norm(
        normed + outer, second_gain_f, full_second_shift.astype(jnp.float32)
    )
    square_sums = jnp.stack([jnp.sum(stream * stream), jnp.sum(attention * attention)])

    output_grad = cotangent[0].astype(jnp.float32)
    second_stream_grad, second_gain_grad, second_shift_grad = norm_back(
        output_grad, second_normal, second_inverse, second_gain_f
    )
    outer_grad_bf = second_stream_grad.astype(jnp.bfloat16)
    outer_bias_grad = column_sum(outer_grad_bf)
    outer_weight_grad = outer_product(activated_bf, outer_grad_bf)
    inner_grad_bf = (back_product(outer_grad_bf, full_outer) * gelu_slope(inner)).astype(
        jnp.bfloat16
    )
    inner_bias_grad = column_sum(inner_grad_bf)
    inner_weight_grad = outer_product(normed_bf, inner_grad_bf)
    normed_grad = second_stream_grad + back_product(inner_grad_bf, full_inner)
    stream_grad, first_gain_grad, first_shift_grad = norm_back(
        normed_grad, first_normal, first_inverse, first_gain_f
    )
    attention_grad_bf = stream_grad.astype(jnp.bfloat16)
    output_bias_grad = column_sum(attention_grad_bf)
    output_weight_grad = outer_product(mixed_bf, attention_grad_bf)
    mixed_grad_bf = back_product(attention_grad_bf, full_output).astype(jnp.bfloat16)

    dq_blocks, dk_blocks, dv_blocks = attend_back(
        query_blocks,
        mixed_grad_bf.reshape(blocks_here, BLK, features),
        key_blocks,
        value_blocks,
        log_total,
        index,
        edge,
    )
    dq = dq_blocks.reshape(length, features)
    dk = dk_blocks.reshape(slots * BLK, features)
    dv = dv_blocks.reshape(slots * BLK, features)
    far_grad = (
        (back_product(dk[length:], full_key) + back_product(dv[length:], full_value))
        .astype(jnp.bfloat16)
        .reshape(slots - blocks_here, BLK, features)
    )
    query_bias_grad = column_sum(dq)
    value_bias_grad = column_sum(dv)
    weight_grads = tuple(
        grad.astype(jnp.bfloat16).reshape(groups, -1, grad.shape[-1])
        for grad in (
            outer_product(token_rows, dq),
            outer_product(ext_flat, dk),
            outer_product(ext_flat, dv),
            output_weight_grad,
            inner_weight_grad,
            outer_weight_grad,
        )
    )
    vector_grads = (
        query_bias_grad,
        value_bias_grad,
        output_bias_grad,
        first_gain_grad,
        first_shift_grad,
        outer_bias_grad,
        second_gain_grad,
        second_shift_grad,
    )
    small_grads = jnp.concatenate(
        [vector.reshape(groups, 1, part) for vector in vector_grads]
        + [
            inner_bias_grad.reshape(groups, inner_parts, part),
            jnp.broadcast_to(
                jnp.pad(square_sums, (0, part - 2)).reshape(1, 1, part), (groups, 1, part)
            ),
        ],
        axis=1,
    )
    small_grads = jnp.pad(
        small_grads, ((0, 0), (0, (-small_grads.shape[1]) % 8), (0, (-part) % 128))
    )
    chained = count == 8
    back, rim, glob, small_sums, *chain_sums = return_grads(
        far_grad, small_grads, weight_grads if chained else (), count, capacity
    )
    near_grad = (
        stream_grad
        + back_product(dq, full_query)
        + back_product(dk[:length], full_key)
        + back_product(dv[:length], full_value)
    ).reshape(blocks_here, BLK, features)
    tokens_grad = unpack_grads(near_grad, back, rim, glob, picked, filled, edge)

    if chained:
        units = chain_sums[0].reshape(-1, part, features).astype(jnp.float32)
        across = full_inner.shape[1] // features
        sums = [units[i] for i in range(4)] + [
            jnp.concatenate([units[4 + i] for i in range(across)], axis=1),
            units[4 + across :].reshape(-1, features),
        ]
    else:
        sums = lax.psum(
            tuple(
                lax.psum_scatter(
                    grad.reshape(-1, grad.shape[-1]), "wsh", scatter_dimension=0, tiled=True
                )
                for grad in weight_grads
            ),
            "ctx",
        )
        sums = [total.astype(jnp.float32) for total in sums]
    element_count = count * groups * length * features
    stream_rms = jnp.sqrt(small_sums[8 + inner_parts, :2] / element_count)
    (
        query_bias_grad,
        value_bias_grad,
        output_bias_grad,
        first_gain_grad,
        first_shift_grad,
        outer_bias_grad,
        second_gain_grad,
        second_shift_grad,
    ) = (small_sums[i, :part] for i in range(8))
    inner_bias_grad = small_sums[8 : 8 + inner_parts, :part].reshape(-1)
    query_weight_sum, key_weight_sum, value_weight_sum, output_weight_sum = sums[:4]
    return (
        final.astype(jnp.bfloat16)[None],
        tokens_grad.reshape(1, length, features),
        query_weight_sum,
        query_bias_grad,
        key_weight_sum,
        value_weight_sum,
        value_bias_grad,
        output_weight_sum,
        output_bias_grad,
        first_gain_grad,
        first_shift_grad,
        sums[4],
        inner_bias_grad,
        sums[5],
        outer_bias_grad,
        second_gain_grad,
        second_shift_grad,
        stream_rms,
    )


def solution(mesh):
    in_specs = (
        P("wsh", "ctx", None),
        P("wsh", "ctx", None),
        P("wsh", None, None),
        P("wsh", None),
        P("wsh"),
        P("wsh", None),
        P("wsh", None),
        P("wsh"),
        P("wsh", None),
        P("wsh"),
        P("wsh"),
        P("wsh"),
        P("wsh", None),
        P("wsh"),
        P("wsh", None),
        P("wsh"),
        P("wsh"),
        P("wsh"),
    )
    out_specs = (
        P("wsh", "ctx", None),
        P("wsh", "ctx", None),
        P("wsh", None),
        P("wsh"),
        P("wsh", None),
        P("wsh", None),
        P("wsh"),
        P("wsh", None),
        P("wsh"),
        P("wsh"),
        P("wsh"),
        P("wsh", None),
        P("wsh"),
        P("wsh", None),
        P("wsh"),
        P("wsh"),
        P("wsh"),
        P(),
    )
    return jax.shard_map(shards, mesh=mesh, in_specs=in_specs, out_specs=out_specs, check_vma=False)
```

```python
import functools
import math

import jax
import jax.numpy as jnp
from jax import lax
from jax.experimental import pallas as pl
from jax.experimental.pallas import tpu as pltpu
from jax.sharding import PartitionSpec as P

HD = 64
BLK = 64
PACKED = 4
LANES = PACKED * HD
LISTED = 8
EXTRA = 4

EPSILON = 1e-06
NEG_FILL = -1e30
MESH = pl.DeviceIdType.MESH
MIB = 1 << 20
MID_ROWS = 256
MID_CHUNK = 768


def lasting(microseconds):
    return pl.CostEstimate(
        flops=int(microseconds * 1e9), bytes_accessed=int(microseconds * 1e6), transcendentals=0
    )


def request_tables(random_rows, cycle_size, blocks_here):
    wanted = random_rows.reshape(cycle_size, 3 * blocks_here)
    source = wanted // blocks_here
    within = wanted % blocks_here
    positions = jnp.arange(wanted.shape[1])
    earlier = positions[None, :] < positions[:, None]
    same_source = source[:, :, None] == source[:, None, :]
    ranking = jnp.sum(same_source & earlier[None], axis=2, dtype=jnp.int32)
    return (source, within, ranking)


def send_slots(source, within, ranking, own_index, capacity):
    slot_ids = jnp.arange(capacity, dtype=jnp.int32)
    selected = (source[:, None, :] == own_index) & (ranking[:, None, :] == slot_ids[None, :, None])
    filled = jnp.any(selected, axis=2)
    picked = jnp.sum(jnp.where(selected, within[:, None, :], 0), axis=2, dtype=jnp.int32)
    return (filled.astype(jnp.int32), picked)


def key_slots(own_source, own_rank, blocks_here, capacity):
    block = jnp.arange(blocks_here, dtype=jnp.int32)
    left = jnp.where(block == 0, blocks_here, block - 1)
    right = jnp.where(block == blocks_here - 1, blocks_here + 1, block + 1)
    drawn = (blocks_here + EXTRA + (own_source - 1) * capacity + own_rank).reshape(blocks_here, 3)
    fixed = jnp.stack(
        [
            left,
            block,
            right,
            jnp.full_like(block, blocks_here + 2),
            jnp.full_like(block, blocks_here + 3),
        ],
        axis=1,
    )
    return jnp.concatenate([fixed, drawn], axis=1).astype(jnp.int32)


def pack_kernel(picked_ref, rows_ref, out_ref, sems):
    slots = out_ref.shape[0]

    def copy(i):
        return pltpu.make_async_copy(rows_ref.at[picked_ref[i]], out_ref.at[i], sems.at[i])

    @pl.loop(0, slots)
    def _(i):
        copy(i).start()

    @pl.loop(0, slots)
    def _(i):
        copy(i).wait()


def pack_blocks(rows, picked):
    slots = picked.shape[0]
    return pl.pallas_call(
        pack_kernel,
        out_shape=jax.ShapeDtypeStruct((slots,) + rows.shape[1:], rows.dtype),
        grid_spec=pltpu.PrefetchScalarGridSpec(
            num_scalar_prefetch=1,
            grid=(1,),
            in_specs=[pl.BlockSpec(rows.shape, lambda i, t: (0, 0, 0))],
            out_specs=pl.BlockSpec(memory_space=pl.ANY),
            scratch_shapes=[pltpu.SemaphoreType.DMA((slots,))],
        ),
        name="pack_blocks",
    )(picked, rows)


def greet(count, groups):
    barrier = pltpu.get_barrier_semaphore()
    me = lax.axis_index("ctx")
    w = lax.axis_index("wsh")

    @pl.loop(1, count)
    def _(delta):
        pl.semaphore_signal(
            barrier, inc=1, device_id={"ctx": (me + delta) % count}, device_id_type=MESH
        )

    for delta in range(1, groups):
        pl.semaphore_signal(
            barrier, inc=1, device_id={"wsh": (w + delta) % groups}, device_id_type=MESH
        )
    pl.semaphore_wait(barrier, count + groups - 2)


def relays(count):
    return ((3, 2, (4, 6)), (4, 5, (3, 1))) if count == 8 else ()


def spread_kernel(count, capacity, *refs):
    weights = (len(refs) - 2 - 2 - 14) // 3
    pack, rows = refs[:2]
    shards = refs[2 : 2 + weights]
    ext, passing = refs[2 + weights : 4 + weights]
    fulls = refs[4 + weights : 4 + 2 * weights]
    rest = refs[4 + 2 * weights :]
    held = rest[:weights]
    rand_s, rand_r, halo_s, halo_r, glob_s, glob_r, wgt_s, wgt_r = rest[weights : weights + 8]
    pass_s, pass_r, loc_in, loc_out, own_pack, own_row = rest[weights + 8 :]
    blocks = rows.shape[0]
    base = blocks + EXTRA
    me = lax.axis_index("ctx")
    w = lax.axis_index("wsh")
    sib = w + 1 - 2 * (w % 2)
    far = (w + 2) % 4
    last = count - 1
    is_source = jnp.logical_and(me >= 1, me <= last - 1)
    routes = relays(count)
    greet(count, 4)

    def relayed(dst):
        found = me < 0
        for source, _, targets in routes:
            for target in targets:
                found = jnp.logical_or(found, jnp.logical_and(me == source, dst == target))
        return found

    def weight_copy(i, step):
        if step == 2:
            src, dst, target = fulls[i].at[far], fulls[i].at[far], sib
        else:
            src, dst, target = shards[i], fulls[i].at[w], (far, sib)[step]
        return pltpu.make_async_remote_copy(
            src_ref=src,
            dst_ref=dst,
            send_sem=wgt_s.at[i, step],
            recv_sem=wgt_r.at[i, step],
            device_id={"wsh": target},
            device_id_type=MESH,
        )

    def random_copy(dst, k):
        return pltpu.make_async_remote_copy(
            src_ref=pack.at[dst, k],
            dst_ref=ext.at[base + (me - 1) * capacity + k],
            send_sem=rand_s.at[dst, k],
            recv_sem=rand_r.at[me, k],
            device_id={"ctx": dst},
            device_id_type=MESH,
        )

    def random_landed(source, k):
        return pltpu.make_async_remote_copy(
            src_ref=pack.at[source, k],
            dst_ref=ext.at[base + (source - 1) * capacity + k],
            send_sem=rand_s.at[source, k],
            recv_sem=rand_r.at[source, k],
            device_id={"ctx": source},
            device_id_type=MESH,
        )

    def to_relay(via, r, dst, k):
        return pltpu.make_async_remote_copy(
            src_ref=pack.at[dst, k],
            dst_ref=passing.at[r, k],
            send_sem=rand_s.at[dst, k],
            recv_sem=pass_r.at[r, k],
            device_id={"ctx": via},
            device_id_type=MESH,
        )

    def from_relay(source, r, dst, k):
        return pltpu.make_async_remote_copy(
            src_ref=passing.at[r, k],
            dst_ref=ext.at[base + (source - 1) * capacity + k],
            send_sem=pass_s.at[r, k],
            recv_sem=rand_r.at[source, k],
            device_id={"ctx": dst},
            device_id_type=MESH,
        )

    def halo_copy(side):
        return pltpu.make_async_remote_copy(
            src_ref=rows.at[blocks - 1 if side == 0 else 0],
            dst_ref=ext.at[blocks + side],
            send_sem=halo_s.at[side],
            recv_sem=halo_r.at[side],
            device_id={"ctx": me + 1 if side == 0 else me - 1},
            device_id_type=MESH,
        )

    def global_copy(which, dst):
        return pltpu.make_async_remote_copy(
            src_ref=rows.at[0 if which == 0 else blocks - 1],
            dst_ref=ext.at[blocks + 2 + which],
            send_sem=glob_s.at[dst],
            recv_sem=glob_r.at[which],
            device_id={"ctx": dst},
            device_id_type=MESH,
        )

    def held_in(i):
        return pltpu.make_async_copy(shards[i], held[i], loc_in.at[2 + i])

    def held_out(i):
        return pltpu.make_async_copy(held[i], fulls[i].at[w], loc_out.at[2 + i])

    def rows_in():
        return pltpu.make_async_copy(rows, own_row, loc_in.at[0])

    def rows_out():
        return pltpu.make_async_copy(own_row, ext.at[pl.ds(0, blocks)], loc_out.at[0])

    def pack_in():
        return pltpu.make_async_copy(pack.at[me], own_pack, loc_in.at[1])

    def pack_out():
        return pltpu.make_async_copy(
            own_pack, ext.at[pl.ds(base + (me - 1) * capacity, capacity)], loc_out.at[1]
        )

    def rim_out(side):
        return pltpu.make_async_copy(own_row.at[0], ext.at[blocks + side], loc_out.at[2 + weights])

    def global_out(which):
        return pltpu.make_async_copy(
            own_row.at[0 if which == 0 else blocks - 1],
            ext.at[blocks + 2 + which],
            loc_out.at[3 + weights],
        )

    for i in range(weights):
        weight_copy(i, 0).start()
        weight_copy(i, 1).start()

    @pl.when(me < last)
    def _():
        halo_copy(0).start()

    @pl.when(me > 0)
    def _():
        halo_copy(1).start()

    for which, owner in ((0, 0), (1, last)):

        @pl.when(me == owner)
        def _():
            @pl.loop(1, count)
            def _(delta):
                global_copy(which, (me + delta) % count).start()

    for k in range(capacity):
        for source, via, targets in routes:

            @pl.when(me == source)
            def _():
                for r, target in enumerate(targets):
                    to_relay(via, r, target, k).start()

        @pl.when(is_source)
        def _():
            @pl.loop(1, count)
            def _(delta):
                dst = (me + delta) % count

                @pl.when(jnp.logical_not(relayed(dst)))
                def _():
                    random_copy(dst, k).start()

    rows_in().start()
    for i in range(weights):
        held_in(i).start()

    @pl.when(is_source)
    def _():
        pack_in().start()
        pack_in().wait()
        pack_out().start()

    rows_in().wait()
    rows_out().start()
    for which, owner in ((0, 0), (1, last)):

        @pl.when(me == owner)
        def _():
            rim_out(which).start()
            global_out(which).start()

    for i in range(weights):
        held_in(i).wait()
        held_out(i).start()

    for step in range(max(capacity, weights)):
        if step < capacity:
            for source, via, targets in routes:

                @pl.when(me == via)
                def _():
                    for r, target in enumerate(targets):
                        to_relay(via, r, target, step).wait_recv()
                        from_relay(source, r, target, step).start()

        if step < weights:
            weight_copy(step, 0).wait_recv()
            weight_copy(step, 2).start()

    rows_out().wait()
    for i in range(weights):
        held_out(i).wait()

    @pl.when(is_source)
    def _():
        pack_out().wait()

        for k in range(capacity):

            @pl.loop(1, count)
            def _(delta):
                random_copy((me + delta) % count, k).wait_send()

    for source, via, targets in routes:

        @pl.when(me == via)
        def _():
            for r, target in enumerate(targets):
                for k in range(capacity):
                    from_relay(source, r, target, k).wait_send()

    for which, owner in ((0, 0), (1, last)):

        @pl.when(me == owner)
        def _():
            rim_out(which).wait()
            global_out(which).wait()

            @pl.loop(1, count)
            def _(delta):
                global_copy(which, (me + delta) % count).wait_send()

        @pl.when(me != owner)
        def _():
            global_copy(which, owner).wait_recv()

    @pl.when(me < last)
    def _():
        halo_copy(0).wait_send()
        halo_copy(1).wait_recv()

    @pl.when(me > 0)
    def _():
        halo_copy(1).wait_send()
        halo_copy(0).wait_recv()

    for k in range(capacity):

        @pl.loop(1, last)
        def _(source):
            @pl.when(source != me)
            def _():
                random_landed(source, k).wait_recv()

    for i in range(weights):
        for step in range(3):
            weight_copy(i, step).wait_send()
        weight_copy(i, 1).wait_recv()
        weight_copy(i, 2).wait_recv()


def spread(pack, rows, shards, count, capacity):
    blocks = rows.shape[0]
    tail = rows.shape[1:]
    weights = len(shards)
    slots = blocks + EXTRA + (count - 2) * capacity
    outs = pl.pallas_call(
        functools.partial(spread_kernel, count, capacity),
        out_shape=[
            jax.ShapeDtypeStruct((slots,) + tail, rows.dtype),
            jax.ShapeDtypeStruct((2, capacity) + tail, rows.dtype),
        ]
        + [jax.ShapeDtypeStruct((4,) + shard.shape, shard.dtype) for shard in shards],
        in_specs=[pl.BlockSpec(memory_space=pl.ANY)] * (2 + weights),
        out_specs=[pl.BlockSpec(memory_space=pl.ANY)] * (2 + weights),
        scratch_shapes=[pltpu.VMEM(shard.shape, shard.dtype) for shard in shards]
        + [
            pltpu.SemaphoreType.DMA((count, capacity)),
            pltpu.SemaphoreType.DMA((count, capacity)),
            pltpu.SemaphoreType.DMA((2,)),
            pltpu.SemaphoreType.DMA((2,)),
            pltpu.SemaphoreType.DMA((count,)),
            pltpu.SemaphoreType.DMA((2,)),
            pltpu.SemaphoreType.DMA((weights, 3)),
            pltpu.SemaphoreType.DMA((weights, 3)),
            pltpu.SemaphoreType.DMA((2, capacity)),
            pltpu.SemaphoreType.DMA((2, capacity)),
            pltpu.SemaphoreType.DMA((4 + weights,)),
            pltpu.SemaphoreType.DMA((4 + weights,)),
            pltpu.VMEM((capacity,) + tail, rows.dtype),
            pltpu.VMEM(rows.shape, rows.dtype),
        ],
        compiler_params=pltpu.CompilerParams(
            collective_id=0, has_side_effects=True, vmem_limit_bytes=56 * MIB
        ),
        cost_estimate=lasting(110),
        name="spread_rows",
    )(pack, rows, *shards)
    return outs[0], outs[2:]


class Reducer:
    def __init__(self, count, grads, out, scratch):
        self.grads = grads
        self.out = out
        (
            self.own,
            self.from_sib,
            self.from_far,
            self.from_pair,
            self.chain_in,
            self.load_sem,
            self.sib_s,
            self.sib_r,
            self.far_s,
            self.far_r,
            self.pair_s,
            self.pair_r,
            self.chain_s,
            self.chain_r,
            self.wide_s,
            self.wide_r,
            self.back_s,
            self.back_r,
        ) = scratch
        self.units = out.shape[0]
        self.top = count // 2 - 1
        me = lax.axis_index("ctx")
        w = lax.axis_index("wsh")
        self.w = w
        self.me = me
        self.sib = w + 1 - 2 * (w % 2)
        self.far = (w + 2) % 4
        self.sib_far = (self.sib + 2) % 4
        self.side = me % 2
        self.level = me // 2
        self.pair = me + 1 - 2 * self.side

    def unit(self, u, quarter):
        singles = len(self.grads) - 2
        inner, outer = self.grads[-2:]
        part, features = self.out.shape[1] * self.out.shape[2], self.out.shape[3]
        if u < singles:
            return self.grads[u].at[quarter]
        u -= singles
        across = inner.shape[2] // features
        if u < across:
            return inner.at[quarter, :, pl.ds(u * features, features)]
        return outer.at[quarter, pl.ds((u - across) * part, part)]

    def load(self, u, slot):
        return pltpu.make_async_copy(
            self.unit(u, (self.w, self.far)[slot]), self.own.at[u, slot], self.load_sem.at[u, slot]
        )

    def remote(self, src, dst, send, recv, **device):
        return pltpu.make_async_remote_copy(
            src_ref=src,
            dst_ref=dst,
            send_sem=send,
            recv_sem=recv,
            device_id=device,
            device_id_type=MESH,
        )

    def to_sib(self, u, slot):
        return self.remote(
            self.unit(u, (self.sib, self.sib_far)[slot]),
            self.from_sib.at[u, slot],
            self.sib_s.at[u, slot],
            self.sib_r.at[u, slot],
            wsh=self.sib,
        )

    def to_far(self, u):
        return self.remote(
            self.own.at[u, 1],
            self.from_far.at[u],
            self.far_s.at[u],
            self.far_r.at[u],
            wsh=self.far,
        )

    def half(self, u, side):
        rows = self.out.shape[2]
        return self.own.at[u, 0, pl.ds(pl.multiple_of(side * rows, rows), rows)]

    def to_pair(self, u):
        return self.remote(
            self.half(u, 1 - self.side),
            self.from_pair.at[u],
            self.pair_s.at[u],
            self.pair_r.at[u],
            ctx=self.pair,
        )

    def toward(self, u):
        return 2 if u % 2 == 0 else -2

    def place(self, u, hop):
        return hop if u % 2 == 0 else self.top - hop

    def along(self, u):
        return self.remote(
            self.from_pair.at[u],
            self.chain_in.at[u],
            self.chain_s.at[u],
            self.chain_r.at[u],
            ctx=self.me + self.toward(u),
        )

    def widen(self, u):
        place = self.out.at[u, self.side]
        return self.remote(
            place, place, self.wide_s.at[u], self.wide_r.at[u], ctx=self.me - self.toward(u)
        )

    def give_back(self, u, side):
        place = self.out.at[u, side]
        return self.remote(place, place, self.back_s.at[u], self.back_r.at[u], ctx=self.pair)


    def begin(self, u):
        for slot in (1, 0):
            self.to_sib(u, slot).start()
            self.load(u, slot).start()

    def join_sib(self, u):
        for slot in (1, 0):
            self.load(u, slot).wait()
            self.to_sib(u, slot).wait_recv()
            self.own[u, slot] = add_bf16(self.own[u, slot], self.from_sib[u, slot])
            if slot == 1:
                self.to_far(u).start()

    def join_far(self, u):
        self.to_far(u).wait_recv()
        self.own[u, 0] = add_bf16(self.own[u, 0], self.from_far[u])
        self.to_pair(u).start()

    def join_pair(self, u):
        self.to_pair(u).wait_recv()
        self.from_pair[u] = add_bf16(self.half(u, self.side)[...], self.from_pair[u])

    def gather(self, u, hop):
        @pl.when(self.level == self.place(u, hop))
        def _():
            if hop > 0:
                self.along(u).wait_recv()
                total = add_bf16(self.from_pair[u], self.chain_in[u])
                if hop < self.top:
                    self.from_pair[u] = total
                else:
                    self.out[u, self.side] = total
            if hop < self.top:
                self.along(u).start()
            else:
                self.widen(u).start()
                self.give_back(u, self.side).start()

    def spread_out(self, u, hop):
        @pl.when(self.level == self.place(u, hop))
        def _():
            self.widen(u).wait_recv()
            if hop > 0:
                self.widen(u).start()
            self.give_back(u, self.side).start()

    def steps(self):
        return self.units + 2 * self.top + 3

    def step(self, t):
        lag = 0

        def unit(lag):
            u = t - lag
            return u if 0 <= u < self.units else None

        for stage in (self.join_sib, self.join_far, self.join_pair):
            if unit(lag) is not None:
                stage(unit(lag))
            lag += 1
        lag -= 1
        for hop in range(self.top + 1):
            if unit(lag) is not None:
                self.gather(unit(lag), hop)
            lag += 1
        for hop in range(self.top - 1, -1, -1):
            if unit(lag) is not None:
                self.spread_out(unit(lag), hop)
            lag += 1

    def finish(self):
        for u in range(self.units):
            self.give_back(u, 1 - self.side).wait_recv()
            self.give_back(u, self.side).wait_send()

            @pl.when(self.level != self.place(u, self.top))
            def _():
                self.along(u).wait_send()

            @pl.when(self.level != self.place(u, 0))
            def _():
                self.widen(u).wait_send()

            for slot in range(2):
                self.to_sib(u, slot).wait_send()
            self.to_far(u).wait_send()
            self.to_pair(u).wait_send()


def add_bf16(left, right):
    return (left.astype(jnp.float32) + right.astype(jnp.float32)).astype(jnp.bfloat16)


def unit_count(grads):
    inner, outer = grads[-2:]
    features = outer.shape[2]
    return len(grads) - 2 + inner.shape[2] // features + outer.shape[1] // (features // 4)


def reducer_shapes(grads):
    units = unit_count(grads)
    features = grads[-1].shape[2]
    part = features // 4
    dma = pltpu.SemaphoreType.DMA
    kind = jnp.bfloat16
    out = jax.ShapeDtypeStruct((units, 2, part // 2, features), kind)
    scratch = [
        pltpu.VMEM((units, 2, part, features), kind),
        pltpu.VMEM((units, 2, part, features), kind),
        pltpu.VMEM((units, part, features), kind),
        pltpu.VMEM((units, part // 2, features), kind),
        pltpu.VMEM((units, part // 2, features), kind),
        dma((units, 2)),
        dma((units, 2)),
        dma((units, 2)),
        dma((units,)),
        dma((units,)),
        dma((units,)),
        dma((units,)),
        dma((units,)),
        dma((units,)),
        dma((units,)),
        dma((units,)),
        dma((units,)),
        dma((units,)),
    ]
    return out, scratch


def return_kernel(count, capacity, weights, far_grad, small, *refs):
    grads = refs[:weights]
    back, rim, glob, small_out = refs[weights : weights + 4]
    refs = refs[weights + 4 :]
    reducer = None
    if weights:
        reducer = Reducer(count, grads, refs[0], refs[1 + 15 :])
        refs = refs[1:]
    rand_s, rand_r, halo_s, halo_r, glob_s, glob_r, loc, own_far, own_glob = refs[:9]
    group_part, ring_part, group_s, group_r, ring_s, ring_r = refs[9:15]
    me = lax.axis_index("ctx")
    w = lax.axis_index("wsh")
    last = count - 1
    groups = small.shape[0]
    is_source = jnp.logical_and(me >= 1, me <= last - 1)
    greet(count, groups)

    def random_copy(owner, sender, k):
        return pltpu.make_async_remote_copy(
            src_ref=far_grad.at[EXTRA + (owner - 1) * capacity + k],
            dst_ref=back.at[sender, k],
            send_sem=rand_s.at[owner, k],
            recv_sem=rand_r.at[sender, k],
            device_id={"ctx": owner},
            device_id_type=MESH,
        )

    def landed(sender, k):
        return pltpu.make_async_remote_copy(
            src_ref=far_grad.at[EXTRA + k],
            dst_ref=back.at[sender, k],
            send_sem=rand_s.at[sender, k],
            recv_sem=rand_r.at[sender, k],
            device_id={"ctx": sender},
            device_id_type=MESH,
        )

    def send_random(k):
        @pl.loop(1, count)
        def _(delta):
            owner = (me + delta) % count

            @pl.when(jnp.logical_and(owner >= 1, owner <= last - 1))
            def _():
                random_copy(owner, me, k).start()

    def halo_copy(side):
        return pltpu.make_async_remote_copy(
            src_ref=far_grad.at[side],
            dst_ref=rim.at[1 - side],
            send_sem=halo_s.at[side],
            recv_sem=halo_r.at[side],
            device_id={"ctx": me - 1 if side == 0 else me + 1},
            device_id_type=MESH,
        )

    def global_copy(which, sender):
        return pltpu.make_async_remote_copy(
            src_ref=far_grad.at[2 + which],
            dst_ref=glob.at[sender],
            send_sem=glob_s.at[which],
            recv_sem=glob_r.at[sender],
            device_id={"ctx": 0 if which == 0 else last},
            device_id_type=MESH,
        )

    def group_copy(target, sender):
        return pltpu.make_async_remote_copy(
            src_ref=small.at[target],
            dst_ref=group_part.at[sender],
            send_sem=group_s.at[target],
            recv_sem=group_r.at[sender],
            device_id={"wsh": target},
            device_id_type=MESH,
        )

    def ring_copy(target, sender):
        return pltpu.make_async_remote_copy(
            src_ref=ring_part.at[me],
            dst_ref=ring_part.at[sender],
            send_sem=ring_s.at[target],
            recv_sem=ring_r.at[sender],
            device_id={"ctx": target},
            device_id_type=MESH,
        )

    for delta in range(1, groups):
        group_copy((w + delta) % groups, w).start()

    @pl.when(me > 0)
    def _():
        halo_copy(0).start()
        global_copy(0, me).start()

    @pl.when(me < last)
    def _():
        halo_copy(1).start()
        global_copy(1, me).start()

    if reducer:
        for u in range(reducer.units):
            reducer.begin(u)
    else:
        for k in range(capacity):
            send_random(k)

    total = small[w]
    for delta in range(1, groups):
        sender = (w + delta) % groups
        group_copy(w, sender).wait_recv()
        total = total + group_part[sender]
    ring_part[me] = total

    @pl.loop(1, count)
    def _(delta):
        ring_copy((me + delta) % count, me).start()

    def own_random_in():
        return pltpu.make_async_copy(
            far_grad.at[pl.ds(EXTRA + (me - 1) * capacity, capacity)], own_far, loc.at[0]
        )

    def own_random_out():
        return pltpu.make_async_copy(own_far, back.at[me], loc.at[1])

    def own_global_in(which):
        return pltpu.make_async_copy(far_grad.at[2 + which], own_glob, loc.at[2])

    def own_global_out():
        return pltpu.make_async_copy(own_glob, glob.at[me], loc.at[3])

    @pl.when(is_source)
    def _():
        own_random_in().start()
        own_random_in().wait()
        own_random_out().start()
        own_random_out().wait()

    for which, owner in ((0, 0), (1, last)):

        @pl.when(me == owner)
        def _():
            own_global_in(which).start()
            own_global_in(which).wait()
            own_global_out().start()
            own_global_out().wait()

    @pl.loop(1, count)
    def _(delta):
        ring_copy(me, (me + delta) % count).wait_recv()

    small_out[...] = jnp.sum(ring_part[...], axis=0)

    if reducer:
        for t in range(reducer.steps()):
            if t < capacity:
                send_random(t)
            reducer.step(t)
        reducer.finish()

    @pl.loop(1, count)
    def _(delta):
        ring_copy((me + delta) % count, me).wait_send()

    for delta in range(1, groups):
        group_copy((w + delta) % groups, w).wait_send()

    @pl.when(is_source)
    def _():
        @pl.loop(0, count)
        def _(sender):
            @pl.when(sender != me)
            def _():
                for k in range(capacity):
                    landed(sender, k).wait_recv()

    for which, owner in ((0, 0), (1, last)):

        @pl.when(me == owner)
        def _():
            @pl.loop(0, count)
            def _(sender):
                @pl.when(sender != me)
                def _():
                    global_copy(which, sender).wait_recv()

    @pl.when(me > 0)
    def _():
        halo_copy(0).wait_send()
        halo_copy(1).wait_recv()
        global_copy(0, me).wait_send()

    @pl.when(me < last)
    def _():
        halo_copy(1).wait_send()
        halo_copy(0).wait_recv()
        global_copy(1, me).wait_send()

    @pl.loop(1, count)
    def _(delta):
        owner = (me + delta) % count

        @pl.when(jnp.logical_and(owner >= 1, owner <= last - 1))
        def _():
            for k in range(capacity):
                random_copy(owner, me, k).wait_send()


def return_grads(far_grad, small, grads, count, capacity):
    tail = far_grad.shape[1:]
    kind = far_grad.dtype
    groups = small.shape[0]
    hbm = pl.BlockSpec(memory_space=pl.ANY)
    vmem = pl.BlockSpec(memory_space=pltpu.VMEM)
    sums, sum_scratch = reducer_shapes(grads) if grads else (None, [])
    dma = pltpu.SemaphoreType.DMA
    return pl.pallas_call(
        functools.partial(return_kernel, count, capacity, len(grads)),
        out_shape=[
            jax.ShapeDtypeStruct((count, capacity) + tail, kind),
            jax.ShapeDtypeStruct((2,) + tail, kind),
            jax.ShapeDtypeStruct((count,) + tail, kind),
            jax.ShapeDtypeStruct(small.shape[1:], jnp.float32),
        ]
        + ([sums] if grads else []),
        in_specs=[hbm, vmem] + [hbm] * len(grads),
        out_specs=[hbm, hbm, hbm, vmem] + ([vmem] if grads else []),
        scratch_shapes=[
            dma((count, capacity)),
            dma((count, capacity)),
            dma((2,)),
            dma((2,)),
            dma((2,)),
            dma((count,)),
            dma((4,)),
            pltpu.VMEM((capacity,) + tail, kind),
            pltpu.VMEM(tail, kind),
            pltpu.VMEM(small.shape, jnp.float32),
            pltpu.VMEM((count,) + small.shape[1:], jnp.float32),
            dma((groups,)),
            dma((groups,)),
            dma((count,)),
            dma((count,)),
        ]
        + sum_scratch,
        compiler_params=pltpu.CompilerParams(
            collective_id=1, has_side_effects=True, vmem_limit_bytes=56 * MIB
        ),
        cost_estimate=lasting(150),
        name="return_grads",
    )(far_grad, small, *grads)


def unpack_kernel(
    capacity, picked_ref, filled_ref, edge_ref, base_ref, back_ref, rim_ref, glob_ref, out_ref, acc
):
    step = pl.program_id(0)
    blocks = base_ref.shape[0]

    @pl.when(step == 0)
    def _():
        acc[...] = base_ref[...]

        @pl.when(edge_ref[0] == 0)
        def _():
            acc[0] += rim_ref[0].astype(jnp.float32)

        @pl.when(edge_ref[1] == 0)
        def _():
            acc[blocks - 1] += rim_ref[1].astype(jnp.float32)

    for k in range(capacity):
        slot = step * capacity + k

        @pl.when(filled_ref[slot] == 1)
        def _():
            acc[picked_ref[slot]] += back_ref[0, k].astype(jnp.float32)

    for which, block in ((0, 0), (1, blocks - 1)):

        @pl.when(edge_ref[which] == 1)
        def _():
            acc[block] += glob_ref[0].astype(jnp.float32)

    @pl.when(step == pl.num_programs(0) - 1)
    def _():
        out_ref[...] = acc[...].astype(out_ref.dtype)


def unpack_grads(base, back, rim, glob, picked, filled, edge):
    count, capacity = back.shape[:2]
    blocks, block_rows, features = base.shape
    return pl.pallas_call(
        functools.partial(unpack_kernel, capacity),
        out_shape=jax.ShapeDtypeStruct(base.shape, jnp.bfloat16),
        grid_spec=pltpu.PrefetchScalarGridSpec(
            num_scalar_prefetch=3,
            grid=(count,),
            in_specs=[
                pl.BlockSpec(base.shape, lambda i, *t: (0, 0, 0)),
                pl.BlockSpec((1,) + back.shape[1:], lambda i, *t: (i, 0, 0, 0)),
                pl.BlockSpec(rim.shape, lambda i, *t: (0, 0, 0)),
                pl.BlockSpec((1, block_rows, features), lambda i, *t: (i, 0, 0)),
            ],
            out_specs=pl.BlockSpec(base.shape, lambda i, *t: (0, 0, 0)),
            scratch_shapes=[pltpu.VMEM(base.shape, jnp.float32)],
        ),
        compiler_params=pltpu.CompilerParams(vmem_limit_bytes=32 * MIB),
        name="unpack_grads",
    )(picked, filled, edge, base, back, rim, glob)


def head_mask():
    rows = lax.broadcasted_iota(jnp.int32, (LANES, LANES), 0) // HD
    columns = lax.broadcasted_iota(jnp.int32, (LANES, LANES), 1) // HD
    return rows == columns


def spread_heads(block, mask):
    tiled = jnp.concatenate([block] * PACKED, axis=0)
    return jnp.where(mask, tiled, jnp.zeros_like(tiled))


def fold_heads(square, mask):
    kept = jnp.where(mask, square, 0.0)
    total = kept[:BLK]
    for i in range(1, PACKED):
        total = total + kept[i * BLK : (i + 1) * BLK]
    return total


def listed_rows(ref, index_ref, b):
    return jnp.concatenate([ref[index_ref[b * LISTED + j]] for j in range(LISTED)], axis=0)


def nt(left, right):
    return lax.dot_general(
        left, right, (((1,), (1,)), ((), ())), preferred_element_type=jnp.float32
    )


def nn(left, right):
    return jnp.dot(left, right, preferred_element_type=jnp.float32)


def tn(left, right):
    return lax.dot_general(
        left, right, (((0,), (0,)), ((), ())), preferred_element_type=jnp.float32
    )


def mask_edges(scores, edge_ref, b, blocks):
    low = jnp.logical_and(b == 0, edge_ref[0] == 1)
    high = jnp.logical_and(b == blocks - 1, edge_ref[1] == 1)
    first = jnp.where(low, NEG_FILL, scores[:BLK])
    third = jnp.where(high, NEG_FILL, scores[2 * BLK : 3 * BLK])
    return jnp.concatenate([first, scores[BLK : 2 * BLK], third, scores[3 * BLK :]], axis=0)


def forward_kernel(index_ref, edge_ref, q_ref, k_ref, v_ref, o_ref, log_ref):
    blocks = q_ref.shape[0]
    mask = head_mask()

    @pl.loop(0, blocks)
    def _(b):
        query = spread_heads(q_ref[b] * HD**-0.5, mask)
        scores = mask_edges(nt(listed_rows(k_ref, index_ref, b), query), edge_ref, b, blocks)
        top = jnp.max(scores, axis=0, keepdims=True)
        raised = jnp.exp(scores - top)
        total = jnp.sum(raised, axis=0, keepdims=True)
        probs = (raised * (1.0 / total)).astype(jnp.bfloat16)
        log_ref[b] = top + jnp.log(total)
        mixed = tn(probs, listed_rows(v_ref, index_ref, b))
        o_ref[b] = fold_heads(mixed, mask).astype(o_ref.dtype)


def attend(queries, keys, values, index, edge):
    blocks, block_rows, features = queries.shape
    slots = keys.shape[0]
    groups = features // LANES
    column = lambda g, *t: (0, 0, g)
    return pl.pallas_call(
        forward_kernel,
        out_shape=[
            jax.ShapeDtypeStruct(queries.shape, jnp.bfloat16),
            jax.ShapeDtypeStruct((blocks, 1, features), jnp.float32),
        ],
        grid_spec=pltpu.PrefetchScalarGridSpec(
            num_scalar_prefetch=2,
            grid=(groups,),
            in_specs=[
                pl.BlockSpec((blocks, block_rows, LANES), column),
                pl.BlockSpec((slots, block_rows, LANES), column),
                pl.BlockSpec((slots, block_rows, LANES), column),
            ],
            out_specs=[
                pl.BlockSpec((blocks, block_rows, LANES), column),
                pl.BlockSpec((blocks, 1, LANES), column),
            ],
        ),
        compiler_params=pltpu.CompilerParams(vmem_limit_bytes=40 * MIB),
        cost_estimate=lasting(37),
        name="attend",
    )(index, edge, queries, keys, values)


def backward_kernel(
    index_ref,
    edge_ref,
    q_ref,
    g_ref,
    k_ref,
    v_ref,
    log_ref,
    dq_ref,
    dk_ref,
    dv_ref,
    key_sum,
    value_sum,
):
    blocks = q_ref.shape[0]
    near = blocks + EXTRA
    mask = head_mask()
    key_sum[...] = jnp.zeros_like(key_sum)
    value_sum[...] = jnp.zeros_like(value_sum)
    dk_ref[...] = jnp.zeros_like(dk_ref)
    dv_ref[...] = jnp.zeros_like(dv_ref)

    @pl.loop(0, blocks)
    def _(b):
        query = spread_heads(q_ref[b] * HD**-0.5, mask)
        upstream = spread_heads(g_ref[b], mask)
        key_rows = listed_rows(k_ref, index_ref, b)
        scores = mask_edges(nt(key_rows, query), edge_ref, b, blocks)
        probs = jnp.exp(scores - log_ref[b])
        prob_grad = nt(listed_rows(v_ref, index_ref, b), upstream)
        delta = jnp.sum(probs * prob_grad, axis=0, keepdims=True)
        score_grad = (probs * (prob_grad - delta)).astype(jnp.bfloat16)
        value_grad = nn(probs.astype(jnp.bfloat16), upstream)
        key_grad = nn(score_grad, query)
        query_grad = fold_heads(tn(score_grad, key_rows), mask) * HD**-0.5
        dq_ref[b] = query_grad.astype(dq_ref.dtype)
        for j in range(LISTED):
            slot = index_ref[b * LISTED + j]
            piece = slice(j * BLK, (j + 1) * BLK)
            if j < 5:
                key_sum[slot] += key_grad[piece]
                value_sum[slot] += value_grad[piece]
            else:
                dk_ref[slot] = key_grad[piece].astype(dk_ref.dtype)
                dv_ref[slot] = value_grad[piece].astype(dv_ref.dtype)

    dk_ref[:near] = key_sum[...].astype(dk_ref.dtype)
    dv_ref[:near] = value_sum[...].astype(dv_ref.dtype)


def attend_back(queries, upstream, keys, values, log_total, index, edge):
    blocks, block_rows, features = queries.shape
    slots = keys.shape[0]
    groups = features // LANES
    column = lambda g, *t: (0, 0, g)
    few = pl.BlockSpec((blocks, block_rows, LANES), column)
    many = pl.BlockSpec((slots, block_rows, LANES), column)
    return pl.pallas_call(
        backward_kernel,
        out_shape=[
            jax.ShapeDtypeStruct(queries.shape, jnp.bfloat16),
            jax.ShapeDtypeStruct(keys.shape, jnp.bfloat16),
            jax.ShapeDtypeStruct(keys.shape, jnp.bfloat16),
        ],
        grid_spec=pltpu.PrefetchScalarGridSpec(
            num_scalar_prefetch=2,
            grid=(groups,),
            in_specs=[few, few, many, many, pl.BlockSpec((blocks, 1, LANES), column)],
            out_specs=[few, many, many],
            scratch_shapes=[
                pltpu.VMEM((blocks + EXTRA, block_rows, LANES), jnp.float32),
                pltpu.VMEM((blocks + EXTRA, block_rows, LANES), jnp.float32),
            ],
        ),
        compiler_params=pltpu.CompilerParams(vmem_limit_bytes=48 * MIB),
        cost_estimate=lasting(44),
        name="attend_back",
    )(index, edge, queries, upstream, keys, values, log_total)


def layer_norm(hidden, gain, shift):
    center = hidden - jnp.mean(hidden, axis=-1, keepdims=True)
    inverse = lax.rsqrt(jnp.mean(center * center, axis=-1, keepdims=True) + EPSILON)
    normal = center * inverse
    return (normal * gain + shift, normal, inverse)


def norm_back(upstream, normal, inverse, gain):
    scaled = upstream * gain
    return inverse * (
        scaled
        - jnp.mean(scaled, axis=-1, keepdims=True)
        - normal * jnp.mean(scaled * normal, axis=-1, keepdims=True)
    )


def erf_f32(x):
    return lax.erf(x)


def mid_kernel(
    chunk,
    mixed_ref,
    rows_ref,
    cot_ref,
    vec_ref,
    inner_bias_ref,
    wo_ref,
    w1_ref,
    w2_ref,
    final_ref,
    stream_grad_ref,
    mixed_grad_ref,
    normed_ref,
    act_ref,
    outer_grad_ref,
    inner_grad_ref,
    att_grad_ref,
    sums_ref,
    inner_sums_ref,
    slope,
):
    @pl.when(pl.program_id(0) == 0)
    def _():
        sums_ref[...] = jnp.zeros_like(sums_ref)
        inner_sums_ref[...] = jnp.zeros_like(inner_sums_ref)

    def vector(i):
        return vec_ref[i : i + 1]

    def tally(i, value):
        sums_ref[i : i + 1] += jnp.sum(value, axis=0, keepdims=True)

    hidden = w1_ref.shape[1]
    pieces = [slice(at, at + chunk) for at in range(0, hidden, chunk)]
    attention = nn(mixed_ref[...], wo_ref[...]) + vector(2)
    stream = rows_ref[...].astype(jnp.float32) + attention
    tally(6, stream * stream)
    tally(7, attention * attention)
    first_gain = vector(3)
    normed, first_normal, first_inverse = layer_norm(stream, first_gain, vector(4))
    normed_bf = normed.astype(jnp.bfloat16)
    normed_ref[...] = normed_bf
    outer = jnp.zeros_like(normed)
    for piece in pieces:
        inner = nn(normed_bf, w1_ref[:, piece]) + inner_bias_ref[:, piece]
        cumulative = 0.5 * (1.0 + erf_f32(inner * (1.0 / math.sqrt(2.0))))
        density = jnp.exp(-0.5 * inner * inner) * (1.0 / math.sqrt(2.0 * math.pi))
        slope[:, piece] = cumulative + inner * density
        active = (inner * cumulative).astype(jnp.bfloat16)
        act_ref[:, piece] = active
        outer = outer + nn(active, w2_ref[piece])
    second_gain = vector(6)
    final, second_normal, second_inverse = layer_norm(
        normed + (outer + vector(5)), second_gain, vector(7)
    )
    final_ref[...] = final.astype(final_ref.dtype)
    upstream = cot_ref[...].astype(jnp.float32)
    tally(4, upstream * second_normal)
    tally(5, upstream)
    second_grad = norm_back(upstream, second_normal, second_inverse, second_gain)
    outer_grad = second_grad.astype(jnp.bfloat16)
    outer_grad_ref[...] = outer_grad
    tally(3, outer_grad.astype(jnp.float32))
    normed_grad = second_grad
    for piece in pieces:
        inner_grad = (nt(outer_grad, w2_ref[piece]) * slope[:, piece]).astype(jnp.bfloat16)
        inner_grad_ref[:, piece] = inner_grad
        inner_sums_ref[:, piece] += jnp.sum(
            inner_grad.astype(jnp.float32), axis=0, keepdims=True
        )
        normed_grad = normed_grad + nt(inner_grad, w1_ref[:, piece])
    tally(1, normed_grad * first_normal)
    tally(2, normed_grad)
    stream_grad = norm_back(normed_grad, first_normal, first_inverse, first_gain)
    stream_grad_ref[...] = stream_grad
    att_grad = stream_grad.astype(jnp.bfloat16)
    att_grad_ref[...] = att_grad
    tally(0, att_grad.astype(jnp.float32))
    mixed_grad_ref[...] = nt(att_grad, wo_ref[...]).astype(jnp.bfloat16)


def middle(mixed, rows, cotangent, vectors, inner_bias, wo, w1, w2):
    length, features = rows.shape
    hidden = w1.shape[1]
    block = min(MID_ROWS, length)
    by_row = pl.BlockSpec((block, features), lambda i: (i, 0))
    wide = pl.BlockSpec((block, hidden), lambda i: (i, 0))

    def whole(array):
        return pl.BlockSpec(array.shape, lambda i: (0, 0), pipeline_mode=pl.Buffered(1))

    narrow_bf = jax.ShapeDtypeStruct((length, features), jnp.bfloat16)
    wide_bf = jax.ShapeDtypeStruct((length, hidden), jnp.bfloat16)
    return pl.pallas_call(
        functools.partial(mid_kernel, MID_CHUNK),
        grid=(length // block,),
        out_shape=[
            narrow_bf,
            jax.ShapeDtypeStruct((length, features), jnp.float32),
            narrow_bf,
            narrow_bf,
            wide_bf,
            narrow_bf,
            wide_bf,
            narrow_bf,
            jax.ShapeDtypeStruct((8, features), jnp.float32),
            jax.ShapeDtypeStruct((1, hidden), jnp.float32),
        ],
        in_specs=[
            by_row,
            by_row,
            by_row,
            whole(vectors),
            whole(inner_bias),
            whole(wo),
            whole(w1),
            whole(w2),
        ],
        out_specs=[
            by_row,
            by_row,
            by_row,
            by_row,
            wide,
            by_row,
            wide,
            by_row,
            pl.BlockSpec((8, features), lambda i: (0, 0)),
            pl.BlockSpec((1, hidden), lambda i: (0, 0)),
        ],
        scratch_shapes=[pltpu.VMEM((block, hidden), jnp.float32)],
        compiler_params=pltpu.CompilerParams(vmem_limit_bytes=56 * MIB),
        cost_estimate=lasting(50),
        name="middle",
    )(mixed, rows, cotangent, vectors, inner_bias, wo, w1, w2)


def outer_product(left, right):
    return jnp.einsum("ta,tb->ab", left, right, preferred_element_type=jnp.float32)


def back_product(upstream, weight):
    return jnp.einsum("tb,ab->ta", upstream, weight, preferred_element_type=jnp.float32)


def column_sum(upstream):
    return jnp.sum(upstream.astype(jnp.float32), axis=0)


def shards(
    tokens,
    cotangent,
    random_blocks,
    query_weight,
    query_bias,
    key_weight,
    value_weight,
    value_bias,
    output_weight,
    output_bias,
    first_gain,
    first_shift,
    inner_weight,
    inner_bias,
    outer_weight,
    outer_bias,
    second_gain,
    second_shift,
):
    token_rows = tokens[0]
    length, features = token_rows.shape
    blocks_here = length // BLK
    count = lax.axis_size("ctx")
    groups = lax.axis_size("wsh")
    own_index = lax.axis_index("ctx")
    capacity = (3 * blocks_here + count - 3) // (count - 2)
    part = features // groups
    inner_parts = inner_bias.shape[0] // part

    small = jnp.concatenate(
        (
            query_bias,
            value_bias,
            output_bias,
            first_gain,
            first_shift,
            outer_bias,
            second_gain,
            second_shift,
            inner_bias,
        )
    )
    small = jnp.pad(small, (0, (-small.shape[0]) % 2048)).reshape(-1, 128)

    source, within, ranking = request_tables(random_blocks[0], count, blocks_here)
    filled, picked = send_slots(source, within, ranking, own_index, capacity)
    filled, picked = filled.reshape(-1), picked.reshape(-1)
    own_source = lax.dynamic_index_in_dim(source, own_index, 0, keepdims=False)
    own_rank = lax.dynamic_index_in_dim(ranking, own_index, 0, keepdims=False)
    index = key_slots(own_source, own_rank, blocks_here, capacity).reshape(-1)
    edge = jnp.stack([own_index == 0, own_index == count - 1]).astype(jnp.int32)

    row_blocks = token_rows.reshape(blocks_here, BLK, features)
    pack = pack_blocks(row_blocks, picked).reshape(count, capacity, BLK, features)
    ext_rows, fulls = spread(
        pack,
        row_blocks,
        (
            query_weight,
            key_weight,
            value_weight,
            output_weight,
            inner_weight,
            outer_weight,
            small,
        ),
        count,
        capacity,
    )
    full_query, full_key, full_value, full_output, full_inner, full_outer = (
        full.reshape(-1, full.shape[-1]) for full in fulls[:6]
    )
    gathered = fulls[6].reshape(groups, -1).astype(jnp.float32)
    vectors = gathered[:, : 8 * part].reshape(groups, 8, part)
    vectors = jnp.transpose(vectors, (1, 0, 2)).reshape(8, features)
    full_inner_bias = gathered[:, 8 * part : (8 + inner_parts) * part].reshape(1, -1)

    slots = ext_rows.shape[0]
    ext_flat = ext_rows.reshape(slots * BLK, features)
    queries_bf = (
        jnp.dot(token_rows, full_query, preferred_element_type=jnp.float32) + vectors[0]
    ).astype(jnp.bfloat16)
    keys_bf = jnp.dot(ext_flat, full_key, preferred_element_type=jnp.float32).astype(jnp.bfloat16)
    values_bf = (
        jnp.dot(ext_flat, full_value, preferred_element_type=jnp.float32) + vectors[1]
    ).astype(jnp.bfloat16)
    query_blocks = queries_bf.reshape(blocks_here, BLK, features)
    key_blocks = keys_bf.reshape(slots, BLK, features)
    value_blocks = values_bf.reshape(slots, BLK, features)
    mixed_blocks, log_total = attend(query_blocks, key_blocks, value_blocks, index, edge)
    mixed_bf = mixed_blocks.reshape(length, features)

    (
        final,
        stream_grad,
        mixed_grad_bf,
        normed_bf,
        activated_bf,
        outer_grad_bf,
        inner_grad_bf,
        attention_grad_bf,
        middle_sums,
        inner_bias_grad,
    ) = middle(
        mixed_bf,
        token_rows,
        cotangent[0],
        vectors,
        full_inner_bias,
        full_output,
        full_inner,
        full_outer,
    )
    output_weight_grad = outer_product(mixed_bf, attention_grad_bf)
    inner_weight_grad = outer_product(normed_bf, inner_grad_bf)
    outer_weight_grad = outer_product(activated_bf, outer_grad_bf)
    square_sums = jnp.sum(middle_sums[6:8], axis=1)

    dq_blocks, dk_blocks, dv_blocks = attend_back(
        query_blocks,
        mixed_grad_bf.reshape(blocks_here, BLK, features),
        key_blocks,
        value_blocks,
        log_total,
        index,
        edge,
    )
    dq = dq_blocks.reshape(length, features)
    dk = dk_blocks.reshape(slots * BLK, features)
    dv = dv_blocks.reshape(slots * BLK, features)
    far_grad = (
        (back_product(dk[length:], full_key) + back_product(dv[length:], full_value))
        .astype(jnp.bfloat16)
        .reshape(slots - blocks_here, BLK, features)
    )
    query_bias_grad = column_sum(dq)
    value_bias_grad = column_sum(dv)
    weight_grads = tuple(
        grad.astype(jnp.bfloat16).reshape(groups, -1, grad.shape[-1])
        for grad in (
            outer_product(token_rows, dq),
            outer_product(ext_flat, dk),
            outer_product(ext_flat, dv),
            output_weight_grad,
            inner_weight_grad,
            outer_weight_grad,
        )
    )
    vector_grads = jnp.concatenate(
        [query_bias_grad[None], value_bias_grad[None], middle_sums[:6]], axis=0
    )
    small_grads = jnp.concatenate(
        [
            jnp.transpose(vector_grads.reshape(8, groups, part), (1, 0, 2)),
            inner_bias_grad.reshape(groups, inner_parts, part),
            jnp.broadcast_to(
                jnp.pad(square_sums, (0, part - 2)).reshape(1, 1, part), (groups, 1, part)
            ),
        ],
        axis=1,
    )
    small_grads = jnp.pad(
        small_grads, ((0, 0), (0, (-small_grads.shape[1]) % 8), (0, (-part) % 128))
    )
    chained = count == 8
    back, rim, glob, small_sums, *chain_sums = return_grads(
        far_grad, small_grads, weight_grads if chained else (), count, capacity
    )
    near_grad = (
        stream_grad
        + back_product(dq, full_query)
        + back_product(dk[:length], full_key)
        + back_product(dv[:length], full_value)
    ).reshape(blocks_here, BLK, features)
    tokens_grad = unpack_grads(near_grad, back, rim, glob, picked, filled, edge)

    if chained:
        units = chain_sums[0].reshape(-1, part, features).astype(jnp.float32)
        across = full_inner.shape[1] // features
        sums = [units[i] for i in range(4)] + [
            jnp.concatenate([units[4 + i] for i in range(across)], axis=1),
            units[4 + across :].reshape(-1, features),
        ]
    else:
        sums = lax.psum(
            tuple(
                lax.psum_scatter(
                    grad.reshape(-1, grad.shape[-1]), "wsh", scatter_dimension=0, tiled=True
                )
                for grad in weight_grads
            ),
            "ctx",
        )
        sums = [total.astype(jnp.float32) for total in sums]
    element_count = count * groups * length * features
    stream_rms = jnp.sqrt(small_sums[8 + inner_parts, :2] / element_count)
    (
        query_bias_grad,
        value_bias_grad,
        output_bias_grad,
        first_gain_grad,
        first_shift_grad,
        outer_bias_grad,
        second_gain_grad,
        second_shift_grad,
    ) = (small_sums[i, :part] for i in range(8))
    inner_bias_grad = small_sums[8 : 8 + inner_parts, :part].reshape(-1)
    query_weight_sum, key_weight_sum, value_weight_sum, output_weight_sum = sums[:4]
    return (
        final[None],
        tokens_grad.reshape(1, length, features),
        query_weight_sum,
        query_bias_grad,
        key_weight_sum,
        value_weight_sum,
        value_bias_grad,
        output_weight_sum,
        output_bias_grad,
        first_gain_grad,
        first_shift_grad,
        sums[4],
        inner_bias_grad,
        sums[5],
        outer_bias_grad,
        second_gain_grad,
        second_shift_grad,
        stream_rms,
    )


def solution(mesh):
    in_specs = (
        P("wsh", "ctx", None),
        P("wsh", "ctx", None),
        P("wsh", None, None),
        P("wsh", None),
        P("wsh"),
        P("wsh", None),
        P("wsh", None),
        P("wsh"),
        P("wsh", None),
        P("wsh"),
        P("wsh"),
        P("wsh"),
        P("wsh", None),
        P("wsh"),
        P("wsh", None),
        P("wsh"),
        P("wsh"),
        P("wsh"),
    )
    out_specs = (
        P("wsh", "ctx", None),
        P("wsh", "ctx", None),
        P("wsh", None),
        P("wsh"),
        P("wsh", None),
        P("wsh", None),
        P("wsh"),
        P("wsh", None),
        P("wsh"),
        P("wsh"),
        P("wsh"),
        P("wsh", None),
        P("wsh"),
        P("wsh", None),
        P("wsh"),
        P("wsh"),
        P("wsh"),
        P(),
    )
    return jax.shard_map(shards, mesh=mesh, in_specs=in_specs, out_specs=out_specs, check_vma=False)
```

```python
import functools
import math

import jax
import jax.numpy as jnp
from jax import lax
from jax.experimental import pallas as pl
from jax.experimental.pallas import tpu as pltpu
from jax.sharding import PartitionSpec as P

HD = 64
BLK = 64
PACKED = 4
LANES = PACKED * HD
LISTED = 8
EXTRA = 4

EPSILON = 1e-06
NEG_FILL = -1e30
MESH = pl.DeviceIdType.MESH
MIB = 1 << 20
MID_ROWS = 256
MID_CHUNK = 768
GAP = 0
UNROLL = 4
EARLY = 2
PACE = (3,) * 12


def lasting(microseconds):
    return pl.CostEstimate(
        flops=int(microseconds * 1e9), bytes_accessed=int(microseconds * 1e6), transcendentals=0
    )


def request_tables(random_rows, cycle_size, blocks_here):
    wanted = random_rows.reshape(cycle_size, 3 * blocks_here)
    source = wanted // blocks_here
    within = wanted % blocks_here
    positions = jnp.arange(wanted.shape[1])
    earlier = positions[None, :] < positions[:, None]
    same_source = source[:, :, None] == source[:, None, :]
    ranking = jnp.sum(same_source & earlier[None], axis=2, dtype=jnp.int32)
    return (source, within, ranking)


def send_slots(source, within, ranking, own_index, capacity):
    slot_ids = jnp.arange(capacity, dtype=jnp.int32)
    selected = (source[:, None, :] == own_index) & (ranking[:, None, :] == slot_ids[None, :, None])
    filled = jnp.any(selected, axis=2)
    picked = jnp.sum(jnp.where(selected, within[:, None, :], 0), axis=2, dtype=jnp.int32)
    return (filled.astype(jnp.int32), picked)


def key_slots(own_source, own_rank, blocks_here, capacity):
    block = jnp.arange(blocks_here, dtype=jnp.int32)
    left = jnp.where(block == 0, blocks_here, block - 1)
    right = jnp.where(block == blocks_here - 1, blocks_here + 1, block + 1)
    drawn = (blocks_here + EXTRA + (own_source - 1) * capacity + own_rank).reshape(blocks_here, 3)
    fixed = jnp.stack(
        [
            left,
            block,
            right,
            jnp.full_like(block, blocks_here + 2),
            jnp.full_like(block, blocks_here + 3),
        ],
        axis=1,
    )
    return jnp.concatenate([fixed, drawn], axis=1).astype(jnp.int32)


def pack_kernel(picked_ref, rows_ref, out_ref, sems):
    slots = out_ref.shape[0]

    def copy(i):
        return pltpu.make_async_copy(rows_ref.at[picked_ref[i]], out_ref.at[i], sems.at[i])

    @pl.loop(0, slots)
    def _(i):
        copy(i).start()

    @pl.loop(0, slots)
    def _(i):
        copy(i).wait()


def pack_blocks(rows, picked):
    slots = picked.shape[0]
    return pl.pallas_call(
        pack_kernel,
        out_shape=jax.ShapeDtypeStruct((slots,) + rows.shape[1:], rows.dtype),
        grid_spec=pltpu.PrefetchScalarGridSpec(
            num_scalar_prefetch=1,
            grid=(1,),
            in_specs=[pl.BlockSpec(rows.shape, lambda i, t: (0, 0, 0))],
            out_specs=pl.BlockSpec(memory_space=pl.ANY),
            scratch_shapes=[pltpu.SemaphoreType.DMA((slots,))],
        ),
        name="pack_blocks",
    )(picked, rows)


def greet(count, groups):
    barrier = pltpu.get_barrier_semaphore()
    me = lax.axis_index("ctx")
    w = lax.axis_index("wsh")

    @pl.loop(1, count)
    def _(delta):
        pl.semaphore_signal(
            barrier, inc=1, device_id={"ctx": (me + delta) % count}, device_id_type=MESH
        )

    for delta in range(1, groups):
        pl.semaphore_signal(
            barrier, inc=1, device_id={"wsh": (w + delta) % groups}, device_id_type=MESH
        )
    pl.semaphore_wait(barrier, count + groups - 2)


def relays(count):
    return ((3, 2, (4, 6)), (4, 5, (3, 1))) if count == 8 else ()


def spread_kernel(count, capacity, *refs):
    weights = (len(refs) - 2 - 2 - 14) // 3
    pack, rows = refs[:2]
    shards = refs[2 : 2 + weights]
    ext, passing = refs[2 + weights : 4 + weights]
    fulls = refs[4 + weights : 4 + 2 * weights]
    rest = refs[4 + 2 * weights :]
    held = rest[:weights]
    rand_s, rand_r, halo_s, halo_r, glob_s, glob_r, wgt_s, wgt_r = rest[weights : weights + 8]
    pass_s, pass_r, loc_in, loc_out, own_pack, own_row = rest[weights + 8 :]
    blocks = rows.shape[0]
    base = blocks + EXTRA
    me = lax.axis_index("ctx")
    w = lax.axis_index("wsh")
    sib = w + 1 - 2 * (w % 2)
    far = (w + 2) % 4
    last = count - 1
    is_source = jnp.logical_and(me >= 1, me <= last - 1)
    routes = relays(count)
    greet(count, 4)

    def relayed(dst):
        found = me < 0
        for source, _, targets in routes:
            for target in targets:
                found = jnp.logical_or(found, jnp.logical_and(me == source, dst == target))
        return found

    def weight_copy(i, step):
        if step == 2:
            src, dst, target = fulls[i].at[far], fulls[i].at[far], sib
        else:
            src, dst, target = shards[i], fulls[i].at[w], (far, sib)[step]
        return pltpu.make_async_remote_copy(
            src_ref=src,
            dst_ref=dst,
            send_sem=wgt_s.at[i, step],
            recv_sem=wgt_r.at[i, step],
            device_id={"wsh": target},
            device_id_type=MESH,
        )

    def random_copy(dst, k):
        return pltpu.make_async_remote_copy(
            src_ref=pack.at[dst, k],
            dst_ref=ext.at[base + (me - 1) * capacity + k],
            send_sem=rand_s.at[dst, k],
            recv_sem=rand_r.at[me, k],
            device_id={"ctx": dst},
            device_id_type=MESH,
        )

    def random_landed(source, k):
        return pltpu.make_async_remote_copy(
            src_ref=pack.at[source, k],
            dst_ref=ext.at[base + (source - 1) * capacity + k],
            send_sem=rand_s.at[source, k],
            recv_sem=rand_r.at[source, k],
            device_id={"ctx": source},
            device_id_type=MESH,
        )

    def to_relay(via, r, dst, k):
        return pltpu.make_async_remote_copy(
            src_ref=pack.at[dst, k],
            dst_ref=passing.at[r, k],
            send_sem=rand_s.at[dst, k],
            recv_sem=pass_r.at[r, k],
            device_id={"ctx": via},
            device_id_type=MESH,
        )

    def from_relay(source, r, dst, k):
        return pltpu.make_async_remote_copy(
            src_ref=passing.at[r, k],
            dst_ref=ext.at[base + (source - 1) * capacity + k],
            send_sem=pass_s.at[r, k],
            recv_sem=rand_r.at[source, k],
            device_id={"ctx": dst},
            device_id_type=MESH,
        )

    def halo_copy(side):
        return pltpu.make_async_remote_copy(
            src_ref=rows.at[blocks - 1 if side == 0 else 0],
            dst_ref=ext.at[blocks + side],
            send_sem=halo_s.at[side],
            recv_sem=halo_r.at[side],
            device_id={"ctx": me + 1 if side == 0 else me - 1},
            device_id_type=MESH,
        )

    def global_copy(which, dst):
        return pltpu.make_async_remote_copy(
            src_ref=rows.at[0 if which == 0 else blocks - 1],
            dst_ref=ext.at[blocks + 2 + which],
            send_sem=glob_s.at[dst],
            recv_sem=glob_r.at[which],
            device_id={"ctx": dst},
            device_id_type=MESH,
        )

    def held_in(i):
        return pltpu.make_async_copy(shards[i], held[i], loc_in.at[2 + i])

    def held_out(i):
        return pltpu.make_async_copy(held[i], fulls[i].at[w], loc_out.at[2 + i])

    def rows_in():
        return pltpu.make_async_copy(rows, own_row, loc_in.at[0])

    def rows_out():
        return pltpu.make_async_copy(own_row, ext.at[pl.ds(0, blocks)], loc_out.at[0])

    def pack_in():
        return pltpu.make_async_copy(pack.at[me], own_pack, loc_in.at[1])

    def pack_out():
        return pltpu.make_async_copy(
            own_pack, ext.at[pl.ds(base + (me - 1) * capacity, capacity)], loc_out.at[1]
        )

    def rim_out(side):
        return pltpu.make_async_copy(own_row.at[0], ext.at[blocks + side], loc_out.at[2 + weights])

    def global_out(which):
        return pltpu.make_async_copy(
            own_row.at[0 if which == 0 else blocks - 1],
            ext.at[blocks + 2 + which],
            loc_out.at[3 + weights],
        )

    for i in range(weights):
        weight_copy(i, 0).start()
        weight_copy(i, 1).start()

    @pl.when(me < last)
    def _():
        halo_copy(0).start()

    @pl.when(me > 0)
    def _():
        halo_copy(1).start()

    for which, owner in ((0, 0), (1, last)):

        @pl.when(me == owner)
        def _():
            @pl.loop(1, count)
            def _(delta):
                global_copy(which, (me + delta) % count).start()

    for k in range(capacity):
        for source, via, targets in routes:

            @pl.when(me == source)
            def _():
                for r, target in enumerate(targets):
                    to_relay(via, r, target, k).start()

        @pl.when(is_source)
        def _():
            @pl.loop(1, count)
            def _(delta):
                dst = (me + delta) % count

                @pl.when(jnp.logical_not(relayed(dst)))
                def _():
                    random_copy(dst, k).start()

    rows_in().start()
    for i in range(weights):
        held_in(i).start()

    @pl.when(is_source)
    def _():
        pack_in().start()
        pack_in().wait()
        pack_out().start()

    rows_in().wait()
    rows_out().start()
    for which, owner in ((0, 0), (1, last)):

        @pl.when(me == owner)
        def _():
            rim_out(which).start()
            global_out(which).start()

    for i in range(weights):
        held_in(i).wait()
        held_out(i).start()

    for step in range(max(capacity, weights)):
        if step < capacity:
            for source, via, targets in routes:

                @pl.when(me == via)
                def _():
                    for r, target in enumerate(targets):
                        to_relay(via, r, target, step).wait_recv()
                        from_relay(source, r, target, step).start()

        if step < weights:
            weight_copy(step, 0).wait_recv()
            weight_copy(step, 2).start()

    rows_out().wait()
    for i in range(weights):
        held_out(i).wait()

    @pl.when(is_source)
    def _():
        pack_out().wait()

        for k in range(capacity):

            @pl.loop(1, count)
            def _(delta):
                random_copy((me + delta) % count, k).wait_send()

    for source, via, targets in routes:

        @pl.when(me == via)
        def _():
            for r, target in enumerate(targets):
                for k in range(capacity):
                    from_relay(source, r, target, k).wait_send()

    for which, owner in ((0, 0), (1, last)):

        @pl.when(me == owner)
        def _():
            rim_out(which).wait()
            global_out(which).wait()

            @pl.loop(1, count)
            def _(delta):
                global_copy(which, (me + delta) % count).wait_send()

        @pl.when(me != owner)
        def _():
            global_copy(which, owner).wait_recv()

    @pl.when(me < last)
    def _():
        halo_copy(0).wait_send()
        halo_copy(1).wait_recv()

    @pl.when(me > 0)
    def _():
        halo_copy(1).wait_send()
        halo_copy(0).wait_recv()

    for k in range(capacity):

        @pl.loop(1, last)
        def _(source):
            @pl.when(source != me)
            def _():
                random_landed(source, k).wait_recv()

    for i in range(weights):
        for step in range(3):
            weight_copy(i, step).wait_send()
        weight_copy(i, 1).wait_recv()
        weight_copy(i, 2).wait_recv()


def spread(pack, rows, shards, count, capacity):
    blocks = rows.shape[0]
    tail = rows.shape[1:]
    weights = len(shards)
    slots = blocks + EXTRA + (count - 2) * capacity
    outs = pl.pallas_call(
        functools.partial(spread_kernel, count, capacity),
        out_shape=[
            jax.ShapeDtypeStruct((slots,) + tail, rows.dtype),
            jax.ShapeDtypeStruct((2, capacity) + tail, rows.dtype),
        ]
        + [jax.ShapeDtypeStruct((4,) + shard.shape, shard.dtype) for shard in shards],
        in_specs=[pl.BlockSpec(memory_space=pl.ANY)] * (2 + weights),
        out_specs=[pl.BlockSpec(memory_space=pl.ANY)] * (2 + weights),
        scratch_shapes=[pltpu.VMEM(shard.shape, shard.dtype) for shard in shards]
        + [
            pltpu.SemaphoreType.DMA((count, capacity)),
            pltpu.SemaphoreType.DMA((count, capacity)),
            pltpu.SemaphoreType.DMA((2,)),
            pltpu.SemaphoreType.DMA((2,)),
            pltpu.SemaphoreType.DMA((count,)),
            pltpu.SemaphoreType.DMA((2,)),
            pltpu.SemaphoreType.DMA((weights, 3)),
            pltpu.SemaphoreType.DMA((weights, 3)),
            pltpu.SemaphoreType.DMA((2, capacity)),
            pltpu.SemaphoreType.DMA((2, capacity)),
            pltpu.SemaphoreType.DMA((4 + weights,)),
            pltpu.SemaphoreType.DMA((4 + weights,)),
            pltpu.VMEM((capacity,) + tail, rows.dtype),
            pltpu.VMEM(rows.shape, rows.dtype),
        ],
        compiler_params=pltpu.CompilerParams(
            collective_id=0, has_side_effects=True, vmem_limit_bytes=56 * MIB
        ),
        cost_estimate=lasting(110),
        name="spread_rows",
    )(pack, rows, *shards)
    return outs[0], outs[2:]


class Reducer:
    def __init__(self, count, unit, staged, out, scratch):
        self.unit = unit
        self.staged = staged
        self.out = out
        (
            self.ring,
            self.from_sib,
            self.from_far,
            self.from_pair,
            self.chain_in,
            self.load_sem,
            self.sib_s,
            self.sib_r,
            self.far_s,
            self.far_r,
            self.pair_s,
            self.pair_r,
            self.chain_s,
            self.chain_r,
            self.wide_s,
            self.wide_r,
            self.back_s,
            self.back_r,
        ) = scratch
        self.units = out.shape[0]
        self.top = count // 2 - 1
        me = lax.axis_index("ctx")
        w = lax.axis_index("wsh")
        self.w = w
        self.me = me
        self.sib = w + 1 - 2 * (w % 2)
        self.far = (w + 2) % 4
        self.sib_far = (self.sib + 2) % 4
        self.side = me % 2
        self.level = me // 2
        self.pair = me + 1 - 2 * self.side

    def load(self, u, slot):
        return pltpu.make_async_copy(
            self.unit(u, (self.w, self.far)[slot]),
            self.ring.at[u % 2, slot],
            self.load_sem.at[u, slot],
        )

    def remote(self, src, dst, send, recv, **device):
        return pltpu.make_async_remote_copy(
            src_ref=src,
            dst_ref=dst,
            send_sem=send,
            recv_sem=recv,
            device_id=device,
            device_id_type=MESH,
        )

    def to_sib(self, u, slot):
        return self.remote(
            self.unit(u, (self.sib, self.sib_far)[slot]),
            self.from_sib.at[u, slot],
            self.sib_s.at[u, slot],
            self.sib_r.at[u, slot],
            wsh=self.sib,
        )

    def to_far(self, u):
        return self.remote(
            self.from_sib.at[u, 1],
            self.from_far.at[u],
            self.far_s.at[u],
            self.far_r.at[u],
            wsh=self.far,
        )

    def half(self, u, side):
        rows = self.out.shape[2]
        return self.from_sib.at[u, 0, pl.ds(pl.multiple_of(side * rows, rows), rows)]

    def to_pair(self, u):
        return self.remote(
            self.half(u, 1 - self.side),
            self.from_pair.at[u],
            self.pair_s.at[u],
            self.pair_r.at[u],
            ctx=self.pair,
        )

    def toward(self, u):
        return 2 if u % 2 == 0 else -2

    def place(self, u, hop):
        return hop if u % 2 == 0 else self.top - hop

    def along(self, u):
        return self.remote(
            self.from_pair.at[u],
            self.chain_in.at[u],
            self.chain_s.at[u],
            self.chain_r.at[u],
            ctx=self.me + self.toward(u),
        )

    def widen(self, u):
        place = self.out.at[u, self.side]
        return self.remote(
            place, place, self.wide_s.at[u], self.wide_r.at[u], ctx=self.me - self.toward(u)
        )

    def give_back(self, u, side):
        place = self.out.at[u, side]
        return self.remote(place, place, self.back_s.at[u], self.back_r.at[u], ctx=self.pair)


    def begin(self, u):
        for slot in (1, 0):
            self.to_sib(u, slot).start()
            if u < min(2, self.staged):
                self.load(u, slot).start()

    def join_sib(self, u):
        for slot in (1, 0):
            if u < self.staged:
                self.load(u, slot).wait()
                own = self.ring[u % 2, slot]
            else:
                own = self.unit(u, (self.w, self.far)[slot])[...]
            self.to_sib(u, slot).wait_recv()
            self.from_sib[u, slot] = add_bf16(own, self.from_sib[u, slot])
            if slot == 1:
                self.to_far(u).start()
            if u + 2 < self.staged:
                self.load(u + 2, slot).start()

    def join_far(self, u):
        self.to_far(u).wait_recv()
        self.from_sib[u, 0] = add_bf16(self.from_sib[u, 0], self.from_far[u])
        self.to_pair(u).start()

    def join_pair(self, u):
        self.to_pair(u).wait_recv()
        self.from_pair[u] = add_bf16(self.half(u, self.side)[...], self.from_pair[u])

    def gather(self, u, hop):
        @pl.when(self.level == self.place(u, hop))
        def _():
            if hop > 0:
                self.along(u).wait_recv()
                total = add_bf16(self.from_pair[u], self.chain_in[u])
                if hop < self.top:
                    self.from_pair[u] = total
                else:
                    self.out[u, self.side] = total
            if hop < self.top:
                self.along(u).start()
            else:
                self.widen(u).start()
                self.give_back(u, self.side).start()

    def spread_out(self, u, hop):
        @pl.when(self.level == self.place(u, hop))
        def _():
            self.widen(u).wait_recv()
            if hop > 0:
                self.widen(u).start()
            self.give_back(u, self.side).start()

    def step(self, t):
        def unit(lag):
            u = t - lag
            if u >= self.staged:
                u = u - GAP if u >= self.staged + GAP else -1
            return u if 0 <= u < self.units else None

        if unit(0) is not None:
            self.join_far(unit(0))
        if unit(1) is not None:
            self.join_pair(unit(1))
        lag = 1
        for hop in range(self.top + 1):
            if unit(lag) is not None:
                self.gather(unit(lag), hop)
            lag += 1
        for hop in range(self.top - 1, -1, -1):
            if unit(lag) is not None:
                self.spread_out(unit(lag), hop)
            lag += 1

    def steps(self):
        return self.units + GAP + 2 * self.top + 1

    def finish(self):
        for u in range(self.units):
            self.give_back(u, 1 - self.side).wait_recv()
            self.give_back(u, self.side).wait_send()

            @pl.when(self.level != self.place(u, self.top))
            def _():
                self.along(u).wait_send()

            @pl.when(self.level != self.place(u, 0))
            def _():
                self.widen(u).wait_send()

            for slot in range(2):
                self.to_sib(u, slot).wait_send()
            self.to_far(u).wait_send()
            self.to_pair(u).wait_send()


def add_bf16(left, right):
    return (left.astype(jnp.float32) + right.astype(jnp.float32)).astype(jnp.bfloat16)


def reducer_shapes(units, part, features):
    dma = pltpu.SemaphoreType.DMA
    kind = jnp.bfloat16
    out = jax.ShapeDtypeStruct((units, 2, part // 2, features), kind)
    scratch = [
        pltpu.VMEM((2, 2, part, features), kind),
        pltpu.VMEM((units, 2, part, features), kind),
        pltpu.VMEM((units, part, features), kind),
        pltpu.VMEM((units, part // 2, features), kind),
        pltpu.VMEM((units, part // 2, features), kind),
        dma((units, 2)),
        dma((units, 2)),
        dma((units, 2)),
    ] + [dma((units,)) for _ in range(10)]
    return out, scratch


class Returner:
    def __init__(self, count, capacity, far_ref, rim_ref, outs, small, sems):
        self.count, self.capacity, self.small = count, capacity, small
        self.far_ref, self.rim_ref = far_ref, rim_ref
        self.back, self.rim, self.glob, self.small_out = outs
        (
            self.rand_s,
            self.rand_r,
            self.halo_s,
            self.halo_r,
            self.glob_s,
            self.glob_r,
            self.loc,
            self.group_part,
            self.ring_part,
            self.group_s,
            self.group_r,
            self.ring_s,
            self.ring_r,
        ) = sems
        self.me = lax.axis_index("ctx")
        self.w = lax.axis_index("wsh")
        self.last = count - 1
        self.groups = small.shape[0]
        self.is_source = jnp.logical_and(self.me >= 1, self.me <= self.last - 1)

    def remote(self, src, dst, send, recv, **device):
        return pltpu.make_async_remote_copy(
            src_ref=src,
            dst_ref=dst,
            send_sem=send,
            recv_sem=recv,
            device_id=device,
            device_id_type=MESH,
        )

    def random_copy(self, owner, k):
        return self.remote(
            self.far_ref.at[(owner - 1) * self.capacity + k],
            self.back.at[self.me, k],
            self.rand_s.at[owner, k],
            self.rand_r.at[self.me, k],
            ctx=owner,
        )

    def landed(self, sender, k):
        return self.remote(
            self.far_ref.at[k],
            self.back.at[sender, k],
            self.rand_s.at[sender, k],
            self.rand_r.at[sender, k],
            ctx=sender,
        )

    def own_random(self):
        return pltpu.make_async_copy(
            self.far_ref.at[pl.ds((self.me - 1) * self.capacity, self.capacity)],
            self.back.at[self.me],
            self.loc.at[0],
        )

    def halo_copy(self, side):
        return self.remote(
            self.rim_ref.at[side],
            self.rim.at[1 - side],
            self.halo_s.at[side],
            self.halo_r.at[side],
            ctx=self.me - 1 if side == 0 else self.me + 1,
        )

    def global_copy(self, which, sender):
        return self.remote(
            self.rim_ref.at[2 + which],
            self.glob.at[sender],
            self.glob_s.at[which],
            self.glob_r.at[sender],
            ctx=0 if which == 0 else self.last,
        )

    def own_global(self, which):
        return pltpu.make_async_copy(
            self.rim_ref.at[2 + which], self.glob.at[self.me], self.loc.at[1]
        )

    def group_copy(self, target, sender):
        return self.remote(
            self.small.at[target],
            self.group_part.at[sender],
            self.group_s.at[target],
            self.group_r.at[sender],
            wsh=target,
        )

    def ring_copy(self, target, sender):
        return self.remote(
            self.ring_part.at[self.me],
            self.ring_part.at[sender],
            self.ring_s.at[target],
            self.ring_r.at[sender],
            ctx=target,
        )

    def send_random(self, owner, slots):
        @pl.when(owner != self.me)
        def _():
            for k in slots:
                self.random_copy(owner, k).start()

    def send_round(self, k):
        @pl.loop(0, self.count - 2)
        def _(i):
            self.send_random(1 + (self.me + i) % (self.count - 2), (k,))

    def keep_own(self):
        @pl.when(self.is_source)
        def _():
            self.own_random().start()

    def send_rims(self):
        @pl.when(self.me > 0)
        def _():
            self.halo_copy(0).start()
            self.global_copy(0, self.me).start()

        @pl.when(self.me < self.last)
        def _():
            self.halo_copy(1).start()
            self.global_copy(1, self.me).start()

        for which, owner in ((0, 0), (1, self.last)):

            @pl.when(self.me == owner)
            def _():
                self.own_global(which).start()

    def send_small(self):
        for delta in range(1, self.groups):
            self.group_copy((self.w + delta) % self.groups, self.w).start()

    def pass_small(self):
        total = self.small[self.w]
        for delta in range(1, self.groups):
            sender = (self.w + delta) % self.groups
            self.group_copy(self.w, sender).wait_recv()
            total = total + self.group_part[sender]
        self.ring_part[self.me] = total

        @pl.loop(1, self.count)
        def _(delta):
            self.ring_copy((self.me + delta) % self.count, self.me).start()

    def end_small(self):
        @pl.loop(1, self.count)
        def _(delta):
            self.ring_copy(self.me, (self.me + delta) % self.count).wait_recv()

        self.small_out[...] = jnp.sum(self.ring_part[...], axis=0)

        @pl.loop(1, self.count)
        def _(delta):
            self.ring_copy((self.me + delta) % self.count, self.me).wait_send()

        for delta in range(1, self.groups):
            self.group_copy((self.w + delta) % self.groups, self.w).wait_send()

    def finish(self):
        @pl.when(self.is_source)
        def _():
            self.own_random().wait()

            @pl.loop(0, self.count)
            def _(sender):
                @pl.when(sender != self.me)
                def _():
                    for k in range(self.capacity):
                        self.landed(sender, k).wait_recv()

        for which, owner in ((0, 0), (1, self.last)):

            @pl.when(self.me == owner)
            def _():
                self.own_global(which).wait()

                @pl.loop(0, self.count)
                def _(sender):
                    @pl.when(sender != self.me)
                    def _():
                        self.global_copy(which, sender).wait_recv()

        @pl.when(self.me > 0)
        def _():
            self.halo_copy(0).wait_send()
            self.halo_copy(1).wait_recv()
            self.global_copy(0, self.me).wait_send()

        @pl.when(self.me < self.last)
        def _():
            self.halo_copy(1).wait_send()
            self.halo_copy(0).wait_recv()
            self.global_copy(1, self.me).wait_send()

        @pl.loop(1, self.last)
        def _(owner):
            @pl.when(owner != self.me)
            def _():
                for k in range(self.capacity):
                    self.random_copy(owner, k).wait_send()


def returner_shapes(count, capacity, tail, small):
    kind = jnp.bfloat16
    dma = pltpu.SemaphoreType.DMA
    groups = small.shape[0]
    outs = [
        jax.ShapeDtypeStruct((count, capacity) + tail, kind),
        jax.ShapeDtypeStruct((2,) + tail, kind),
        jax.ShapeDtypeStruct((count,) + tail, kind),
        jax.ShapeDtypeStruct(small.shape[1:], jnp.float32),
    ]
    sems = [
        dma((count, capacity)),
        dma((count, capacity)),
        dma((2,)),
        dma((2,)),
        dma((2,)),
        dma((count,)),
        dma((2,)),
        pltpu.VMEM(small.shape, jnp.float32),
        pltpu.VMEM((count,) + small.shape[1:], jnp.float32),
        dma((groups,)),
        dma((groups,)),
        dma((count,)),
        dma((count,)),
    ]
    return outs, sems


HBM_SPEC = pl.BlockSpec(memory_space=pl.ANY)
VMEM_SPEC = pl.BlockSpec(memory_space=pltpu.VMEM)
RETURN_SPECS = [HBM_SPEC, HBM_SPEC, HBM_SPEC, VMEM_SPEC]


def return_kernel(count, capacity, far_ref, rim_ref, small, *refs):
    mover = Returner(count, capacity, far_ref, rim_ref, refs[:4], small, refs[4:])
    greet(count, small.shape[0])
    mover.send_small()
    mover.send_rims()

    for k in range(capacity):
        mover.send_round(k)
    mover.keep_own()
    mover.pass_small()
    mover.end_small()
    mover.finish()


def return_grads(far_grad, small, count, capacity):
    tail = far_grad.shape[1:]
    outs, sems = returner_shapes(count, capacity, tail, small)
    return pl.pallas_call(
        functools.partial(return_kernel, count, capacity),
        out_shape=outs,
        in_specs=[VMEM_SPEC, VMEM_SPEC, VMEM_SPEC],
        out_specs=RETURN_SPECS,
        scratch_shapes=sems,
        compiler_params=pltpu.CompilerParams(
            collective_id=1, has_side_effects=True, vmem_limit_bytes=56 * MIB
        ),
        name="return_grads",
    )(far_grad[EXTRA:], far_grad[:EXTRA], small)


def tail_kernel(
    count,
    capacity,
    dq_hbm,
    dk_hbm,
    dv_hbm,
    x_hbm,
    stream_hbm,
    outer_hbm,
    inner_hbm,
    wo_hbm,
    wq_ref,
    wk_ref,
    wv_ref,
    small_in,
    *refs,
):
    outs, near_hbm, sums = refs[:4], refs[4], refs[5]
    (
        xbuf,
        kbuf,
        vbuf,
        qbuf,
        wq_sum,
        wk_sum,
        wv_sum,
        shares,
        sending,
        rims,
        stage,
        small,
        bias_sum,
        load_sem,
        q_sem,
        stage_sem,
    ) = refs[6:22]
    returner_sems, reducer_scratch = refs[22:35], refs[35:]
    blocks, _, features = dq_hbm.shape
    length = blocks * BLK
    near = blocks + EXTRA
    chunk = capacity * BLK
    part = features // 4
    me = lax.axis_index("ctx")
    sources = count - 2
    mover = Returner(count, capacity, sending, rims, outs, small, returner_sems)
    across = inner_hbm.shape[2] // features
    stacked = outer_hbm.shape[1] // part
    staged = stacked + across + 1

    def unit(u, quarter):
        if u < stacked:
            return outer_hbm.at[quarter, pl.ds(u * part, part)]
        if u < stacked + across:
            return inner_hbm.at[quarter, :, pl.ds((u - stacked) * features, features)]
        if u < staged:
            return wo_hbm.at[quarter]
        return shares.at[u - staged, quarter]

    reducer = Reducer(count, unit, staged, sums, reducer_scratch)

    def loads(at, slot, size):
        here, there = pl.ds(at, size), pl.ds(0, size)
        return [
            pltpu.make_async_copy(src.at[here], dst.at[slot, there], load_sem.at[slot, n])
            for n, (src, dst) in enumerate(((x_hbm, xbuf), (dk_hbm, kbuf), (dv_hbm, vbuf)))
        ]

    def far_loads(i, slot):
        return loads(near + ((me + i) % sources) * capacity, slot, capacity)

    def own_loads(n):
        half = blocks // 2
        return loads(n * half, n, half) + [
            pltpu.make_async_copy(dq_hbm.at[pl.ds(n * half, half)], qbuf.at[n], q_sem.at[n])
        ]

    def start(copies):
        for copy in copies:
            copy.start()

    def end(copies):
        for copy in copies:
            copy.wait()

    def gather_weights(rows, key_grad, value_grad):
        wk_sum[...] += tn(rows, key_grad)
        wv_sum[...] += tn(rows, value_grad)
        bias_sum[1:2] += jnp.sum(value_grad.astype(jnp.float32), axis=0, keepdims=True)

    start(far_loads(0, 0))
    greet(count, small.shape[0])
    for u in range(staged):
        reducer.begin(u)
    bias_sum[...] = jnp.zeros_like(bias_sum)
    wk_sum[...] = jnp.zeros_like(wk_sum)
    wv_sum[...] = jnp.zeros_like(wv_sum)

    for third in range(3):

        @pl.loop(third * sources // 3, (third + 1) * sources // 3)
        def _(i):
            slot = i % 2
            end(far_loads(i, slot))

            @pl.when(i + 1 < sources)
            def _():
                start(far_loads(i + 1, 1 - slot))

            key_grad = kbuf[slot].reshape(chunk, features)
            value_grad = vbuf[slot].reshape(chunk, features)
            row_grad = nt(key_grad, wk_ref[...]) + nt(value_grad, wv_ref[...])
            s = 1 + (me + i) % sources
            sending[pl.ds((s - 1) * capacity, capacity)] = row_grad.astype(sending.dtype).reshape(
                capacity, BLK, features
            )
            mover.send_random(s, range(EARLY))
            gather_weights(xbuf[slot].reshape(chunk, features), key_grad, value_grad)

        for u in range(third * staged // 3, (third + 1) * staged // 3):
            reducer.join_sib(u)
    mover.keep_own()

    rim_loads = loads(blocks, 0, EXTRA)
    start(rim_loads)
    end(rim_loads)
    rim_rows = EXTRA * BLK
    key_grad = kbuf[0, :EXTRA].reshape(rim_rows, features)
    value_grad = vbuf[0, :EXTRA].reshape(rim_rows, features)
    row_grad = nt(key_grad, wk_ref[...]) + nt(value_grad, wv_ref[...])
    rims[...] = row_grad.astype(rims.dtype).reshape(EXTRA, BLK, features)
    mover.send_rims()
    gather_weights(xbuf[0, :EXTRA].reshape(rim_rows, features), key_grad, value_grad)

    start(own_loads(0))
    start(own_loads(1))
    wq_sum[...] = jnp.zeros_like(wq_sum)
    half = length // 2

    def stage_load(n):
        return pltpu.make_async_copy(
            stream_hbm.at[pl.ds(n * half, half)], stage.at[n], stage_sem.at[0, n]
        )

    def stage_store(n):
        return pltpu.make_async_copy(
            stage.at[n], near_hbm.at[pl.ds(n * half, half)], stage_sem.at[1, n]
        )

    for n in range(2):
        stage_load(n).start()
        end(own_loads(n))

    @pl.loop(0, 2)
    def _(n):
        rows = xbuf[n].reshape(half, features)
        query_grad = qbuf[n].reshape(half, features)
        gather_weights(rows, kbuf[n].reshape(half, features), vbuf[n].reshape(half, features))
        wq_sum[...] += tn(rows, query_grad)
        bias_sum[0:1] += jnp.sum(query_grad.astype(jnp.float32), axis=0, keepdims=True)

    for u, total in ((0, wq_sum), (1, wk_sum), (2, wv_sum)):
        for quarter in range(4):
            shares[u, quarter] = total[quarter * part : (quarter + 1) * part].astype(shares.dtype)
        reducer.begin(staged + u)
    small[...] = small_in[...]
    for quarter in range(4):
        lanes = slice(quarter * part, (quarter + 1) * part)
        small[quarter, 0:2, :part] = bias_sum[0:2, lanes]
    mover.send_small()

    ticks = iter(range(reducer.steps()))
    waiting = list(range(EARLY * sources, capacity * sources))

    def advance():
        tick = next(ticks)
        reducer.step(tick)
        wave = PACE[tick] if tick < len(PACE) else 0
        for n in waiting[:wave]:
            mover.send_random(1 + (me + n % sources) % sources, (n // sources,))
        del waiting[:wave]
        return tick + 1

    advance()
    advance()
    for u in range(staged, reducer.units):
        reducer.join_sib(u)
    mover.pass_small()

    for n in range(2):
        stage_load(n).wait()
        stage[n] = (
            stage[n]
            + nt(qbuf[n].reshape(half, features), wq_ref[...])
            + nt(kbuf[n].reshape(half, features), wk_ref[...])
            + nt(vbuf[n].reshape(half, features), wv_ref[...])
        )
        stage_store(n).start()
        advance()
    while advance() < reducer.steps():
        pass
    for n in range(2):
        stage_store(n).wait()
    mover.end_small()
    reducer.finish()
    mover.finish()


def backward_tail(
    dq,
    dk,
    dv,
    ext_rows,
    stream_grad,
    outer_grad,
    inner_grad,
    output_grad,
    wq,
    wk,
    wv,
    small,
    count,
    capacity,
):
    blocks, block_rows, features = dq.shape
    tail = (block_rows, features)
    far_slots = (count - 2) * capacity
    part = features // 4
    outs, sems = returner_shapes(count, capacity, tail, small)
    units = outer_grad.shape[1] // part + inner_grad.shape[2] // features + 4
    sums, sum_scratch = reducer_shapes(units, part, features)
    kind = jnp.bfloat16
    dma = pltpu.SemaphoreType.DMA
    square = pltpu.VMEM((features, features), jnp.float32)
    some = pltpu.VMEM((2, capacity) + tail, kind)
    return pl.pallas_call(
        functools.partial(tail_kernel, count, capacity),
        out_shape=outs + [jax.ShapeDtypeStruct(stream_grad.shape, jnp.float32), sums],
        in_specs=[HBM_SPEC] * 8 + [VMEM_SPEC] * 4,
        out_specs=RETURN_SPECS + [HBM_SPEC, VMEM_SPEC],
        scratch_shapes=[some] * 4
        + [square] * 3
        + [
            pltpu.VMEM((3, 4, part, features), kind),
            pltpu.VMEM((far_slots,) + tail, kind),
            pltpu.VMEM((EXTRA,) + tail, kind),
            pltpu.VMEM((2, blocks * block_rows // 2, features), jnp.float32),
            pltpu.VMEM(small.shape, jnp.float32),
            pltpu.VMEM((8, features), jnp.float32),
            dma((2, 3)),
            dma((2,)),
            dma((2, 2)),
        ]
        + sems
        + sum_scratch,
        compiler_params=pltpu.CompilerParams(
            collective_id=1, has_side_effects=True, vmem_limit_bytes=58 * MIB
        ),
        cost_estimate=lasting(150),
        name="backward_tail",
    )(
        dq,
        dk,
        dv,
        ext_rows,
        stream_grad,
        outer_grad,
        inner_grad,
        output_grad,
        wq,
        wk,
        wv,
        small,
    )


def unpack_kernel(
    capacity, picked_ref, filled_ref, edge_ref, base_ref, back_ref, rim_ref, glob_ref, out_ref, acc
):
    step = pl.program_id(0)
    blocks = base_ref.shape[0]

    @pl.when(step == 0)
    def _():
        acc[...] = base_ref[...]

        @pl.when(edge_ref[0] == 0)
        def _():
            acc[0] += rim_ref[0].astype(jnp.float32)

        @pl.when(edge_ref[1] == 0)
        def _():
            acc[blocks - 1] += rim_ref[1].astype(jnp.float32)

    for k in range(capacity):
        slot = step * capacity + k

        @pl.when(filled_ref[slot] == 1)
        def _():
            acc[picked_ref[slot]] += back_ref[0, k].astype(jnp.float32)

    for which, block in ((0, 0), (1, blocks - 1)):

        @pl.when(edge_ref[which] == 1)
        def _():
            acc[block] += glob_ref[0].astype(jnp.float32)

    @pl.when(step == pl.num_programs(0) - 1)
    def _():
        out_ref[...] = acc[...].astype(out_ref.dtype)


def unpack_grads(base, back, rim, glob, picked, filled, edge):
    count, capacity = back.shape[:2]
    blocks, block_rows, features = base.shape
    return pl.pallas_call(
        functools.partial(unpack_kernel, capacity),
        out_shape=jax.ShapeDtypeStruct(base.shape, jnp.bfloat16),
        grid_spec=pltpu.PrefetchScalarGridSpec(
            num_scalar_prefetch=3,
            grid=(count,),
            in_specs=[
                pl.BlockSpec(base.shape, lambda i, *t: (0, 0, 0)),
                pl.BlockSpec((1,) + back.shape[1:], lambda i, *t: (i, 0, 0, 0)),
                pl.BlockSpec(rim.shape, lambda i, *t: (0, 0, 0)),
                pl.BlockSpec((1, block_rows, features), lambda i, *t: (i, 0, 0)),
            ],
            out_specs=pl.BlockSpec(base.shape, lambda i, *t: (0, 0, 0)),
            scratch_shapes=[pltpu.VMEM(base.shape, jnp.float32)],
        ),
        compiler_params=pltpu.CompilerParams(vmem_limit_bytes=32 * MIB),
        name="unpack_grads",
    )(picked, filled, edge, base, back, rim, glob)


def head_mask():
    rows = lax.broadcasted_iota(jnp.int32, (LANES, LANES), 0) // HD
    columns = lax.broadcasted_iota(jnp.int32, (LANES, LANES), 1) // HD
    return rows == columns


def spread_heads(block, mask):
    tiled = jnp.concatenate([block] * PACKED, axis=0)
    return jnp.where(mask, tiled, jnp.zeros_like(tiled))


def fold_heads(square, mask):
    kept = jnp.where(mask, square, 0.0)
    total = kept[:BLK]
    for i in range(1, PACKED):
        total = total + kept[i * BLK : (i + 1) * BLK]
    return total


def listed_rows(ref, index_ref, b):
    return jnp.concatenate([ref[index_ref[b * LISTED + j]] for j in range(LISTED)], axis=0)


def nt(left, right):
    return lax.dot_general(
        left, right, (((1,), (1,)), ((), ())), preferred_element_type=jnp.float32
    )


def nn(left, right):
    return jnp.dot(left, right, preferred_element_type=jnp.float32)


def tn(left, right):
    return lax.dot_general(
        left, right, (((0,), (0,)), ((), ())), preferred_element_type=jnp.float32
    )


def mask_edges(scores, edge_ref, b, blocks):
    low = jnp.logical_and(b == 0, edge_ref[0] == 1)
    high = jnp.logical_and(b == blocks - 1, edge_ref[1] == 1)
    first = jnp.where(low, NEG_FILL, scores[:BLK])
    third = jnp.where(high, NEG_FILL, scores[2 * BLK : 3 * BLK])
    return jnp.concatenate([first, scores[BLK : 2 * BLK], third, scores[3 * BLK :]], axis=0)


def forward_kernel(index_ref, edge_ref, q_ref, k_ref, v_ref, o_ref, log_ref):
    blocks = q_ref.shape[0]
    mask = head_mask()

    @pl.loop(0, blocks, unroll=True)
    def _(b):
        query = spread_heads(q_ref[b] * HD**-0.5, mask)
        scores = mask_edges(nt(listed_rows(k_ref, index_ref, b), query), edge_ref, b, blocks)
        top = jnp.max(scores, axis=0, keepdims=True)
        raised = jnp.exp(scores - top)
        total = jnp.sum(raised, axis=0, keepdims=True)
        probs = (raised * (1.0 / total)).astype(jnp.bfloat16)
        log_ref[b] = top + jnp.log(total)
        mixed = tn(probs, listed_rows(v_ref, index_ref, b))
        o_ref[b] = fold_heads(mixed, mask).astype(o_ref.dtype)


def attend(queries, keys, values, index, edge):
    blocks, block_rows, features = queries.shape
    slots = keys.shape[0]
    groups = features // LANES
    column = lambda g, *t: (0, 0, g)
    return pl.pallas_call(
        forward_kernel,
        out_shape=[
            jax.ShapeDtypeStruct(queries.shape, jnp.bfloat16),
            jax.ShapeDtypeStruct((blocks, 1, features), jnp.float32),
        ],
        grid_spec=pltpu.PrefetchScalarGridSpec(
            num_scalar_prefetch=2,
            grid=(groups,),
            in_specs=[
                pl.BlockSpec((blocks, block_rows, LANES), column),
                pl.BlockSpec((slots, block_rows, LANES), column),
                pl.BlockSpec((slots, block_rows, LANES), column),
            ],
            out_specs=[
                pl.BlockSpec((blocks, block_rows, LANES), column),
                pl.BlockSpec((blocks, 1, LANES), column),
            ],
        ),
        compiler_params=pltpu.CompilerParams(vmem_limit_bytes=40 * MIB),
        cost_estimate=lasting(37),
        name="attend",
    )(index, edge, queries, keys, values)


def backward_kernel(
    index_ref,
    edge_ref,
    q_ref,
    g_ref,
    k_ref,
    v_ref,
    log_ref,
    dq_ref,
    dk_ref,
    dv_ref,
    key_sum,
    value_sum,
):
    blocks = q_ref.shape[0]
    near = blocks + EXTRA
    mask = head_mask()
    key_sum[...] = jnp.zeros_like(key_sum)
    value_sum[...] = jnp.zeros_like(value_sum)
    dk_ref[...] = jnp.zeros_like(dk_ref)
    dv_ref[...] = jnp.zeros_like(dv_ref)

    @pl.loop(0, blocks, unroll=UNROLL)
    def _(b):
        query = spread_heads(q_ref[b] * HD**-0.5, mask)
        upstream = spread_heads(g_ref[b], mask)
        key_rows = listed_rows(k_ref, index_ref, b)
        scores = mask_edges(nt(key_rows, query), edge_ref, b, blocks)
        probs = jnp.exp(scores - log_ref[b])
        prob_grad = nt(listed_rows(v_ref, index_ref, b), upstream)
        delta = jnp.sum(probs * prob_grad, axis=0, keepdims=True)
        score_grad = (probs * (prob_grad - delta)).astype(jnp.bfloat16)
        value_grad = nn(probs.astype(jnp.bfloat16), upstream)
        key_grad = nn(score_grad, query)
        query_grad = fold_heads(tn(score_grad, key_rows), mask) * HD**-0.5
        dq_ref[b] = query_grad.astype(dq_ref.dtype)
        for j in range(LISTED):
            slot = index_ref[b * LISTED + j]
            piece = slice(j * BLK, (j + 1) * BLK)
            if j < 5:
                key_sum[slot] += key_grad[piece]
                value_sum[slot] += value_grad[piece]
            else:
                dk_ref[slot] = key_grad[piece].astype(dk_ref.dtype)
                dv_ref[slot] = value_grad[piece].astype(dv_ref.dtype)

    dk_ref[:near] = key_sum[...].astype(dk_ref.dtype)
    dv_ref[:near] = value_sum[...].astype(dv_ref.dtype)


def attend_back(queries, upstream, keys, values, log_total, index, edge):
    blocks, block_rows, features = queries.shape
    slots = keys.shape[0]
    groups = features // LANES
    column = lambda g, *t: (0, 0, g)
    few = pl.BlockSpec((blocks, block_rows, LANES), column)
    many = pl.BlockSpec((slots, block_rows, LANES), column)
    return pl.pallas_call(
        backward_kernel,
        out_shape=[
            jax.ShapeDtypeStruct(queries.shape, jnp.bfloat16),
            jax.ShapeDtypeStruct(keys.shape, jnp.bfloat16),
            jax.ShapeDtypeStruct(keys.shape, jnp.bfloat16),
        ],
        grid_spec=pltpu.PrefetchScalarGridSpec(
            num_scalar_prefetch=2,
            grid=(groups,),
            in_specs=[few, few, many, many, pl.BlockSpec((blocks, 1, LANES), column)],
            out_specs=[few, many, many],
            scratch_shapes=[
                pltpu.VMEM((blocks + EXTRA, block_rows, LANES), jnp.float32),
                pltpu.VMEM((blocks + EXTRA, block_rows, LANES), jnp.float32),
            ],
        ),
        compiler_params=pltpu.CompilerParams(vmem_limit_bytes=48 * MIB),
        cost_estimate=lasting(44),
        name="attend_back",
    )(index, edge, queries, upstream, keys, values, log_total)


def layer_norm(hidden, gain, shift):
    center = hidden - jnp.mean(hidden, axis=-1, keepdims=True)
    inverse = lax.rsqrt(jnp.mean(center * center, axis=-1, keepdims=True) + EPSILON)
    normal = center * inverse
    return (normal * gain + shift, normal, inverse)


def norm_back(upstream, normal, inverse, gain):
    scaled = upstream * gain
    return inverse * (
        scaled
        - jnp.mean(scaled, axis=-1, keepdims=True)
        - normal * jnp.mean(scaled * normal, axis=-1, keepdims=True)
    )


def erf_f32(x):
    return lax.erf(x)


def mid_kernel(
    chunk,
    mixed_ref,
    rows_ref,
    cot_ref,
    vec_ref,
    inner_bias_ref,
    wo_ref,
    w1_ref,
    w2_ref,
    final_ref,
    stream_grad_ref,
    mixed_grad_ref,
    normed_ref,
    act_ref,
    outer_grad_ref,
    inner_grad_ref,
    att_grad_ref,
    sums_ref,
    inner_sums_ref,
    slope,
):
    @pl.when(pl.program_id(0) == 0)
    def _():
        sums_ref[...] = jnp.zeros_like(sums_ref)
        inner_sums_ref[...] = jnp.zeros_like(inner_sums_ref)

    def vector(i):
        return vec_ref[i : i + 1]

    def tally(i, value):
        sums_ref[i : i + 1] += jnp.sum(value, axis=0, keepdims=True)

    hidden = w1_ref.shape[1]
    pieces = [slice(at, at + chunk) for at in range(0, hidden, chunk)]
    attention = nn(mixed_ref[...], wo_ref[...]) + vector(2)
    stream = rows_ref[...].astype(jnp.float32) + attention
    tally(6, stream * stream)
    tally(7, attention * attention)
    first_gain = vector(3)
    normed, first_normal, first_inverse = layer_norm(stream, first_gain, vector(4))
    normed_bf = normed.astype(jnp.bfloat16)
    normed_ref[...] = normed_bf
    outer = jnp.zeros_like(normed)
    for piece in pieces:
        inner = nn(normed_bf, w1_ref[:, piece]) + inner_bias_ref[:, piece]
        cumulative = 0.5 * (1.0 + erf_f32(inner * (1.0 / math.sqrt(2.0))))
        density = jnp.exp(-0.5 * inner * inner) * (1.0 / math.sqrt(2.0 * math.pi))
        slope[:, piece] = cumulative + inner * density
        active = (inner * cumulative).astype(jnp.bfloat16)
        act_ref[:, piece] = active
        outer = outer + nn(active, w2_ref[piece])
    second_gain = vector(6)
    final, second_normal, second_inverse = layer_norm(
        normed + (outer + vector(5)), second_gain, vector(7)
    )
    final_ref[...] = final.astype(final_ref.dtype)
    upstream = cot_ref[...].astype(jnp.float32)
    tally(4, upstream * second_normal)
    tally(5, upstream)
    second_grad = norm_back(upstream, second_normal, second_inverse, second_gain)
    outer_grad = second_grad.astype(jnp.bfloat16)
    outer_grad_ref[...] = outer_grad
    tally(3, outer_grad.astype(jnp.float32))
    normed_grad = second_grad
    for piece in pieces:
        inner_grad = (nt(outer_grad, w2_ref[piece]) * slope[:, piece]).astype(jnp.bfloat16)
        inner_grad_ref[:, piece] = inner_grad
        inner_sums_ref[:, piece] += jnp.sum(
            inner_grad.astype(jnp.float32), axis=0, keepdims=True
        )
        normed_grad = normed_grad + nt(inner_grad, w1_ref[:, piece])
    tally(1, normed_grad * first_normal)
    tally(2, normed_grad)
    stream_grad = norm_back(normed_grad, first_normal, first_inverse, first_gain)
    stream_grad_ref[...] = stream_grad
    att_grad = stream_grad.astype(jnp.bfloat16)
    att_grad_ref[...] = att_grad
    tally(0, att_grad.astype(jnp.float32))
    mixed_grad = nt(att_grad, wo_ref[...]).astype(jnp.bfloat16)
    mixed_grad_ref[...] = mixed_grad


def middle(mixed, rows, cotangent, vectors, inner_bias, wo, w1, w2):
    length, features = rows.shape
    hidden = w1.shape[1]
    block = min(MID_ROWS, length)
    by_row = pl.BlockSpec((block, features), lambda i: (i, 0))
    wide = pl.BlockSpec((block, hidden), lambda i: (i, 0))

    def whole(array):
        return pl.BlockSpec(array.shape, lambda i: (0, 0), pipeline_mode=pl.Buffered(1))

    narrow_bf = jax.ShapeDtypeStruct((length, features), jnp.bfloat16)
    wide_bf = jax.ShapeDtypeStruct((length, hidden), jnp.bfloat16)
    return pl.pallas_call(
        functools.partial(mid_kernel, MID_CHUNK),
        grid=(length // block,),
        out_shape=[
            narrow_bf,
            jax.ShapeDtypeStruct((length, features), jnp.float32),
            narrow_bf,
            narrow_bf,
            wide_bf,
            narrow_bf,
            wide_bf,
            narrow_bf,
            jax.ShapeDtypeStruct((8, features), jnp.float32),
            jax.ShapeDtypeStruct((1, hidden), jnp.float32),
        ],
        in_specs=[
            by_row,
            by_row,
            by_row,
            whole(vectors),
            whole(inner_bias),
            whole(wo),
            whole(w1),
            whole(w2),
        ],
        out_specs=[
            by_row,
            by_row,
            by_row,
            by_row,
            wide,
            by_row,
            wide,
            by_row,
            pl.BlockSpec((8, features), lambda i: (0, 0)),
            pl.BlockSpec((1, hidden), lambda i: (0, 0)),
        ],
        scratch_shapes=[pltpu.VMEM((block, hidden), jnp.float32)],
        compiler_params=pltpu.CompilerParams(vmem_limit_bytes=56 * MIB),
        cost_estimate=lasting(50),
        name="middle",
    )(mixed, rows, cotangent, vectors, inner_bias, wo, w1, w2)


def outer_product(left, right):
    return jnp.einsum("ta,tb->ab", left, right, preferred_element_type=jnp.float32)


def back_product(upstream, weight):
    return jnp.einsum("tb,ab->ta", upstream, weight, preferred_element_type=jnp.float32)


def column_sum(upstream):
    return jnp.sum(upstream.astype(jnp.float32), axis=0)


def shards(
    tokens,
    cotangent,
    random_blocks,
    query_weight,
    query_bias,
    key_weight,
    value_weight,
    value_bias,
    output_weight,
    output_bias,
    first_gain,
    first_shift,
    inner_weight,
    inner_bias,
    outer_weight,
    outer_bias,
    second_gain,
    second_shift,
):
    token_rows = tokens[0]
    length, features = token_rows.shape
    blocks_here = length // BLK
    count = lax.axis_size("ctx")
    groups = lax.axis_size("wsh")
    own_index = lax.axis_index("ctx")
    capacity = (3 * blocks_here + count - 3) // (count - 2)
    part = features // groups
    inner_parts = inner_bias.shape[0] // part

    small = jnp.concatenate(
        (
            query_bias,
            value_bias,
            output_bias,
            first_gain,
            first_shift,
            outer_bias,
            second_gain,
            second_shift,
            inner_bias,
        )
    )
    small = jnp.pad(small, (0, (-small.shape[0]) % 2048)).reshape(-1, 128)

    source, within, ranking = request_tables(random_blocks[0], count, blocks_here)
    filled, picked = send_slots(source, within, ranking, own_index, capacity)
    filled, picked = filled.reshape(-1), picked.reshape(-1)
    own_source = lax.dynamic_index_in_dim(source, own_index, 0, keepdims=False)
    own_rank = lax.dynamic_index_in_dim(ranking, own_index, 0, keepdims=False)
    index = key_slots(own_source, own_rank, blocks_here, capacity).reshape(-1)
    edge = jnp.stack([own_index == 0, own_index == count - 1]).astype(jnp.int32)

    row_blocks = token_rows.reshape(blocks_here, BLK, features)
    pack = pack_blocks(row_blocks, picked).reshape(count, capacity, BLK, features)
    ext_rows, fulls = spread(
        pack,
        row_blocks,
        (
            query_weight,
            key_weight,
            value_weight,
            output_weight,
            inner_weight,
            outer_weight,
            small,
        ),
        count,
        capacity,
    )
    full_query, full_key, full_value, full_output, full_inner, full_outer = (
        full.reshape(-1, full.shape[-1]) for full in fulls[:6]
    )
    gathered = fulls[6].reshape(groups, -1).astype(jnp.float32)
    vectors = gathered[:, : 8 * part].reshape(groups, 8, part)
    vectors = jnp.transpose(vectors, (1, 0, 2)).reshape(8, features)
    full_inner_bias = gathered[:, 8 * part : (8 + inner_parts) * part].reshape(1, -1)

    slots = ext_rows.shape[0]
    ext_flat = ext_rows.reshape(slots * BLK, features)
    queries_bf = (
        jnp.dot(token_rows, full_query, preferred_element_type=jnp.float32) + vectors[0]
    ).astype(jnp.bfloat16)
    keys_bf = jnp.dot(ext_flat, full_key, preferred_element_type=jnp.float32).astype(jnp.bfloat16)
    values_bf = (
        jnp.dot(ext_flat, full_value, preferred_element_type=jnp.float32) + vectors[1]
    ).astype(jnp.bfloat16)
    query_blocks = queries_bf.reshape(blocks_here, BLK, features)
    key_blocks = keys_bf.reshape(slots, BLK, features)
    value_blocks = values_bf.reshape(slots, BLK, features)
    mixed_blocks, log_total = attend(query_blocks, key_blocks, value_blocks, index, edge)
    mixed_bf = mixed_blocks.reshape(length, features)

    (
        final,
        stream_grad,
        mixed_grad_bf,
        normed_bf,
        activated_bf,
        outer_grad_bf,
        inner_grad_bf,
        attention_grad_bf,
        middle_sums,
        inner_bias_grad,
    ) = middle(
        mixed_bf,
        token_rows,
        cotangent[0],
        vectors,
        full_inner_bias,
        full_output,
        full_inner,
        full_outer,
    )
    output_weight_grad = outer_product(mixed_bf, attention_grad_bf)
    inner_weight_grad = outer_product(normed_bf, inner_grad_bf)
    outer_weight_grad = outer_product(activated_bf, outer_grad_bf)
    square_sums = jnp.sum(middle_sums[6:8], axis=1)

    fused = count == 8 and 3 * blocks_here == capacity * (count - 2)

    def small_parts(query_row, value_row):
        rows = jnp.concatenate([query_row, value_row, middle_sums[:6]], axis=0)
        parts = jnp.concatenate(
            [
                jnp.transpose(rows.reshape(8, groups, part), (1, 0, 2)),
                inner_bias_grad.reshape(groups, inner_parts, part),
                jnp.broadcast_to(
                    jnp.pad(square_sums, (0, part - 2)).reshape(1, 1, part), (groups, 1, part)
                ),
            ],
            axis=1,
        )
        return jnp.pad(parts, ((0, 0), (0, (-parts.shape[1]) % 8), (0, (-part) % 128)))

    mixed_grad_blocks = mixed_grad_bf.reshape(blocks_here, BLK, features)
    dq_blocks, dk_blocks, dv_blocks = attend_back(
        query_blocks, mixed_grad_blocks, key_blocks, value_blocks, log_total, index, edge
    )
    if fused:
        empty = jnp.zeros((1, features), jnp.float32)
        back, rim, glob, small_sums, near_grad, unit_sums = backward_tail(
            dq_blocks,
            dk_blocks,
            dv_blocks,
            ext_rows,
            stream_grad,
            outer_weight_grad.astype(jnp.bfloat16).reshape(groups, -1, features),
            inner_weight_grad.astype(jnp.bfloat16).reshape(groups, part, -1),
            output_weight_grad.astype(jnp.bfloat16).reshape(groups, part, features),
            full_query,
            full_key,
            full_value,
            small_parts(empty, empty),
            count,
            capacity,
        )
        stacked = full_outer.shape[0] // features
        across = full_inner.shape[1] // features
        units = unit_sums.reshape(-1, part, features).astype(jnp.float32)
        sums = [units[stacked + across + i] for i in (1, 2, 3, 0)] + [
            jnp.concatenate([units[stacked + i] for i in range(across)], axis=1),
            units[:stacked].reshape(-1, features),
        ]
    else:
        dq = dq_blocks.reshape(length, features)
        dk = dk_blocks.reshape(slots * BLK, features)
        dv = dv_blocks.reshape(slots * BLK, features)
        far_grad = (
            (back_product(dk[length:], full_key) + back_product(dv[length:], full_value))
            .astype(jnp.bfloat16)
            .reshape(slots - blocks_here, BLK, features)
        )
        back, rim, glob, small_sums = return_grads(
            far_grad, small_parts(column_sum(dq)[None], column_sum(dv)[None]), count, capacity
        )
        near_grad = (
            stream_grad
            + back_product(dq, full_query)
            + back_product(dk[:length], full_key)
            + back_product(dv[:length], full_value)
        )
        sums = lax.psum(
            tuple(
                lax.psum_scatter(
                    grad.astype(jnp.bfloat16), "wsh", scatter_dimension=0, tiled=True
                )
                for grad in (
                    outer_product(token_rows, dq),
                    outer_product(ext_flat, dk),
                    outer_product(ext_flat, dv),
                    output_weight_grad,
                    inner_weight_grad,
                    outer_weight_grad,
                )
            ),
            "ctx",
        )
        sums = [total.astype(jnp.float32) for total in sums]
    tokens_grad = unpack_grads(
        near_grad.reshape(blocks_here, BLK, features), back, rim, glob, picked, filled, edge
    )
    element_count = count * groups * length * features
    stream_rms = jnp.sqrt(small_sums[8 + inner_parts, :2] / element_count)
    (
        query_bias_grad,
        value_bias_grad,
        output_bias_grad,
        first_gain_grad,
        first_shift_grad,
        outer_bias_grad,
        second_gain_grad,
        second_shift_grad,
    ) = (small_sums[i, :part] for i in range(8))
    inner_bias_grad = small_sums[8 : 8 + inner_parts, :part].reshape(-1)
    query_weight_sum, key_weight_sum, value_weight_sum, output_weight_sum = sums[:4]
    return (
        final[None],
        tokens_grad.reshape(1, length, features),
        query_weight_sum,
        query_bias_grad,
        key_weight_sum,
        value_weight_sum,
        value_bias_grad,
        output_weight_sum,
        output_bias_grad,
        first_gain_grad,
        first_shift_grad,
        sums[4],
        inner_bias_grad,
        sums[5],
        outer_bias_grad,
        second_gain_grad,
        second_shift_grad,
        stream_rms,
    )


def solution(mesh):
    in_specs = (
        P("wsh", "ctx", None),
        P("wsh", "ctx", None),
        P("wsh", None, None),
        P("wsh", None),
        P("wsh"),
        P("wsh", None),
        P("wsh", None),
        P("wsh"),
        P("wsh", None),
        P("wsh"),
        P("wsh"),
        P("wsh"),
        P("wsh", None),
        P("wsh"),
        P("wsh", None),
        P("wsh"),
        P("wsh"),
        P("wsh"),
    )
    out_specs = (
        P("wsh", "ctx", None),
        P("wsh", "ctx", None),
        P("wsh", None),
        P("wsh"),
        P("wsh", None),
        P("wsh", None),
        P("wsh"),
        P("wsh", None),
        P("wsh"),
        P("wsh"),
        P("wsh"),
        P("wsh", None),
        P("wsh"),
        P("wsh", None),
        P("wsh"),
        P("wsh"),
        P("wsh"),
        P(),
    )
    return jax.shard_map(shards, mesh=mesh, in_specs=in_specs, out_specs=out_specs, check_vma=False)
```

```python
import functools
import math

import jax
import jax.numpy as jnp
from jax import lax
from jax.experimental import pallas as pl
from jax.experimental.pallas import tpu as pltpu
from jax.sharding import PartitionSpec as P

HD = 64
BLK = 64
PACKED = 4
LANES = PACKED * HD
LISTED = 8
EXTRA = 4

EPSILON = 1e-06
NEG_FILL = -1e30
MESH = pl.DeviceIdType.MESH
MIB = 1 << 20
MID_ROWS = 256
MID_CHUNK = 768
GAP = 0
EARLY = 4
PACE = (2,) * 12


def lasting(microseconds):
    return pl.CostEstimate(
        flops=int(microseconds * 1e9), bytes_accessed=int(microseconds * 1e6), transcendentals=0
    )


def request_tables(random_rows, cycle_size, blocks_here):
    wanted = random_rows.reshape(cycle_size, 3 * blocks_here)
    source = wanted // blocks_here
    within = wanted % blocks_here
    positions = jnp.arange(wanted.shape[1])
    earlier = positions[None, :] < positions[:, None]
    same_source = source[:, :, None] == source[:, None, :]
    ranking = jnp.sum(same_source & earlier[None], axis=2, dtype=jnp.int32)
    return (source, within, ranking)


def send_slots(source, within, ranking, own_index, capacity):
    slot_ids = jnp.arange(capacity, dtype=jnp.int32)
    selected = (source[:, None, :] == own_index) & (ranking[:, None, :] == slot_ids[None, :, None])
    filled = jnp.any(selected, axis=2)
    picked = jnp.sum(jnp.where(selected, within[:, None, :], 0), axis=2, dtype=jnp.int32)
    return (filled.astype(jnp.int32), picked)


def key_slots(own_source, own_rank, blocks_here, capacity):
    block = jnp.arange(blocks_here, dtype=jnp.int32)
    left = jnp.where(block == 0, blocks_here, block - 1)
    right = jnp.where(block == blocks_here - 1, blocks_here + 1, block + 1)
    drawn = (blocks_here + EXTRA + (own_source - 1) * capacity + own_rank).reshape(blocks_here, 3)
    fixed = jnp.stack(
        [
            left,
            block,
            right,
            jnp.full_like(block, blocks_here + 2),
            jnp.full_like(block, blocks_here + 3),
        ],
        axis=1,
    )
    return jnp.concatenate([fixed, drawn], axis=1).astype(jnp.int32)


def pack_kernel(picked_ref, rows_ref, out_ref, sems):
    slots = out_ref.shape[0]

    def copy(i):
        return pltpu.make_async_copy(rows_ref.at[picked_ref[i]], out_ref.at[i], sems.at[i])

    @pl.loop(0, slots)
    def _(i):
        copy(i).start()

    @pl.loop(0, slots)
    def _(i):
        copy(i).wait()


def pack_blocks(rows, picked):
    slots = picked.shape[0]
    return pl.pallas_call(
        pack_kernel,
        out_shape=jax.ShapeDtypeStruct((slots,) + rows.shape[1:], rows.dtype),
        grid_spec=pltpu.PrefetchScalarGridSpec(
            num_scalar_prefetch=1,
            grid=(1,),
            in_specs=[pl.BlockSpec(rows.shape, lambda i, t: (0, 0, 0))],
            out_specs=pl.BlockSpec(memory_space=pl.ANY),
            scratch_shapes=[pltpu.SemaphoreType.DMA((slots,))],
        ),
        name="pack_blocks",
    )(picked, rows)


def greet(count, groups):
    barrier = pltpu.get_barrier_semaphore()
    me = lax.axis_index("ctx")
    w = lax.axis_index("wsh")

    @pl.loop(1, count)
    def _(delta):
        pl.semaphore_signal(
            barrier, inc=1, device_id={"ctx": (me + delta) % count}, device_id_type=MESH
        )

    for delta in range(1, groups):
        pl.semaphore_signal(
            barrier, inc=1, device_id={"wsh": (w + delta) % groups}, device_id_type=MESH
        )
    pl.semaphore_wait(barrier, count + groups - 2)


def relays(count):
    return ((3, 2, (4, 6)), (4, 5, (3, 1))) if count == 8 else ()


def spread_kernel(count, capacity, *refs):
    weights = (len(refs) - 2 - 2 - 14) // 3
    pack, rows = refs[:2]
    shards = refs[2 : 2 + weights]
    ext, passing = refs[2 + weights : 4 + weights]
    fulls = refs[4 + weights : 4 + 2 * weights]
    rest = refs[4 + 2 * weights :]
    held = rest[:weights]
    rand_s, rand_r, halo_s, halo_r, glob_s, glob_r, wgt_s, wgt_r = rest[weights : weights + 8]
    pass_s, pass_r, loc_in, loc_out, own_pack, own_row = rest[weights + 8 :]
    blocks = rows.shape[0]
    base = blocks + EXTRA
    me = lax.axis_index("ctx")
    w = lax.axis_index("wsh")
    sib = w + 1 - 2 * (w % 2)
    far = (w + 2) % 4
    last = count - 1
    is_source = jnp.logical_and(me >= 1, me <= last - 1)
    routes = relays(count)
    greet(count, 4)

    def relayed(dst):
        found = me < 0
        for source, _, targets in routes:
            for target in targets:
                found = jnp.logical_or(found, jnp.logical_and(me == source, dst == target))
        return found

    def weight_copy(i, step):
        if step == 2:
            src, dst, target = fulls[i].at[far], fulls[i].at[far], sib
        else:
            src, dst, target = shards[i], fulls[i].at[w], (far, sib)[step]
        return pltpu.make_async_remote_copy(
            src_ref=src,
            dst_ref=dst,
            send_sem=wgt_s.at[i, step],
            recv_sem=wgt_r.at[i, step],
            device_id={"wsh": target},
            device_id_type=MESH,
        )

    def random_copy(dst, k):
        return pltpu.make_async_remote_copy(
            src_ref=pack.at[dst, k],
            dst_ref=ext.at[base + (me - 1) * capacity + k],
            send_sem=rand_s.at[dst, k],
            recv_sem=rand_r.at[me, k],
            device_id={"ctx": dst},
            device_id_type=MESH,
        )

    def random_landed(source, k):
        return pltpu.make_async_remote_copy(
            src_ref=pack.at[source, k],
            dst_ref=ext.at[base + (source - 1) * capacity + k],
            send_sem=rand_s.at[source, k],
            recv_sem=rand_r.at[source, k],
            device_id={"ctx": source},
            device_id_type=MESH,
        )

    def to_relay(via, r, dst, k):
        return pltpu.make_async_remote_copy(
            src_ref=pack.at[dst, k],
            dst_ref=passing.at[r, k],
            send_sem=rand_s.at[dst, k],
            recv_sem=pass_r.at[r, k],
            device_id={"ctx": via},
            device_id_type=MESH,
        )

    def from_relay(source, r, dst, k):
        return pltpu.make_async_remote_copy(
            src_ref=passing.at[r, k],
            dst_ref=ext.at[base + (source - 1) * capacity + k],
            send_sem=pass_s.at[r, k],
            recv_sem=rand_r.at[source, k],
            device_id={"ctx": dst},
            device_id_type=MESH,
        )

    def halo_copy(side):
        return pltpu.make_async_remote_copy(
            src_ref=rows.at[blocks - 1 if side == 0 else 0],
            dst_ref=ext.at[blocks + side],
            send_sem=halo_s.at[side],
            recv_sem=halo_r.at[side],
            device_id={"ctx": me + 1 if side == 0 else me - 1},
            device_id_type=MESH,
        )

    def global_copy(which, dst):
        return pltpu.make_async_remote_copy(
            src_ref=rows.at[0 if which == 0 else blocks - 1],
            dst_ref=ext.at[blocks + 2 + which],
            send_sem=glob_s.at[dst],
            recv_sem=glob_r.at[which],
            device_id={"ctx": dst},
            device_id_type=MESH,
        )

    def held_in(i):
        return pltpu.make_async_copy(shards[i], held[i], loc_in.at[2 + i])

    def held_out(i):
        return pltpu.make_async_copy(held[i], fulls[i].at[w], loc_out.at[2 + i])

    def rows_in():
        return pltpu.make_async_copy(rows, own_row, loc_in.at[0])

    def rows_out():
        return pltpu.make_async_copy(own_row, ext.at[pl.ds(0, blocks)], loc_out.at[0])

    def pack_in():
        return pltpu.make_async_copy(pack.at[me], own_pack, loc_in.at[1])

    def pack_out():
        return pltpu.make_async_copy(
            own_pack, ext.at[pl.ds(base + (me - 1) * capacity, capacity)], loc_out.at[1]
        )

    def rim_out(side):
        return pltpu.make_async_copy(own_row.at[0], ext.at[blocks + side], loc_out.at[2 + weights])

    def global_out(which):
        return pltpu.make_async_copy(
            own_row.at[0 if which == 0 else blocks - 1],
            ext.at[blocks + 2 + which],
            loc_out.at[3 + weights],
        )

    for i in range(weights):
        weight_copy(i, 0).start()
        weight_copy(i, 1).start()

    @pl.when(me < last)
    def _():
        halo_copy(0).start()

    @pl.when(me > 0)
    def _():
        halo_copy(1).start()

    for which, owner in ((0, 0), (1, last)):

        @pl.when(me == owner)
        def _():
            @pl.loop(1, count)
            def _(delta):
                global_copy(which, (me + delta) % count).start()

    for k in range(capacity):
        for source, via, targets in routes:

            @pl.when(me == source)
            def _():
                for r, target in enumerate(targets):
                    to_relay(via, r, target, k).start()

        @pl.when(is_source)
        def _():
            @pl.loop(1, count)
            def _(delta):
                dst = (me + delta) % count

                @pl.when(jnp.logical_not(relayed(dst)))
                def _():
                    random_copy(dst, k).start()

    rows_in().start()
    for i in range(weights):
        held_in(i).start()

    @pl.when(is_source)
    def _():
        pack_in().start()
        pack_in().wait()
        pack_out().start()

    rows_in().wait()
    rows_out().start()
    for which, owner in ((0, 0), (1, last)):

        @pl.when(me == owner)
        def _():
            rim_out(which).start()
            global_out(which).start()

    for i in range(weights):
        held_in(i).wait()
        held_out(i).start()

    for step in range(max(capacity, weights)):
        if step < capacity:
            for source, via, targets in routes:

                @pl.when(me == via)
                def _():
                    for r, target in enumerate(targets):
                        to_relay(via, r, target, step).wait_recv()
                        from_relay(source, r, target, step).start()

        if step < weights:
            weight_copy(step, 0).wait_recv()
            weight_copy(step, 2).start()

    rows_out().wait()
    for i in range(weights):
        held_out(i).wait()

    @pl.when(is_source)
    def _():
        pack_out().wait()

        for k in range(capacity):

            @pl.loop(1, count)
            def _(delta):
                random_copy((me + delta) % count, k).wait_send()

    for source, via, targets in routes:

        @pl.when(me == via)
        def _():
            for r, target in enumerate(targets):
                for k in range(capacity):
                    from_relay(source, r, target, k).wait_send()

    for which, owner in ((0, 0), (1, last)):

        @pl.when(me == owner)
        def _():
            rim_out(which).wait()
            global_out(which).wait()

            @pl.loop(1, count)
            def _(delta):
                global_copy(which, (me + delta) % count).wait_send()

        @pl.when(me != owner)
        def _():
            global_copy(which, owner).wait_recv()

    @pl.when(me < last)
    def _():
        halo_copy(0).wait_send()
        halo_copy(1).wait_recv()

    @pl.when(me > 0)
    def _():
        halo_copy(1).wait_send()
        halo_copy(0).wait_recv()

    for k in range(capacity):

        @pl.loop(1, last)
        def _(source):
            @pl.when(source != me)
            def _():
                random_landed(source, k).wait_recv()

    for i in range(weights):
        for step in range(3):
            weight_copy(i, step).wait_send()
        weight_copy(i, 1).wait_recv()
        weight_copy(i, 2).wait_recv()


def spread(pack, rows, shards, count, capacity):
    blocks = rows.shape[0]
    tail = rows.shape[1:]
    weights = len(shards)
    slots = blocks + EXTRA + (count - 2) * capacity
    outs = pl.pallas_call(
        functools.partial(spread_kernel, count, capacity),
        out_shape=[
            jax.ShapeDtypeStruct((slots,) + tail, rows.dtype),
            jax.ShapeDtypeStruct((2, capacity) + tail, rows.dtype),
        ]
        + [jax.ShapeDtypeStruct((4,) + shard.shape, shard.dtype) for shard in shards],
        in_specs=[pl.BlockSpec(memory_space=pl.ANY)] * (2 + weights),
        out_specs=[pl.BlockSpec(memory_space=pl.ANY)] * (2 + weights),
        scratch_shapes=[pltpu.VMEM(shard.shape, shard.dtype) for shard in shards]
        + [
            pltpu.SemaphoreType.DMA((count, capacity)),
            pltpu.SemaphoreType.DMA((count, capacity)),
            pltpu.SemaphoreType.DMA((2,)),
            pltpu.SemaphoreType.DMA((2,)),
            pltpu.SemaphoreType.DMA((count,)),
            pltpu.SemaphoreType.DMA((2,)),
            pltpu.SemaphoreType.DMA((weights, 3)),
            pltpu.SemaphoreType.DMA((weights, 3)),
            pltpu.SemaphoreType.DMA((2, capacity)),
            pltpu.SemaphoreType.DMA((2, capacity)),
            pltpu.SemaphoreType.DMA((4 + weights,)),
            pltpu.SemaphoreType.DMA((4 + weights,)),
            pltpu.VMEM((capacity,) + tail, rows.dtype),
            pltpu.VMEM(rows.shape, rows.dtype),
        ],
        compiler_params=pltpu.CompilerParams(
            collective_id=0, has_side_effects=True, vmem_limit_bytes=56 * MIB
        ),
        cost_estimate=lasting(110),
        name="spread_rows",
    )(pack, rows, *shards)
    return outs[0], outs[2:]


class Reducer:
    def __init__(self, count, unit, staged, out, scratch):
        self.unit = unit
        self.staged = staged
        self.out = out
        (
            self.ring,
            self.from_sib,
            self.from_far,
            self.from_pair,
            self.chain_in,
            self.load_sem,
            self.sib_s,
            self.sib_r,
            self.far_s,
            self.far_r,
            self.pair_s,
            self.pair_r,
            self.chain_s,
            self.chain_r,
            self.wide_s,
            self.wide_r,
            self.back_s,
            self.back_r,
        ) = scratch
        self.units = out.shape[0]
        self.top = count // 2 - 1
        me = lax.axis_index("ctx")
        w = lax.axis_index("wsh")
        self.w = w
        self.me = me
        self.sib = w + 1 - 2 * (w % 2)
        self.far = (w + 2) % 4
        self.sib_far = (self.sib + 2) % 4
        self.side = me % 2
        self.level = me // 2
        self.pair = me + 1 - 2 * self.side

    def load(self, u, slot):
        return pltpu.make_async_copy(
            self.unit(u, (self.w, self.far)[slot]),
            self.ring.at[u % 2, slot],
            self.load_sem.at[u, slot],
        )

    def remote(self, src, dst, send, recv, **device):
        return pltpu.make_async_remote_copy(
            src_ref=src,
            dst_ref=dst,
            send_sem=send,
            recv_sem=recv,
            device_id=device,
            device_id_type=MESH,
        )

    def to_sib(self, u, slot):
        return self.remote(
            self.unit(u, (self.sib, self.sib_far)[slot]),
            self.from_sib.at[u, slot],
            self.sib_s.at[u, slot],
            self.sib_r.at[u, slot],
            wsh=self.sib,
        )

    def to_far(self, u):
        return self.remote(
            self.from_sib.at[u, 1],
            self.from_far.at[u],
            self.far_s.at[u],
            self.far_r.at[u],
            wsh=self.far,
        )

    def half(self, u, side):
        rows = self.out.shape[2]
        return self.from_sib.at[u, 0, pl.ds(pl.multiple_of(side * rows, rows), rows)]

    def to_pair(self, u):
        return self.remote(
            self.half(u, 1 - self.side),
            self.from_pair.at[u],
            self.pair_s.at[u],
            self.pair_r.at[u],
            ctx=self.pair,
        )

    def toward(self, u):
        return 2 if u % 2 == 0 else -2

    def place(self, u, hop):
        return hop if u % 2 == 0 else self.top - hop

    def along(self, u):
        return self.remote(
            self.from_pair.at[u],
            self.chain_in.at[u],
            self.chain_s.at[u],
            self.chain_r.at[u],
            ctx=self.me + self.toward(u),
        )

    def widen(self, u):
        place = self.out.at[u, self.side]
        return self.remote(
            place, place, self.wide_s.at[u], self.wide_r.at[u], ctx=self.me - self.toward(u)
        )

    def give_back(self, u, side):
        place = self.out.at[u, side]
        return self.remote(place, place, self.back_s.at[u], self.back_r.at[u], ctx=self.pair)


    def begin(self, u):
        for slot in (1, 0):
            self.to_sib(u, slot).start()
            if u < min(2, self.staged):
                self.load(u, slot).start()

    def join_sib(self, u):
        for slot in (1, 0):
            if u < self.staged:
                self.load(u, slot).wait()
                own = self.ring[u % 2, slot]
            else:
                own = self.unit(u, (self.w, self.far)[slot])[...]
            self.to_sib(u, slot).wait_recv()
            self.from_sib[u, slot] = add_bf16(own, self.from_sib[u, slot])
            if slot == 1:
                self.to_far(u).start()
            if u + 2 < self.staged:
                self.load(u + 2, slot).start()

    def join_far(self, u):
        self.to_far(u).wait_recv()
        self.from_sib[u, 0] = add_bf16(self.from_sib[u, 0], self.from_far[u])
        self.to_pair(u).start()

    def join_pair(self, u):
        self.to_pair(u).wait_recv()
        self.from_pair[u] = add_bf16(self.half(u, self.side)[...], self.from_pair[u])

    def gather(self, u, hop):
        @pl.when(self.level == self.place(u, hop))
        def _():
            if hop > 0:
                self.along(u).wait_recv()
                total = add_bf16(self.from_pair[u], self.chain_in[u])
                if hop < self.top:
                    self.from_pair[u] = total
                else:
                    self.out[u, self.side] = total
            if hop < self.top:
                self.along(u).start()
            else:
                self.widen(u).start()
                self.give_back(u, self.side).start()

    def spread_out(self, u, hop):
        @pl.when(self.level == self.place(u, hop))
        def _():
            self.widen(u).wait_recv()
            if hop > 0:
                self.widen(u).start()
            self.give_back(u, self.side).start()

    def step(self, t):
        def unit(lag):
            u = t - lag
            if u >= self.staged:
                u = u - GAP if u >= self.staged + GAP else -1
            return u if 0 <= u < self.units else None

        if unit(0) is not None:
            self.join_far(unit(0))
        if unit(1) is not None:
            self.join_pair(unit(1))
        lag = 1
        for hop in range(self.top + 1):
            if unit(lag) is not None:
                self.gather(unit(lag), hop)
            lag += 1
        for hop in range(self.top - 1, -1, -1):
            if unit(lag) is not None:
                self.spread_out(unit(lag), hop)
            lag += 1

    def steps(self):
        return self.units + GAP + 2 * self.top + 1

    def finish(self):
        for u in range(self.units):
            self.give_back(u, 1 - self.side).wait_recv()
            self.give_back(u, self.side).wait_send()

            @pl.when(self.level != self.place(u, self.top))
            def _():
                self.along(u).wait_send()

            @pl.when(self.level != self.place(u, 0))
            def _():
                self.widen(u).wait_send()

            for slot in range(2):
                self.to_sib(u, slot).wait_send()
            self.to_far(u).wait_send()
            self.to_pair(u).wait_send()


def add_bf16(left, right):
    return (left.astype(jnp.float32) + right.astype(jnp.float32)).astype(jnp.bfloat16)


def reducer_shapes(units, part, features):
    dma = pltpu.SemaphoreType.DMA
    kind = jnp.bfloat16
    out = jax.ShapeDtypeStruct((units, 2, part // 2, features), kind)
    scratch = [
        pltpu.VMEM((2, 2, part, features), kind),
        pltpu.VMEM((units, 2, part, features), kind),
        pltpu.VMEM((units, part, features), kind),
        pltpu.VMEM((units, part // 2, features), kind),
        pltpu.VMEM((units, part // 2, features), kind),
        dma((units, 2)),
        dma((units, 2)),
        dma((units, 2)),
    ] + [dma((units,)) for _ in range(10)]
    return out, scratch


class Returner:
    def __init__(self, count, capacity, far_ref, rim_ref, outs, small, sems):
        self.count, self.capacity, self.small = count, capacity, small
        self.far_ref, self.rim_ref = far_ref, rim_ref
        self.back, self.rim, self.glob, self.small_out = outs
        (
            self.rand_s,
            self.rand_r,
            self.halo_s,
            self.halo_r,
            self.glob_s,
            self.glob_r,
            self.loc,
            self.group_part,
            self.ring_part,
            self.group_s,
            self.group_r,
            self.ring_s,
            self.ring_r,
        ) = sems
        self.me = lax.axis_index("ctx")
        self.w = lax.axis_index("wsh")
        self.last = count - 1
        self.groups = small.shape[0]
        self.is_source = jnp.logical_and(self.me >= 1, self.me <= self.last - 1)

    def remote(self, src, dst, send, recv, **device):
        return pltpu.make_async_remote_copy(
            src_ref=src,
            dst_ref=dst,
            send_sem=send,
            recv_sem=recv,
            device_id=device,
            device_id_type=MESH,
        )

    def random_copy(self, owner, k):
        return self.remote(
            self.far_ref.at[(owner - 1) * self.capacity + k],
            self.back.at[self.me, k],
            self.rand_s.at[owner, k],
            self.rand_r.at[self.me, k],
            ctx=owner,
        )

    def landed(self, sender, k):
        return self.remote(
            self.far_ref.at[k],
            self.back.at[sender, k],
            self.rand_s.at[sender, k],
            self.rand_r.at[sender, k],
            ctx=sender,
        )

    def own_random(self):
        return pltpu.make_async_copy(
            self.far_ref.at[pl.ds((self.me - 1) * self.capacity, self.capacity)],
            self.back.at[self.me],
            self.loc.at[0],
        )

    def halo_copy(self, side):
        return self.remote(
            self.rim_ref.at[side],
            self.rim.at[1 - side],
            self.halo_s.at[side],
            self.halo_r.at[side],
            ctx=self.me - 1 if side == 0 else self.me + 1,
        )

    def global_copy(self, which, sender):
        return self.remote(
            self.rim_ref.at[2 + which],
            self.glob.at[sender],
            self.glob_s.at[which],
            self.glob_r.at[sender],
            ctx=0 if which == 0 else self.last,
        )

    def own_global(self, which):
        return pltpu.make_async_copy(
            self.rim_ref.at[2 + which], self.glob.at[self.me], self.loc.at[1]
        )

    def group_copy(self, target, sender):
        return self.remote(
            self.small.at[target],
            self.group_part.at[sender],
            self.group_s.at[target],
            self.group_r.at[sender],
            wsh=target,
        )

    def ring_copy(self, target, sender):
        return self.remote(
            self.ring_part.at[self.me],
            self.ring_part.at[sender],
            self.ring_s.at[target],
            self.ring_r.at[sender],
            ctx=target,
        )

    def send_random(self, owner, slots):
        @pl.when(owner != self.me)
        def _():
            for k in slots:
                self.random_copy(owner, k).start()

    def send_round(self, k):
        @pl.loop(0, self.count - 2)
        def _(i):
            self.send_random(1 + (self.me + i) % (self.count - 2), (k,))

    def keep_own(self):
        @pl.when(self.is_source)
        def _():
            self.own_random().start()

    def send_rims(self):
        @pl.when(self.me > 0)
        def _():
            self.halo_copy(0).start()
            self.global_copy(0, self.me).start()

        @pl.when(self.me < self.last)
        def _():
            self.halo_copy(1).start()
            self.global_copy(1, self.me).start()

        for which, owner in ((0, 0), (1, self.last)):

            @pl.when(self.me == owner)
            def _():
                self.own_global(which).start()

    def send_small(self):
        for delta in range(1, self.groups):
            self.group_copy((self.w + delta) % self.groups, self.w).start()

    def pass_small(self):
        total = self.small[self.w]
        for delta in range(1, self.groups):
            sender = (self.w + delta) % self.groups
            self.group_copy(self.w, sender).wait_recv()
            total = total + self.group_part[sender]
        self.ring_part[self.me] = total

        @pl.loop(1, self.count)
        def _(delta):
            self.ring_copy((self.me + delta) % self.count, self.me).start()

    def end_small(self):
        @pl.loop(1, self.count)
        def _(delta):
            self.ring_copy(self.me, (self.me + delta) % self.count).wait_recv()

        self.small_out[...] = jnp.sum(self.ring_part[...], axis=0)

        @pl.loop(1, self.count)
        def _(delta):
            self.ring_copy((self.me + delta) % self.count, self.me).wait_send()

        for delta in range(1, self.groups):
            self.group_copy((self.w + delta) % self.groups, self.w).wait_send()

    def finish(self):
        @pl.when(self.is_source)
        def _():
            self.own_random().wait()

            @pl.loop(0, self.count)
            def _(sender):
                @pl.when(sender != self.me)
                def _():
                    for k in range(self.capacity):
                        self.landed(sender, k).wait_recv()

        for which, owner in ((0, 0), (1, self.last)):

            @pl.when(self.me == owner)
            def _():
                self.own_global(which).wait()

                @pl.loop(0, self.count)
                def _(sender):
                    @pl.when(sender != self.me)
                    def _():
                        self.global_copy(which, sender).wait_recv()

        @pl.when(self.me > 0)
        def _():
            self.halo_copy(0).wait_send()
            self.halo_copy(1).wait_recv()
            self.global_copy(0, self.me).wait_send()

        @pl.when(self.me < self.last)
        def _():
            self.halo_copy(1).wait_send()
            self.halo_copy(0).wait_recv()
            self.global_copy(1, self.me).wait_send()

        @pl.loop(1, self.last)
        def _(owner):
            @pl.when(owner != self.me)
            def _():
                for k in range(self.capacity):
                    self.random_copy(owner, k).wait_send()


def returner_shapes(count, capacity, tail, small):
    kind = jnp.bfloat16
    dma = pltpu.SemaphoreType.DMA
    groups = small.shape[0]
    outs = [
        jax.ShapeDtypeStruct((count, capacity) + tail, kind),
        jax.ShapeDtypeStruct((2,) + tail, kind),
        jax.ShapeDtypeStruct((count,) + tail, kind),
        jax.ShapeDtypeStruct(small.shape[1:], jnp.float32),
    ]
    sems = [
        dma((count, capacity)),
        dma((count, capacity)),
        dma((2,)),
        dma((2,)),
        dma((2,)),
        dma((count,)),
        dma((2,)),
        pltpu.VMEM(small.shape, jnp.float32),
        pltpu.VMEM((count,) + small.shape[1:], jnp.float32),
        dma((groups,)),
        dma((groups,)),
        dma((count,)),
        dma((count,)),
    ]
    return outs, sems


HBM_SPEC = pl.BlockSpec(memory_space=pl.ANY)
VMEM_SPEC = pl.BlockSpec(memory_space=pltpu.VMEM)
RETURN_SPECS = [HBM_SPEC, HBM_SPEC, HBM_SPEC, VMEM_SPEC]


def return_kernel(count, capacity, far_ref, rim_ref, small, *refs):
    mover = Returner(count, capacity, far_ref, rim_ref, refs[:4], small, refs[4:])
    greet(count, small.shape[0])
    mover.send_small()
    mover.send_rims()

    for k in range(capacity):
        mover.send_round(k)
    mover.keep_own()
    mover.pass_small()
    mover.end_small()
    mover.finish()


def return_grads(far_grad, small, count, capacity):
    tail = far_grad.shape[1:]
    outs, sems = returner_shapes(count, capacity, tail, small)
    return pl.pallas_call(
        functools.partial(return_kernel, count, capacity),
        out_shape=outs,
        in_specs=[VMEM_SPEC, VMEM_SPEC, VMEM_SPEC],
        out_specs=RETURN_SPECS,
        scratch_shapes=sems,
        compiler_params=pltpu.CompilerParams(
            collective_id=1, has_side_effects=True, vmem_limit_bytes=56 * MIB
        ),
        name="return_grads",
    )(far_grad[EXTRA:], far_grad[:EXTRA], small)


def tail_kernel(
    count,
    capacity,
    dq_hbm,
    dk_hbm,
    dv_hbm,
    x_hbm,
    stream_hbm,
    outer_hbm,
    inner_hbm,
    wo_hbm,
    wq_ref,
    wk_ref,
    wv_ref,
    small_in,
    *refs,
):
    outs, near_hbm, sums = refs[:4], refs[4], refs[5]
    (
        xbuf,
        kbuf,
        vbuf,
        qbuf,
        wq_sum,
        wk_sum,
        wv_sum,
        shares,
        sending,
        rims,
        stage,
        small,
        bias_sum,
        load_sem,
        q_sem,
        stage_sem,
    ) = refs[6:22]
    returner_sems, reducer_scratch = refs[22:35], refs[35:]
    blocks, _, features = dq_hbm.shape
    length = blocks * BLK
    near = blocks + EXTRA
    chunk = capacity * BLK
    part = features // 4
    me = lax.axis_index("ctx")
    sources = count - 2
    mover = Returner(count, capacity, sending, rims, outs, small, returner_sems)
    across = inner_hbm.shape[2] // features
    stacked = outer_hbm.shape[1] // part
    staged = stacked + across + 1

    def unit(u, quarter):
        if u < stacked:
            return outer_hbm.at[quarter, pl.ds(u * part, part)]
        if u < stacked + across:
            return inner_hbm.at[quarter, :, pl.ds((u - stacked) * features, features)]
        if u < staged:
            return wo_hbm.at[quarter]
        return shares.at[u - staged, quarter]

    reducer = Reducer(count, unit, staged, sums, reducer_scratch)

    def loads(at, slot, size):
        here, there = pl.ds(at, size), pl.ds(0, size)
        return [
            pltpu.make_async_copy(src.at[here], dst.at[slot, there], load_sem.at[slot, n])
            for n, (src, dst) in enumerate(((x_hbm, xbuf), (dk_hbm, kbuf), (dv_hbm, vbuf)))
        ]

    def far_loads(i, slot):
        return loads(near + ((me + i) % sources) * capacity, slot, capacity)

    def own_loads(n):
        half = blocks // 2
        return loads(n * half, n, half) + [
            pltpu.make_async_copy(dq_hbm.at[pl.ds(n * half, half)], qbuf.at[n], q_sem.at[n])
        ]

    def start(copies):
        for copy in copies:
            copy.start()

    def end(copies):
        for copy in copies:
            copy.wait()

    def gather_weights(rows, key_grad, value_grad):
        wk_sum[...] += tn(rows, key_grad)
        wv_sum[...] += tn(rows, value_grad)
        bias_sum[1:2] += jnp.sum(value_grad.astype(jnp.float32), axis=0, keepdims=True)

    start(far_loads(0, 0))
    greet(count, small.shape[0])
    for u in range(staged):
        reducer.begin(u)
    bias_sum[...] = jnp.zeros_like(bias_sum)
    wk_sum[...] = jnp.zeros_like(wk_sum)
    wv_sum[...] = jnp.zeros_like(wv_sum)

    for third in range(3):

        @pl.loop(third * sources // 3, (third + 1) * sources // 3)
        def _(i):
            slot = i % 2
            end(far_loads(i, slot))

            @pl.when(i + 1 < sources)
            def _():
                start(far_loads(i + 1, 1 - slot))

            key_grad = kbuf[slot].reshape(chunk, features)
            value_grad = vbuf[slot].reshape(chunk, features)
            row_grad = nt(key_grad, wk_ref[...]) + nt(value_grad, wv_ref[...])
            s = 1 + (me + i) % sources
            sending[pl.ds((s - 1) * capacity, capacity)] = row_grad.astype(sending.dtype).reshape(
                capacity, BLK, features
            )
            mover.send_random(s, range(EARLY))
            gather_weights(xbuf[slot].reshape(chunk, features), key_grad, value_grad)

        for u in range(third * staged // 3, (third + 1) * staged // 3):
            reducer.join_sib(u)
    mover.keep_own()

    rim_loads = loads(blocks, 0, EXTRA)
    start(rim_loads)
    end(rim_loads)
    rim_rows = EXTRA * BLK
    key_grad = kbuf[0, :EXTRA].reshape(rim_rows, features)
    value_grad = vbuf[0, :EXTRA].reshape(rim_rows, features)
    row_grad = nt(key_grad, wk_ref[...]) + nt(value_grad, wv_ref[...])
    rims[...] = row_grad.astype(rims.dtype).reshape(EXTRA, BLK, features)
    mover.send_rims()
    gather_weights(xbuf[0, :EXTRA].reshape(rim_rows, features), key_grad, value_grad)

    start(own_loads(0))
    start(own_loads(1))
    wq_sum[...] = jnp.zeros_like(wq_sum)
    half = length // 2

    def stage_load(n):
        return pltpu.make_async_copy(
            stream_hbm.at[pl.ds(n * half, half)], stage.at[n], stage_sem.at[0, n]
        )

    def stage_store(n):
        return pltpu.make_async_copy(
            stage.at[n], near_hbm.at[pl.ds(n * half, half)], stage_sem.at[1, n]
        )

    for n in range(2):
        stage_load(n).start()
        end(own_loads(n))

    @pl.loop(0, 2)
    def _(n):
        rows = xbuf[n].reshape(half, features)
        query_grad = qbuf[n].reshape(half, features)
        gather_weights(rows, kbuf[n].reshape(half, features), vbuf[n].reshape(half, features))
        wq_sum[...] += tn(rows, query_grad)
        bias_sum[0:1] += jnp.sum(query_grad.astype(jnp.float32), axis=0, keepdims=True)

    for u, total in ((0, wq_sum), (1, wk_sum), (2, wv_sum)):
        for quarter in range(4):
            shares[u, quarter] = total[quarter * part : (quarter + 1) * part].astype(shares.dtype)
        reducer.begin(staged + u)
    small[...] = small_in[...]
    for quarter in range(4):
        lanes = slice(quarter * part, (quarter + 1) * part)
        small[quarter, 0:2, :part] = bias_sum[0:2, lanes]
    mover.send_small()

    ticks = iter(range(reducer.steps()))
    waiting = list(range(EARLY * sources, capacity * sources))

    def advance():
        tick = next(ticks)
        reducer.step(tick)
        wave = PACE[tick] if tick < len(PACE) else 0
        for n in waiting[:wave]:
            mover.send_random(1 + (me + n % sources) % sources, (n // sources,))
        del waiting[:wave]
        return tick + 1

    advance()
    advance()
    for u in range(staged, reducer.units):
        reducer.join_sib(u)
    mover.pass_small()

    for n in range(2):
        stage_load(n).wait()
        stage[n] = (
            stage[n]
            + nt(qbuf[n].reshape(half, features), wq_ref[...])
            + nt(kbuf[n].reshape(half, features), wk_ref[...])
            + nt(vbuf[n].reshape(half, features), wv_ref[...])
        )
        stage_store(n).start()
        advance()
    while advance() < reducer.steps():
        pass
    for n in range(2):
        stage_store(n).wait()
    mover.end_small()
    reducer.finish()
    mover.finish()


def backward_tail(
    dq,
    dk,
    dv,
    ext_rows,
    stream_grad,
    outer_grad,
    inner_grad,
    output_grad,
    wq,
    wk,
    wv,
    small,
    count,
    capacity,
):
    blocks, block_rows, features = dq.shape
    tail = (block_rows, features)
    far_slots = (count - 2) * capacity
    part = features // 4
    outs, sems = returner_shapes(count, capacity, tail, small)
    units = outer_grad.shape[1] // part + inner_grad.shape[2] // features + 4
    sums, sum_scratch = reducer_shapes(units, part, features)
    kind = jnp.bfloat16
    dma = pltpu.SemaphoreType.DMA
    square = pltpu.VMEM((features, features), jnp.float32)
    some = pltpu.VMEM((2, capacity) + tail, kind)
    return pl.pallas_call(
        functools.partial(tail_kernel, count, capacity),
        out_shape=outs + [jax.ShapeDtypeStruct(stream_grad.shape, jnp.float32), sums],
        in_specs=[HBM_SPEC] * 8 + [VMEM_SPEC] * 4,
        out_specs=RETURN_SPECS + [HBM_SPEC, VMEM_SPEC],
        scratch_shapes=[some] * 4
        + [square] * 3
        + [
            pltpu.VMEM((3, 4, part, features), kind),
            pltpu.VMEM((far_slots,) + tail, kind),
            pltpu.VMEM((EXTRA,) + tail, kind),
            pltpu.VMEM((2, blocks * block_rows // 2, features), jnp.float32),
            pltpu.VMEM(small.shape, jnp.float32),
            pltpu.VMEM((8, features), jnp.float32),
            dma((2, 3)),
            dma((2,)),
            dma((2, 2)),
        ]
        + sems
        + sum_scratch,
        compiler_params=pltpu.CompilerParams(
            collective_id=1, has_side_effects=True, vmem_limit_bytes=58 * MIB
        ),
        cost_estimate=lasting(150),
        name="backward_tail",
    )(
        dq,
        dk,
        dv,
        ext_rows,
        stream_grad,
        outer_grad,
        inner_grad,
        output_grad,
        wq,
        wk,
        wv,
        small,
    )


def unpack_kernel(
    capacity, picked_ref, filled_ref, edge_ref, base_ref, back_ref, rim_ref, glob_ref, out_ref, acc
):
    step = pl.program_id(0)
    blocks = base_ref.shape[0]

    @pl.when(step == 0)
    def _():
        acc[...] = base_ref[...]

        @pl.when(edge_ref[0] == 0)
        def _():
            acc[0] += rim_ref[0].astype(jnp.float32)

        @pl.when(edge_ref[1] == 0)
        def _():
            acc[blocks - 1] += rim_ref[1].astype(jnp.float32)

    for k in range(capacity):
        slot = step * capacity + k

        @pl.when(filled_ref[slot] == 1)
        def _():
            acc[picked_ref[slot]] += back_ref[0, k].astype(jnp.float32)

    for which, block in ((0, 0), (1, blocks - 1)):

        @pl.when(edge_ref[which] == 1)
        def _():
            acc[block] += glob_ref[0].astype(jnp.float32)

    @pl.when(step == pl.num_programs(0) - 1)
    def _():
        out_ref[...] = acc[...].astype(out_ref.dtype)


def unpack_grads(base, back, rim, glob, picked, filled, edge):
    count, capacity = back.shape[:2]
    blocks, block_rows, features = base.shape
    return pl.pallas_call(
        functools.partial(unpack_kernel, capacity),
        out_shape=jax.ShapeDtypeStruct(base.shape, jnp.bfloat16),
        grid_spec=pltpu.PrefetchScalarGridSpec(
            num_scalar_prefetch=3,
            grid=(count,),
            in_specs=[
                pl.BlockSpec(base.shape, lambda i, *t: (0, 0, 0)),
                pl.BlockSpec((1,) + back.shape[1:], lambda i, *t: (i, 0, 0, 0)),
                pl.BlockSpec(rim.shape, lambda i, *t: (0, 0, 0)),
                pl.BlockSpec((1, block_rows, features), lambda i, *t: (i, 0, 0)),
            ],
            out_specs=pl.BlockSpec(base.shape, lambda i, *t: (0, 0, 0)),
            scratch_shapes=[pltpu.VMEM(base.shape, jnp.float32)],
        ),
        compiler_params=pltpu.CompilerParams(vmem_limit_bytes=32 * MIB),
        name="unpack_grads",
    )(picked, filled, edge, base, back, rim, glob)


def head_mask():
    rows = lax.broadcasted_iota(jnp.int32, (LANES, LANES), 0) // HD
    columns = lax.broadcasted_iota(jnp.int32, (LANES, LANES), 1) // HD
    return rows == columns


def spread_heads(block, mask):
    tiled = jnp.concatenate([block] * PACKED, axis=0)
    return jnp.where(mask, tiled, jnp.zeros_like(tiled))


def fold_heads(square, mask):
    kept = jnp.where(mask, square, 0.0)
    total = kept[:BLK]
    for i in range(1, PACKED):
        total = total + kept[i * BLK : (i + 1) * BLK]
    return total


def listed_rows(ref, index_ref, b):
    return jnp.concatenate([ref[index_ref[b * LISTED + j]] for j in range(LISTED)], axis=0)


def nt(left, right):
    return lax.dot_general(
        left, right, (((1,), (1,)), ((), ())), preferred_element_type=jnp.float32
    )


def nn(left, right):
    return jnp.dot(left, right, preferred_element_type=jnp.float32)


def tn(left, right):
    return lax.dot_general(
        left, right, (((0,), (0,)), ((), ())), preferred_element_type=jnp.float32
    )


def mask_edges(scores, edge_ref, b, blocks):
    low = jnp.logical_and(b == 0, edge_ref[0] == 1)
    high = jnp.logical_and(b == blocks - 1, edge_ref[1] == 1)
    first = jnp.where(low, NEG_FILL, scores[:BLK])
    third = jnp.where(high, NEG_FILL, scores[2 * BLK : 3 * BLK])
    return jnp.concatenate([first, scores[BLK : 2 * BLK], third, scores[3 * BLK :]], axis=0)


def forward_kernel(index_ref, edge_ref, q_ref, k_ref, v_ref, o_ref, log_ref):
    blocks = q_ref.shape[0]
    mask = head_mask()

    @pl.loop(0, blocks, unroll=True)
    def _(b):
        query = spread_heads(q_ref[b] * HD**-0.5, mask)
        scores = mask_edges(nt(listed_rows(k_ref, index_ref, b), query), edge_ref, b, blocks)
        top = jnp.max(scores, axis=0, keepdims=True)
        raised = jnp.exp(scores - top)
        total = jnp.sum(raised, axis=0, keepdims=True)
        probs = (raised * (1.0 / total)).astype(jnp.bfloat16)
        log_ref[b] = top + jnp.log(total)
        mixed = tn(probs, listed_rows(v_ref, index_ref, b))
        o_ref[b] = fold_heads(mixed, mask).astype(o_ref.dtype)


def attend(queries, keys, values, index, edge):
    blocks, block_rows, features = queries.shape
    slots = keys.shape[0]
    groups = features // LANES
    column = lambda g, *t: (0, 0, g)
    return pl.pallas_call(
        forward_kernel,
        out_shape=[
            jax.ShapeDtypeStruct(queries.shape, jnp.bfloat16),
            jax.ShapeDtypeStruct((blocks, 1, features), jnp.float32),
        ],
        grid_spec=pltpu.PrefetchScalarGridSpec(
            num_scalar_prefetch=2,
            grid=(groups,),
            in_specs=[
                pl.BlockSpec((blocks, block_rows, LANES), column),
                pl.BlockSpec((slots, block_rows, LANES), column),
                pl.BlockSpec((slots, block_rows, LANES), column),
            ],
            out_specs=[
                pl.BlockSpec((blocks, block_rows, LANES), column),
                pl.BlockSpec((blocks, 1, LANES), column),
            ],
        ),
        compiler_params=pltpu.CompilerParams(vmem_limit_bytes=40 * MIB),
        cost_estimate=lasting(37),
        name="attend",
    )(index, edge, queries, keys, values)


def backward_kernel(
    index_ref,
    edge_ref,
    q_ref,
    g_ref,
    k_ref,
    v_ref,
    log_ref,
    dq_ref,
    dk_ref,
    dv_ref,
    key_sum,
    value_sum,
):
    blocks = q_ref.shape[0]
    near = blocks + EXTRA
    mask = head_mask()
    key_sum[...] = jnp.zeros_like(key_sum)
    value_sum[...] = jnp.zeros_like(value_sum)
    dk_ref[...] = jnp.zeros_like(dk_ref)
    dv_ref[...] = jnp.zeros_like(dv_ref)

    @pl.loop(0, blocks, unroll=True)
    def _(b):
        query = spread_heads(q_ref[b] * HD**-0.5, mask)
        upstream = spread_heads(g_ref[b], mask)
        key_rows = listed_rows(k_ref, index_ref, b)
        scores = mask_edges(nt(key_rows, query), edge_ref, b, blocks)
        probs = jnp.exp(scores - log_ref[b])
        prob_grad = nt(listed_rows(v_ref, index_ref, b), upstream)
        delta = jnp.sum(probs * prob_grad, axis=0, keepdims=True)
        score_grad = (probs * (prob_grad - delta)).astype(jnp.bfloat16)
        value_grad = nn(probs.astype(jnp.bfloat16), upstream)
        key_grad = nn(score_grad, query)
        query_grad = fold_heads(tn(score_grad, key_rows), mask) * HD**-0.5
        dq_ref[b] = query_grad.astype(dq_ref.dtype)
        for j in range(LISTED):
            slot = index_ref[b * LISTED + j]
            piece = slice(j * BLK, (j + 1) * BLK)
            if j < 5:
                key_sum[slot] += key_grad[piece]
                value_sum[slot] += value_grad[piece]
            else:
                dk_ref[slot] = key_grad[piece].astype(dk_ref.dtype)
                dv_ref[slot] = value_grad[piece].astype(dv_ref.dtype)

    dk_ref[:near] = key_sum[...].astype(dk_ref.dtype)
    dv_ref[:near] = value_sum[...].astype(dv_ref.dtype)


def attend_back(queries, upstream, keys, values, log_total, index, edge):
    blocks, block_rows, features = queries.shape
    slots = keys.shape[0]
    groups = features // LANES
    column = lambda g, *t: (0, 0, g)
    few = pl.BlockSpec((blocks, block_rows, LANES), column)
    many = pl.BlockSpec((slots, block_rows, LANES), column)
    return pl.pallas_call(
        backward_kernel,
        out_shape=[
            jax.ShapeDtypeStruct(queries.shape, jnp.bfloat16),
            jax.ShapeDtypeStruct(keys.shape, jnp.bfloat16),
            jax.ShapeDtypeStruct(keys.shape, jnp.bfloat16),
        ],
        grid_spec=pltpu.PrefetchScalarGridSpec(
            num_scalar_prefetch=2,
            grid=(groups,),
            in_specs=[few, few, many, many, pl.BlockSpec((blocks, 1, LANES), column)],
            out_specs=[few, many, many],
            scratch_shapes=[
                pltpu.VMEM((blocks + EXTRA, block_rows, LANES), jnp.float32),
                pltpu.VMEM((blocks + EXTRA, block_rows, LANES), jnp.float32),
            ],
        ),
        compiler_params=pltpu.CompilerParams(vmem_limit_bytes=48 * MIB),
        cost_estimate=lasting(44),
        name="attend_back",
    )(index, edge, queries, upstream, keys, values, log_total)


def project_kernel(rows_ref, wk_ref, wv_ref, bias_ref, k_ref, v_ref):
    count, block_rows, features = rows_ref.shape
    rows = rows_ref[...].reshape(count * block_rows, features)
    k_ref[...] = nn(rows, wk_ref[...]).astype(k_ref.dtype).reshape(k_ref.shape)
    values = nn(rows, wv_ref[...]) + bias_ref[...]
    v_ref[...] = values.astype(v_ref.dtype).reshape(v_ref.shape)


def project(rows, wk, wv, bias):
    slots = rows.shape[0]
    step = max(n for n in range(1, 21) if slots % n == 0)
    by_row = pl.BlockSpec((step,) + rows.shape[1:], lambda i: (i, 0, 0))
    whole = pl.BlockSpec(wk.shape, lambda i: (0, 0))
    return pl.pallas_call(
        project_kernel,
        grid=(slots // step,),
        out_shape=[jax.ShapeDtypeStruct(rows.shape, jnp.bfloat16)] * 2,
        in_specs=[by_row, whole, whole, pl.BlockSpec(bias.shape, lambda i: (0, 0))],
        out_specs=[by_row, by_row],
        compiler_params=pltpu.CompilerParams(vmem_limit_bytes=40 * MIB),
        cost_estimate=lasting(13),
        name="project",
    )(rows, wk, wv, bias)


def layer_norm(hidden, gain, shift):
    center = hidden - jnp.mean(hidden, axis=-1, keepdims=True)
    inverse = lax.rsqrt(jnp.mean(center * center, axis=-1, keepdims=True) + EPSILON)
    normal = center * inverse
    return (normal * gain + shift, normal, inverse)


def norm_back(upstream, normal, inverse, gain):
    scaled = upstream * gain
    return inverse * (
        scaled
        - jnp.mean(scaled, axis=-1, keepdims=True)
        - normal * jnp.mean(scaled * normal, axis=-1, keepdims=True)
    )


def erf_f32(x):
    return lax.erf(x)


def mid_kernel(
    chunk,
    mixed_ref,
    rows_ref,
    cot_ref,
    vec_ref,
    inner_bias_ref,
    wo_ref,
    w1_ref,
    w2_ref,
    final_ref,
    stream_grad_ref,
    mixed_grad_ref,
    normed_ref,
    act_ref,
    outer_grad_ref,
    inner_grad_ref,
    att_grad_ref,
    sums_ref,
    inner_sums_ref,
    slope,
):
    @pl.when(pl.program_id(0) == 0)
    def _():
        sums_ref[...] = jnp.zeros_like(sums_ref)
        inner_sums_ref[...] = jnp.zeros_like(inner_sums_ref)

    def vector(i):
        return vec_ref[i : i + 1]

    def tally(i, value):
        sums_ref[i : i + 1] += jnp.sum(value, axis=0, keepdims=True)

    hidden = w1_ref.shape[1]
    pieces = [slice(at, at + chunk) for at in range(0, hidden, chunk)]
    attention = nn(mixed_ref[...], wo_ref[...]) + vector(2)
    stream = rows_ref[...].astype(jnp.float32) + attention
    tally(6, stream * stream)
    tally(7, attention * attention)
    first_gain = vector(3)
    normed, first_normal, first_inverse = layer_norm(stream, first_gain, vector(4))
    normed_bf = normed.astype(jnp.bfloat16)
    normed_ref[...] = normed_bf
    outer = jnp.zeros_like(normed)
    for piece in pieces:
        inner = nn(normed_bf, w1_ref[:, piece]) + inner_bias_ref[:, piece]
        cumulative = 0.5 * (1.0 + erf_f32(inner * (1.0 / math.sqrt(2.0))))
        density = jnp.exp(-0.5 * inner * inner) * (1.0 / math.sqrt(2.0 * math.pi))
        slope[:, piece] = cumulative + inner * density
        active = (inner * cumulative).astype(jnp.bfloat16)
        act_ref[:, piece] = active
        outer = outer + nn(active, w2_ref[piece])
    second_gain = vector(6)
    final, second_normal, second_inverse = layer_norm(
        normed + (outer + vector(5)), second_gain, vector(7)
    )
    final_ref[...] = final.astype(final_ref.dtype)
    upstream = cot_ref[...].astype(jnp.float32)
    tally(4, upstream * second_normal)
    tally(5, upstream)
    second_grad = norm_back(upstream, second_normal, second_inverse, second_gain)
    outer_grad = second_grad.astype(jnp.bfloat16)
    outer_grad_ref[...] = outer_grad
    tally(3, outer_grad.astype(jnp.float32))
    normed_grad = second_grad
    for piece in pieces:
        inner_grad = (nt(outer_grad, w2_ref[piece]) * slope[:, piece]).astype(jnp.bfloat16)
        inner_grad_ref[:, piece] = inner_grad
        inner_sums_ref[:, piece] += jnp.sum(
            inner_grad.astype(jnp.float32), axis=0, keepdims=True
        )
        normed_grad = normed_grad + nt(inner_grad, w1_ref[:, piece])
    tally(1, normed_grad * first_normal)
    tally(2, normed_grad)
    stream_grad = norm_back(normed_grad, first_normal, first_inverse, first_gain)
    stream_grad_ref[...] = stream_grad
    att_grad = stream_grad.astype(jnp.bfloat16)
    att_grad_ref[...] = att_grad
    tally(0, att_grad.astype(jnp.float32))
    mixed_grad = nt(att_grad, wo_ref[...]).astype(jnp.bfloat16)
    mixed_grad_ref[...] = mixed_grad


def middle(mixed, rows, cotangent, vectors, inner_bias, wo, w1, w2):
    length, features = rows.shape
    hidden = w1.shape[1]
    block = min(MID_ROWS, length)
    by_row = pl.BlockSpec((block, features), lambda i: (i, 0))
    wide = pl.BlockSpec((block, hidden), lambda i: (i, 0))

    def whole(array):
        return pl.BlockSpec(array.shape, lambda i: (0, 0), pipeline_mode=pl.Buffered(1))

    narrow_bf = jax.ShapeDtypeStruct((length, features), jnp.bfloat16)
    wide_bf = jax.ShapeDtypeStruct((length, hidden), jnp.bfloat16)
    return pl.pallas_call(
        functools.partial(mid_kernel, MID_CHUNK),
        grid=(length // block,),
        out_shape=[
            narrow_bf,
            jax.ShapeDtypeStruct((length, features), jnp.float32),
            narrow_bf,
            narrow_bf,
            wide_bf,
            narrow_bf,
            wide_bf,
            narrow_bf,
            jax.ShapeDtypeStruct((8, features), jnp.float32),
            jax.ShapeDtypeStruct((1, hidden), jnp.float32),
        ],
        in_specs=[
            by_row,
            by_row,
            by_row,
            whole(vectors),
            whole(inner_bias),
            whole(wo),
            whole(w1),
            whole(w2),
        ],
        out_specs=[
            by_row,
            by_row,
            by_row,
            by_row,
            wide,
            by_row,
            wide,
            by_row,
            pl.BlockSpec((8, features), lambda i: (0, 0)),
            pl.BlockSpec((1, hidden), lambda i: (0, 0)),
        ],
        scratch_shapes=[pltpu.VMEM((block, hidden), jnp.float32)],
        compiler_params=pltpu.CompilerParams(vmem_limit_bytes=56 * MIB),
        cost_estimate=lasting(50),
        name="middle",
    )(mixed, rows, cotangent, vectors, inner_bias, wo, w1, w2)


def outer_product(left, right):
    return jnp.einsum("ta,tb->ab", left, right, preferred_element_type=jnp.float32)


def back_product(upstream, weight):
    return jnp.einsum("tb,ab->ta", upstream, weight, preferred_element_type=jnp.float32)


def column_sum(upstream):
    return jnp.sum(upstream.astype(jnp.float32), axis=0)


def shards(
    tokens,
    cotangent,
    random_blocks,
    query_weight,
    query_bias,
    key_weight,
    value_weight,
    value_bias,
    output_weight,
    output_bias,
    first_gain,
    first_shift,
    inner_weight,
    inner_bias,
    outer_weight,
    outer_bias,
    second_gain,
    second_shift,
):
    token_rows = tokens[0]
    length, features = token_rows.shape
    blocks_here = length // BLK
    count = lax.axis_size("ctx")
    groups = lax.axis_size("wsh")
    own_index = lax.axis_index("ctx")
    capacity = (3 * blocks_here + count - 3) // (count - 2)
    part = features // groups
    inner_parts = inner_bias.shape[0] // part

    small = jnp.concatenate(
        (
            query_bias,
            value_bias,
            output_bias,
            first_gain,
            first_shift,
            outer_bias,
            second_gain,
            second_shift,
            inner_bias,
        )
    )
    small = jnp.pad(small, (0, (-small.shape[0]) % 2048)).reshape(-1, 128)

    source, within, ranking = request_tables(random_blocks[0], count, blocks_here)
    filled, picked = send_slots(source, within, ranking, own_index, capacity)
    filled, picked = filled.reshape(-1), picked.reshape(-1)
    own_source = lax.dynamic_index_in_dim(source, own_index, 0, keepdims=False)
    own_rank = lax.dynamic_index_in_dim(ranking, own_index, 0, keepdims=False)
    index = key_slots(own_source, own_rank, blocks_here, capacity).reshape(-1)
    edge = jnp.stack([own_index == 0, own_index == count - 1]).astype(jnp.int32)

    row_blocks = token_rows.reshape(blocks_here, BLK, features)
    pack = pack_blocks(row_blocks, picked).reshape(count, capacity, BLK, features)
    ext_rows, fulls = spread(
        pack,
        row_blocks,
        (
            query_weight,
            key_weight,
            value_weight,
            output_weight,
            inner_weight,
            outer_weight,
            small,
        ),
        count,
        capacity,
    )
    full_query, full_key, full_value, full_output, full_inner, full_outer = (
        full.reshape(-1, full.shape[-1]) for full in fulls[:6]
    )
    gathered = fulls[6].reshape(groups, -1).astype(jnp.float32)
    vectors = gathered[:, : 8 * part].reshape(groups, 8, part)
    vectors = jnp.transpose(vectors, (1, 0, 2)).reshape(8, features)
    full_inner_bias = gathered[:, 8 * part : (8 + inner_parts) * part].reshape(1, -1)

    slots = ext_rows.shape[0]
    ext_flat = ext_rows.reshape(slots * BLK, features)
    queries_bf = (
        jnp.dot(token_rows, full_query, preferred_element_type=jnp.float32) + vectors[0]
    ).astype(jnp.bfloat16)
    query_blocks = queries_bf.reshape(blocks_here, BLK, features)
    key_blocks, value_blocks = project(ext_rows, full_key, full_value, vectors[1:2])
    mixed_blocks, log_total = attend(query_blocks, key_blocks, value_blocks, index, edge)
    mixed_bf = mixed_blocks.reshape(length, features)

    (
        final,
        stream_grad,
        mixed_grad_bf,
        normed_bf,
        activated_bf,
        outer_grad_bf,
        inner_grad_bf,
        attention_grad_bf,
        middle_sums,
        inner_bias_grad,
    ) = middle(
        mixed_bf,
        token_rows,
        cotangent[0],
        vectors,
        full_inner_bias,
        full_output,
        full_inner,
        full_outer,
    )
    output_weight_grad = outer_product(mixed_bf, attention_grad_bf)
    inner_weight_grad = outer_product(normed_bf, inner_grad_bf)
    outer_weight_grad = outer_product(activated_bf, outer_grad_bf)
    square_sums = jnp.sum(middle_sums[6:8], axis=1)

    fused = count == 8 and 3 * blocks_here == capacity * (count - 2)

    def small_parts(query_row, value_row):
        rows = jnp.concatenate([query_row, value_row, middle_sums[:6]], axis=0)
        parts = jnp.concatenate(
            [
                jnp.transpose(rows.reshape(8, groups, part), (1, 0, 2)),
                inner_bias_grad.reshape(groups, inner_parts, part),
                jnp.broadcast_to(
                    jnp.pad(square_sums, (0, part - 2)).reshape(1, 1, part), (groups, 1, part)
                ),
            ],
            axis=1,
        )
        return jnp.pad(parts, ((0, 0), (0, (-parts.shape[1]) % 8), (0, (-part) % 128)))

    mixed_grad_blocks = mixed_grad_bf.reshape(blocks_here, BLK, features)
    dq_blocks, dk_blocks, dv_blocks = attend_back(
        query_blocks, mixed_grad_blocks, key_blocks, value_blocks, log_total, index, edge
    )
    if fused:
        empty = jnp.zeros((1, features), jnp.float32)
        back, rim, glob, small_sums, near_grad, unit_sums = backward_tail(
            dq_blocks,
            dk_blocks,
            dv_blocks,
            ext_rows,
            stream_grad,
            outer_weight_grad.astype(jnp.bfloat16).reshape(groups, -1, features),
            inner_weight_grad.astype(jnp.bfloat16).reshape(groups, part, -1),
            output_weight_grad.astype(jnp.bfloat16).reshape(groups, part, features),
            full_query,
            full_key,
            full_value,
            small_parts(empty, empty),
            count,
            capacity,
        )
        stacked = full_outer.shape[0] // features
        across = full_inner.shape[1] // features
        units = unit_sums.reshape(-1, part, features).astype(jnp.float32)
        sums = [units[stacked + across + i] for i in (1, 2, 3, 0)] + [
            jnp.concatenate([units[stacked + i] for i in range(across)], axis=1),
            units[:stacked].reshape(-1, features),
        ]
    else:
        dq = dq_blocks.reshape(length, features)
        dk = dk_blocks.reshape(slots * BLK, features)
        dv = dv_blocks.reshape(slots * BLK, features)
        far_grad = (
            (back_product(dk[length:], full_key) + back_product(dv[length:], full_value))
            .astype(jnp.bfloat16)
            .reshape(slots - blocks_here, BLK, features)
        )
        back, rim, glob, small_sums = return_grads(
            far_grad, small_parts(column_sum(dq)[None], column_sum(dv)[None]), count, capacity
        )
        near_grad = (
            stream_grad
            + back_product(dq, full_query)
            + back_product(dk[:length], full_key)
            + back_product(dv[:length], full_value)
        )
        sums = lax.psum(
            tuple(
                lax.psum_scatter(
                    grad.astype(jnp.bfloat16), "wsh", scatter_dimension=0, tiled=True
                )
                for grad in (
                    outer_product(token_rows, dq),
                    outer_product(ext_flat, dk),
                    outer_product(ext_flat, dv),
                    output_weight_grad,
                    inner_weight_grad,
                    outer_weight_grad,
                )
            ),
            "ctx",
        )
        sums = [total.astype(jnp.float32) for total in sums]
    tokens_grad = unpack_grads(
        near_grad.reshape(blocks_here, BLK, features), back, rim, glob, picked, filled, edge
    )
    element_count = count * groups * length * features
    stream_rms = jnp.sqrt(small_sums[8 + inner_parts, :2] / element_count)
    (
        query_bias_grad,
        value_bias_grad,
        output_bias_grad,
        first_gain_grad,
        first_shift_grad,
        outer_bias_grad,
        second_gain_grad,
        second_shift_grad,
    ) = (small_sums[i, :part] for i in range(8))
    inner_bias_grad = small_sums[8 : 8 + inner_parts, :part].reshape(-1)
    query_weight_sum, key_weight_sum, value_weight_sum, output_weight_sum = sums[:4]
    return (
        final[None],
        tokens_grad.reshape(1, length, features),
        query_weight_sum,
        query_bias_grad,
        key_weight_sum,
        value_weight_sum,
        value_bias_grad,
        output_weight_sum,
        output_bias_grad,
        first_gain_grad,
        first_shift_grad,
        sums[4],
        inner_bias_grad,
        sums[5],
        outer_bias_grad,
        second_gain_grad,
        second_shift_grad,
        stream_rms,
    )


def solution(mesh):
    in_specs = (
        P("wsh", "ctx", None),
        P("wsh", "ctx", None),
        P("wsh", None, None),
        P("wsh", None),
        P("wsh"),
        P("wsh", None),
        P("wsh", None),
        P("wsh"),
        P("wsh", None),
        P("wsh"),
        P("wsh"),
        P("wsh"),
        P("wsh", None),
        P("wsh"),
        P("wsh", None),
        P("wsh"),
        P("wsh"),
        P("wsh"),
    )
    out_specs = (
        P("wsh", "ctx", None),
        P("wsh", "ctx", None),
        P("wsh", None),
        P("wsh"),
        P("wsh", None),
        P("wsh", None),
        P("wsh"),
        P("wsh", None),
        P("wsh"),
        P("wsh"),
        P("wsh"),
        P("wsh", None),
        P("wsh"),
        P("wsh", None),
        P("wsh"),
        P("wsh"),
        P("wsh"),
        P(),
    )
    return jax.shard_map(shards, mesh=mesh, in_specs=in_specs, out_specs=out_specs, check_vma=False)
```

```python
import functools
import math

import jax
import jax.numpy as jnp
from jax import lax
from jax.experimental import pallas as pl
from jax.experimental.pallas import tpu as pltpu
from jax.sharding import PartitionSpec as P

HD = 64
BLK = 64
PACKED = 4
LANES = PACKED * HD
LISTED = 8
EXTRA = 4

EPSILON = 1e-06
NEG_FILL = -1e30
MESH = pl.DeviceIdType.MESH
MIB = 1 << 20
MID_ROWS = 256
MID_CHUNK = 768
GAP = 0
EARLY = 4
PACE = (2,) * 12


def lasting(microseconds):
    return pl.CostEstimate(
        flops=int(microseconds * 1e9), bytes_accessed=int(microseconds * 1e6), transcendentals=0
    )


def request_tables(random_rows, cycle_size, blocks_here):
    wanted = random_rows.reshape(cycle_size, 3 * blocks_here)
    source = wanted // blocks_here
    within = wanted % blocks_here
    positions = jnp.arange(wanted.shape[1])
    earlier = positions[None, :] < positions[:, None]
    same_source = source[:, :, None] == source[:, None, :]
    ranking = jnp.sum(same_source & earlier[None], axis=2, dtype=jnp.int32)
    return (source, within, ranking)


def send_slots(source, within, ranking, own_index, capacity):
    slot_ids = jnp.arange(capacity, dtype=jnp.int32)
    selected = (source[:, None, :] == own_index) & (ranking[:, None, :] == slot_ids[None, :, None])
    filled = jnp.any(selected, axis=2)
    picked = jnp.sum(jnp.where(selected, within[:, None, :], 0), axis=2, dtype=jnp.int32)
    return (filled.astype(jnp.int32), picked)


def key_slots(own_source, own_rank, blocks_here, capacity):
    block = jnp.arange(blocks_here, dtype=jnp.int32)
    left = jnp.where(block == 0, blocks_here, block - 1)
    right = jnp.where(block == blocks_here - 1, blocks_here + 1, block + 1)
    drawn = (blocks_here + EXTRA + (own_source - 1) * capacity + own_rank).reshape(blocks_here, 3)
    fixed = jnp.stack(
        [
            left,
            block,
            right,
            jnp.full_like(block, blocks_here + 2),
            jnp.full_like(block, blocks_here + 3),
        ],
        axis=1,
    )
    return jnp.concatenate([fixed, drawn], axis=1).astype(jnp.int32)


def pack_kernel(picked_ref, rows_ref, out_ref, sems):
    slots = out_ref.shape[0]

    def copy(i):
        return pltpu.make_async_copy(rows_ref.at[picked_ref[i]], out_ref.at[i], sems.at[i])

    @pl.loop(0, slots)
    def _(i):
        copy(i).start()

    @pl.loop(0, slots)
    def _(i):
        copy(i).wait()


def pack_blocks(rows, picked):
    slots = picked.shape[0]
    return pl.pallas_call(
        pack_kernel,
        out_shape=jax.ShapeDtypeStruct((slots,) + rows.shape[1:], rows.dtype),
        grid_spec=pltpu.PrefetchScalarGridSpec(
            num_scalar_prefetch=1,
            grid=(1,),
            in_specs=[pl.BlockSpec(rows.shape, lambda i, t: (0, 0, 0))],
            out_specs=pl.BlockSpec(memory_space=pl.ANY),
            scratch_shapes=[pltpu.SemaphoreType.DMA((slots,))],
        ),
        name="pack_blocks",
    )(picked, rows)


def greet(count, groups):
    barrier = pltpu.get_barrier_semaphore()
    me = lax.axis_index("ctx")
    w = lax.axis_index("wsh")

    @pl.loop(1, count)
    def _(delta):
        pl.semaphore_signal(
            barrier, inc=1, device_id={"ctx": (me + delta) % count}, device_id_type=MESH
        )

    for delta in range(1, groups):
        pl.semaphore_signal(
            barrier, inc=1, device_id={"wsh": (w + delta) % groups}, device_id_type=MESH
        )
    pl.semaphore_wait(barrier, count + groups - 2)


def relays(count):
    return ((3, 2, (4, 6)), (4, 5, (3, 1))) if count == 8 else ()


def spread_kernel(count, capacity, *refs):
    weights = (len(refs) - 2 - 2 - 14) // 3
    pack, rows = refs[:2]
    shards = refs[2 : 2 + weights]
    ext, passing = refs[2 + weights : 4 + weights]
    fulls = refs[4 + weights : 4 + 2 * weights]
    rest = refs[4 + 2 * weights :]
    held = rest[:weights]
    rand_s, rand_r, halo_s, halo_r, glob_s, glob_r, wgt_s, wgt_r = rest[weights : weights + 8]
    pass_s, pass_r, loc_in, loc_out, own_pack, own_row = rest[weights + 8 :]
    blocks = rows.shape[0]
    base = blocks + EXTRA
    me = lax.axis_index("ctx")
    w = lax.axis_index("wsh")
    sib = w + 1 - 2 * (w % 2)
    far = (w + 2) % 4
    last = count - 1
    is_source = jnp.logical_and(me >= 1, me <= last - 1)
    routes = relays(count)
    greet(count, 4)

    def relayed(dst):
        found = me < 0
        for source, _, targets in routes:
            for target in targets:
                found = jnp.logical_or(found, jnp.logical_and(me == source, dst == target))
        return found

    def weight_copy(i, step):
        if step == 2:
            src, dst, target = fulls[i].at[far], fulls[i].at[far], sib
        else:
            src, dst, target = shards[i], fulls[i].at[w], (far, sib)[step]
        return pltpu.make_async_remote_copy(
            src_ref=src,
            dst_ref=dst,
            send_sem=wgt_s.at[i, step],
            recv_sem=wgt_r.at[i, step],
            device_id={"wsh": target},
            device_id_type=MESH,
        )

    def random_copy(dst, k):
        return pltpu.make_async_remote_copy(
            src_ref=pack.at[dst, k],
            dst_ref=ext.at[base + (me - 1) * capacity + k],
            send_sem=rand_s.at[dst, k],
            recv_sem=rand_r.at[me, k],
            device_id={"ctx": dst},
            device_id_type=MESH,
        )

    def random_landed(source, k):
        return pltpu.make_async_remote_copy(
            src_ref=pack.at[source, k],
            dst_ref=ext.at[base + (source - 1) * capacity + k],
            send_sem=rand_s.at[source, k],
            recv_sem=rand_r.at[source, k],
            device_id={"ctx": source},
            device_id_type=MESH,
        )

    def to_relay(via, r, dst, k):
        return pltpu.make_async_remote_copy(
            src_ref=pack.at[dst, k],
            dst_ref=passing.at[r, k],
            send_sem=rand_s.at[dst, k],
            recv_sem=pass_r.at[r, k],
            device_id={"ctx": via},
            device_id_type=MESH,
        )

    def from_relay(source, r, dst, k):
        return pltpu.make_async_remote_copy(
            src_ref=passing.at[r, k],
            dst_ref=ext.at[base + (source - 1) * capacity + k],
            send_sem=pass_s.at[r, k],
            recv_sem=rand_r.at[source, k],
            device_id={"ctx": dst},
            device_id_type=MESH,
        )

    def halo_copy(side):
        return pltpu.make_async_remote_copy(
            src_ref=rows.at[blocks - 1 if side == 0 else 0],
            dst_ref=ext.at[blocks + side],
            send_sem=halo_s.at[side],
            recv_sem=halo_r.at[side],
            device_id={"ctx": me + 1 if side == 0 else me - 1},
            device_id_type=MESH,
        )

    def global_copy(which, dst):
        return pltpu.make_async_remote_copy(
            src_ref=rows.at[0 if which == 0 else blocks - 1],
            dst_ref=ext.at[blocks + 2 + which],
            send_sem=glob_s.at[dst],
            recv_sem=glob_r.at[which],
            device_id={"ctx": dst},
            device_id_type=MESH,
        )

    def held_in(i):
        return pltpu.make_async_copy(shards[i], held[i], loc_in.at[2 + i])

    def held_out(i):
        return pltpu.make_async_copy(held[i], fulls[i].at[w], loc_out.at[2 + i])

    def rows_in():
        return pltpu.make_async_copy(rows, own_row, loc_in.at[0])

    def rows_out():
        return pltpu.make_async_copy(own_row, ext.at[pl.ds(0, blocks)], loc_out.at[0])

    def pack_in():
        return pltpu.make_async_copy(pack.at[me], own_pack, loc_in.at[1])

    def pack_out():
        return pltpu.make_async_copy(
            own_pack, ext.at[pl.ds(base + (me - 1) * capacity, capacity)], loc_out.at[1]
        )

    def rim_out(side):
        return pltpu.make_async_copy(own_row.at[0], ext.at[blocks + side], loc_out.at[2 + weights])

    def global_out(which):
        return pltpu.make_async_copy(
            own_row.at[0 if which == 0 else blocks - 1],
            ext.at[blocks + 2 + which],
            loc_out.at[3 + weights],
        )

    for i in range(weights):
        weight_copy(i, 0).start()
        weight_copy(i, 1).start()

    @pl.when(me < last)
    def _():
        halo_copy(0).start()

    @pl.when(me > 0)
    def _():
        halo_copy(1).start()

    for which, owner in ((0, 0), (1, last)):

        @pl.when(me == owner)
        def _():
            @pl.loop(1, count)
            def _(delta):
                global_copy(which, (me + delta) % count).start()

    for k in range(capacity):
        for source, via, targets in routes:

            @pl.when(me == source)
            def _():
                for r, target in enumerate(targets):
                    to_relay(via, r, target, k).start()

        @pl.when(is_source)
        def _():
            @pl.loop(1, count)
            def _(delta):
                dst = (me + delta) % count

                @pl.when(jnp.logical_not(relayed(dst)))
                def _():
                    random_copy(dst, k).start()

    rows_in().start()
    for i in range(weights):
        held_in(i).start()

    @pl.when(is_source)
    def _():
        pack_in().start()
        pack_in().wait()
        pack_out().start()

    rows_in().wait()
    rows_out().start()
    for which, owner in ((0, 0), (1, last)):

        @pl.when(me == owner)
        def _():
            rim_out(which).start()
            global_out(which).start()

    for i in range(weights):
        held_in(i).wait()
        held_out(i).start()

    for step in range(max(capacity, weights)):
        if step < capacity:
            for source, via, targets in routes:

                @pl.when(me == via)
                def _():
                    for r, target in enumerate(targets):
                        to_relay(via, r, target, step).wait_recv()
                        from_relay(source, r, target, step).start()

        if step < weights:
            weight_copy(step, 0).wait_recv()
            weight_copy(step, 2).start()

    rows_out().wait()
    for i in range(weights):
        held_out(i).wait()

    @pl.when(is_source)
    def _():
        pack_out().wait()

        for k in range(capacity):

            @pl.loop(1, count)
            def _(delta):
                random_copy((me + delta) % count, k).wait_send()

    for source, via, targets in routes:

        @pl.when(me == via)
        def _():
            for r, target in enumerate(targets):
                for k in range(capacity):
                    from_relay(source, r, target, k).wait_send()

    for which, owner in ((0, 0), (1, last)):

        @pl.when(me == owner)
        def _():
            rim_out(which).wait()
            global_out(which).wait()

            @pl.loop(1, count)
            def _(delta):
                global_copy(which, (me + delta) % count).wait_send()

        @pl.when(me != owner)
        def _():
            global_copy(which, owner).wait_recv()

    @pl.when(me < last)
    def _():
        halo_copy(0).wait_send()
        halo_copy(1).wait_recv()

    @pl.when(me > 0)
    def _():
        halo_copy(1).wait_send()
        halo_copy(0).wait_recv()

    for k in range(capacity):

        @pl.loop(1, last)
        def _(source):
            @pl.when(source != me)
            def _():
                random_landed(source, k).wait_recv()

    for i in range(weights):
        for step in range(3):
            weight_copy(i, step).wait_send()
        weight_copy(i, 1).wait_recv()
        weight_copy(i, 2).wait_recv()


def spread(pack, rows, shards, count, capacity):
    blocks = rows.shape[0]
    tail = rows.shape[1:]
    weights = len(shards)
    slots = blocks + EXTRA + (count - 2) * capacity
    outs = pl.pallas_call(
        functools.partial(spread_kernel, count, capacity),
        out_shape=[
            jax.ShapeDtypeStruct((slots,) + tail, rows.dtype),
            jax.ShapeDtypeStruct((2, capacity) + tail, rows.dtype),
        ]
        + [jax.ShapeDtypeStruct((4,) + shard.shape, shard.dtype) for shard in shards],
        in_specs=[pl.BlockSpec(memory_space=pl.ANY)] * (2 + weights),
        out_specs=[pl.BlockSpec(memory_space=pl.ANY)] * (2 + weights),
        scratch_shapes=[pltpu.VMEM(shard.shape, shard.dtype) for shard in shards]
        + [
            pltpu.SemaphoreType.DMA((count, capacity)),
            pltpu.SemaphoreType.DMA((count, capacity)),
            pltpu.SemaphoreType.DMA((2,)),
            pltpu.SemaphoreType.DMA((2,)),
            pltpu.SemaphoreType.DMA((count,)),
            pltpu.SemaphoreType.DMA((2,)),
            pltpu.SemaphoreType.DMA((weights, 3)),
            pltpu.SemaphoreType.DMA((weights, 3)),
            pltpu.SemaphoreType.DMA((2, capacity)),
            pltpu.SemaphoreType.DMA((2, capacity)),
            pltpu.SemaphoreType.DMA((4 + weights,)),
            pltpu.SemaphoreType.DMA((4 + weights,)),
            pltpu.VMEM((capacity,) + tail, rows.dtype),
            pltpu.VMEM(rows.shape, rows.dtype),
        ],
        compiler_params=pltpu.CompilerParams(
            collective_id=0, has_side_effects=True, vmem_limit_bytes=56 * MIB
        ),
        cost_estimate=lasting(110),
        name="spread_rows",
    )(pack, rows, *shards)
    return outs[0], outs[2:]


class Reducer:
    def __init__(self, count, unit, staged, out, scratch):
        self.unit = unit
        self.staged = staged
        self.out = out
        (
            self.ring,
            self.from_sib,
            self.from_far,
            self.from_pair,
            self.chain_in,
            self.load_sem,
            self.sib_s,
            self.sib_r,
            self.far_s,
            self.far_r,
            self.pair_s,
            self.pair_r,
            self.chain_s,
            self.chain_r,
            self.wide_s,
            self.wide_r,
            self.back_s,
            self.back_r,
        ) = scratch
        self.units = out.shape[0]
        self.top = count // 2 - 1
        me = lax.axis_index("ctx")
        w = lax.axis_index("wsh")
        self.w = w
        self.me = me
        self.sib = w + 1 - 2 * (w % 2)
        self.far = (w + 2) % 4
        self.sib_far = (self.sib + 2) % 4
        self.side = me % 2
        self.level = me // 2
        self.pair = me + 1 - 2 * self.side

    def load(self, u, slot):
        return pltpu.make_async_copy(
            self.unit(u, (self.w, self.far)[slot]),
            self.ring.at[u % 2, slot],
            self.load_sem.at[u, slot],
        )

    def remote(self, src, dst, send, recv, **device):
        return pltpu.make_async_remote_copy(
            src_ref=src,
            dst_ref=dst,
            send_sem=send,
            recv_sem=recv,
            device_id=device,
            device_id_type=MESH,
        )

    def to_sib(self, u, slot):
        return self.remote(
            self.unit(u, (self.sib, self.sib_far)[slot]),
            self.from_sib.at[u, slot],
            self.sib_s.at[u, slot],
            self.sib_r.at[u, slot],
            wsh=self.sib,
        )

    def to_far(self, u):
        return self.remote(
            self.from_sib.at[u, 1],
            self.from_far.at[u],
            self.far_s.at[u],
            self.far_r.at[u],
            wsh=self.far,
        )

    def half(self, u, side):
        rows = self.out.shape[2]
        return self.from_sib.at[u, 0, pl.ds(pl.multiple_of(side * rows, rows), rows)]

    def to_pair(self, u):
        return self.remote(
            self.half(u, 1 - self.side),
            self.from_pair.at[u],
            self.pair_s.at[u],
            self.pair_r.at[u],
            ctx=self.pair,
        )

    def toward(self, u):
        return 2 if u % 2 == 0 else -2

    def place(self, u, hop):
        return hop if u % 2 == 0 else self.top - hop

    def along(self, u):
        return self.remote(
            self.from_pair.at[u],
            self.chain_in.at[u],
            self.chain_s.at[u],
            self.chain_r.at[u],
            ctx=self.me + self.toward(u),
        )

    def widen(self, u):
        place = self.out.at[u, self.side]
        return self.remote(
            place, place, self.wide_s.at[u], self.wide_r.at[u], ctx=self.me - self.toward(u)
        )

    def give_back(self, u, side):
        place = self.out.at[u, side]
        return self.remote(place, place, self.back_s.at[u], self.back_r.at[u], ctx=self.pair)


    def begin(self, u):
        for slot in (1, 0):
            self.to_sib(u, slot).start()
            if u < min(2, self.staged):
                self.load(u, slot).start()

    def join_sib(self, u):
        for slot in (1, 0):
            if u < self.staged:
                self.load(u, slot).wait()
                own = self.ring[u % 2, slot]
            else:
                own = self.unit(u, (self.w, self.far)[slot])[...]
            self.to_sib(u, slot).wait_recv()
            self.from_sib[u, slot] = add_bf16(own, self.from_sib[u, slot])
            if slot == 1:
                self.to_far(u).start()
            if u + 2 < self.staged:
                self.load(u + 2, slot).start()

    def join_far(self, u):
        self.to_far(u).wait_recv()
        self.from_sib[u, 0] = add_bf16(self.from_sib[u, 0], self.from_far[u])
        self.to_pair(u).start()

    def join_pair(self, u):
        self.to_pair(u).wait_recv()
        self.from_pair[u] = add_bf16(self.half(u, self.side)[...], self.from_pair[u])

    def gather(self, u, hop):
        @pl.when(self.level == self.place(u, hop))
        def _():
            if hop > 0:
                self.along(u).wait_recv()
                total = add_bf16(self.from_pair[u], self.chain_in[u])
                if hop < self.top:
                    self.from_pair[u] = total
                else:
                    self.out[u, self.side] = total
            if hop < self.top:
                self.along(u).start()
            else:
                self.widen(u).start()
                self.give_back(u, self.side).start()

    def spread_out(self, u, hop):
        @pl.when(self.level == self.place(u, hop))
        def _():
            self.widen(u).wait_recv()
            if hop > 0:
                self.widen(u).start()
            self.give_back(u, self.side).start()

    def step(self, t):
        def unit(lag):
            u = t - lag
            if u >= self.staged:
                u = u - GAP if u >= self.staged + GAP else -1
            return u if 0 <= u < self.units else None

        if unit(0) is not None:
            self.join_far(unit(0))
        if unit(1) is not None:
            self.join_pair(unit(1))
        lag = 1
        for hop in range(self.top + 1):
            if unit(lag) is not None:
                self.gather(unit(lag), hop)
            lag += 1
        for hop in range(self.top - 1, -1, -1):
            if unit(lag) is not None:
                self.spread_out(unit(lag), hop)
            lag += 1

    def steps(self):
        return self.units + GAP + 2 * self.top + 1

    def finish(self):
        for u in range(self.units):
            self.give_back(u, 1 - self.side).wait_recv()
            self.give_back(u, self.side).wait_send()

            @pl.when(self.level != self.place(u, self.top))
            def _():
                self.along(u).wait_send()

            @pl.when(self.level != self.place(u, 0))
            def _():
                self.widen(u).wait_send()

            for slot in range(2):
                self.to_sib(u, slot).wait_send()
            self.to_far(u).wait_send()
            self.to_pair(u).wait_send()


def add_bf16(left, right):
    return (left.astype(jnp.float32) + right.astype(jnp.float32)).astype(jnp.bfloat16)


def reducer_shapes(units, part, features):
    dma = pltpu.SemaphoreType.DMA
    kind = jnp.bfloat16
    out = jax.ShapeDtypeStruct((units, 2, part // 2, features), kind)
    scratch = [
        pltpu.VMEM((2, 2, part, features), kind),
        pltpu.VMEM((units, 2, part, features), kind),
        pltpu.VMEM((units, part, features), kind),
        pltpu.VMEM((units, part // 2, features), kind),
        pltpu.VMEM((units, part // 2, features), kind),
        dma((units, 2)),
        dma((units, 2)),
        dma((units, 2)),
    ] + [dma((units,)) for _ in range(10)]
    return out, scratch


class Returner:
    def __init__(self, count, capacity, far_ref, rim_ref, outs, small, sems):
        self.count, self.capacity, self.small = count, capacity, small
        self.far_ref, self.rim_ref = far_ref, rim_ref
        self.back, self.rim, self.glob, self.small_out = outs
        (
            self.rand_s,
            self.rand_r,
            self.halo_s,
            self.halo_r,
            self.glob_s,
            self.glob_r,
            self.loc,
            self.group_part,
            self.ring_part,
            self.group_s,
            self.group_r,
            self.ring_s,
            self.ring_r,
        ) = sems
        self.me = lax.axis_index("ctx")
        self.w = lax.axis_index("wsh")
        self.last = count - 1
        self.groups = small.shape[0]
        self.is_source = jnp.logical_and(self.me >= 1, self.me <= self.last - 1)

    def remote(self, src, dst, send, recv, **device):
        return pltpu.make_async_remote_copy(
            src_ref=src,
            dst_ref=dst,
            send_sem=send,
            recv_sem=recv,
            device_id=device,
            device_id_type=MESH,
        )

    def random_copy(self, owner, k):
        return self.remote(
            self.far_ref.at[(owner - 1) * self.capacity + k],
            self.back.at[self.me, k],
            self.rand_s.at[owner, k],
            self.rand_r.at[self.me, k],
            ctx=owner,
        )

    def landed(self, sender, k):
        return self.remote(
            self.far_ref.at[k],
            self.back.at[sender, k],
            self.rand_s.at[sender, k],
            self.rand_r.at[sender, k],
            ctx=sender,
        )

    def own_random(self):
        return pltpu.make_async_copy(
            self.far_ref.at[pl.ds((self.me - 1) * self.capacity, self.capacity)],
            self.back.at[self.me],
            self.loc.at[0],
        )

    def halo_copy(self, side):
        return self.remote(
            self.rim_ref.at[side],
            self.rim.at[1 - side],
            self.halo_s.at[side],
            self.halo_r.at[side],
            ctx=self.me - 1 if side == 0 else self.me + 1,
        )

    def global_copy(self, which, sender):
        return self.remote(
            self.rim_ref.at[2 + which],
            self.glob.at[sender],
            self.glob_s.at[which],
            self.glob_r.at[sender],
            ctx=0 if which == 0 else self.last,
        )

    def own_global(self, which):
        return pltpu.make_async_copy(
            self.rim_ref.at[2 + which], self.glob.at[self.me], self.loc.at[1]
        )

    def group_copy(self, target, sender):
        return self.remote(
            self.small.at[target],
            self.group_part.at[sender],
            self.group_s.at[target],
            self.group_r.at[sender],
            wsh=target,
        )

    def ring_copy(self, target, sender):
        return self.remote(
            self.ring_part.at[self.me],
            self.ring_part.at[sender],
            self.ring_s.at[target],
            self.ring_r.at[sender],
            ctx=target,
        )

    def send_random(self, owner, slots):
        @pl.when(owner != self.me)
        def _():
            for k in slots:
                self.random_copy(owner, k).start()

    def send_round(self, k):
        @pl.loop(0, self.count - 2)
        def _(i):
            self.send_random(1 + (self.me + i) % (self.count - 2), (k,))

    def keep_own(self):
        @pl.when(self.is_source)
        def _():
            self.own_random().start()

    def send_rims(self):
        @pl.when(self.me > 0)
        def _():
            self.halo_copy(0).start()
            self.global_copy(0, self.me).start()

        @pl.when(self.me < self.last)
        def _():
            self.halo_copy(1).start()
            self.global_copy(1, self.me).start()

        for which, owner in ((0, 0), (1, self.last)):

            @pl.when(self.me == owner)
            def _():
                self.own_global(which).start()

    def send_small(self):
        for delta in range(1, self.groups):
            self.group_copy((self.w + delta) % self.groups, self.w).start()

    def pass_small(self):
        total = self.small[self.w]
        for delta in range(1, self.groups):
            sender = (self.w + delta) % self.groups
            self.group_copy(self.w, sender).wait_recv()
            total = total + self.group_part[sender]
        self.ring_part[self.me] = total

        @pl.loop(1, self.count)
        def _(delta):
            self.ring_copy((self.me + delta) % self.count, self.me).start()

    def end_small(self):
        @pl.loop(1, self.count)
        def _(delta):
            self.ring_copy(self.me, (self.me + delta) % self.count).wait_recv()

        self.small_out[...] = jnp.sum(self.ring_part[...], axis=0)

        @pl.loop(1, self.count)
        def _(delta):
            self.ring_copy((self.me + delta) % self.count, self.me).wait_send()

        for delta in range(1, self.groups):
            self.group_copy((self.w + delta) % self.groups, self.w).wait_send()

    def finish(self):
        @pl.when(self.is_source)
        def _():
            self.own_random().wait()

            @pl.loop(0, self.count)
            def _(sender):
                @pl.when(sender != self.me)
                def _():
                    for k in range(self.capacity):
                        self.landed(sender, k).wait_recv()

        for which, owner in ((0, 0), (1, self.last)):

            @pl.when(self.me == owner)
            def _():
                self.own_global(which).wait()

                @pl.loop(0, self.count)
                def _(sender):
                    @pl.when(sender != self.me)
                    def _():
                        self.global_copy(which, sender).wait_recv()

        @pl.when(self.me > 0)
        def _():
            self.halo_copy(0).wait_send()
            self.halo_copy(1).wait_recv()
            self.global_copy(0, self.me).wait_send()

        @pl.when(self.me < self.last)
        def _():
            self.halo_copy(1).wait_send()
            self.halo_copy(0).wait_recv()
            self.global_copy(1, self.me).wait_send()

        @pl.loop(1, self.last)
        def _(owner):
            @pl.when(owner != self.me)
            def _():
                for k in range(self.capacity):
                    self.random_copy(owner, k).wait_send()


def returner_shapes(count, capacity, tail, small):
    kind = jnp.bfloat16
    dma = pltpu.SemaphoreType.DMA
    groups = small.shape[0]
    outs = [
        jax.ShapeDtypeStruct((count, capacity) + tail, kind),
        jax.ShapeDtypeStruct((2,) + tail, kind),
        jax.ShapeDtypeStruct((count,) + tail, kind),
        jax.ShapeDtypeStruct(small.shape[1:], jnp.float32),
    ]
    sems = [
        dma((count, capacity)),
        dma((count, capacity)),
        dma((2,)),
        dma((2,)),
        dma((2,)),
        dma((count,)),
        dma((2,)),
        pltpu.VMEM(small.shape, jnp.float32),
        pltpu.VMEM((count,) + small.shape[1:], jnp.float32),
        dma((groups,)),
        dma((groups,)),
        dma((count,)),
        dma((count,)),
    ]
    return outs, sems


HBM_SPEC = pl.BlockSpec(memory_space=pl.ANY)
VMEM_SPEC = pl.BlockSpec(memory_space=pltpu.VMEM)
RETURN_SPECS = [HBM_SPEC, HBM_SPEC, HBM_SPEC, VMEM_SPEC]


def return_kernel(count, capacity, far_ref, rim_ref, small, *refs):
    mover = Returner(count, capacity, far_ref, rim_ref, refs[:4], small, refs[4:])
    greet(count, small.shape[0])
    mover.send_small()
    mover.send_rims()

    for k in range(capacity):
        mover.send_round(k)
    mover.keep_own()
    mover.pass_small()
    mover.end_small()
    mover.finish()


def return_grads(far_grad, small, count, capacity):
    tail = far_grad.shape[1:]
    outs, sems = returner_shapes(count, capacity, tail, small)
    return pl.pallas_call(
        functools.partial(return_kernel, count, capacity),
        out_shape=outs,
        in_specs=[VMEM_SPEC, VMEM_SPEC, VMEM_SPEC],
        out_specs=RETURN_SPECS,
        scratch_shapes=sems,
        compiler_params=pltpu.CompilerParams(
            collective_id=1, has_side_effects=True, vmem_limit_bytes=56 * MIB
        ),
        name="return_grads",
    )(far_grad[EXTRA:], far_grad[:EXTRA], small)


def tail_kernel(
    count,
    capacity,
    dq_hbm,
    dk_hbm,
    dv_hbm,
    x_hbm,
    stream_hbm,
    outer_hbm,
    inner_hbm,
    wo_hbm,
    wq_ref,
    wk_ref,
    wv_ref,
    small_in,
    *refs,
):
    outs, near_hbm, sums = refs[:4], refs[4], refs[5]
    (
        xbuf,
        kbuf,
        vbuf,
        qbuf,
        wq_sum,
        wk_sum,
        wv_sum,
        shares,
        sending,
        rims,
        stage,
        small,
        bias_sum,
        load_sem,
        q_sem,
        stage_sem,
    ) = refs[6:22]
    returner_sems, reducer_scratch = refs[22:35], refs[35:]
    blocks, _, features = dq_hbm.shape
    length = blocks * BLK
    near = blocks + EXTRA
    chunk = capacity * BLK
    part = features // 4
    me = lax.axis_index("ctx")
    sources = count - 2
    mover = Returner(count, capacity, sending, rims, outs, small, returner_sems)
    across = inner_hbm.shape[2] // features
    stacked = outer_hbm.shape[1] // part
    staged = stacked + across + 1

    def unit(u, quarter):
        if u < stacked:
            return outer_hbm.at[quarter, pl.ds(u * part, part)]
        if u < stacked + across:
            return inner_hbm.at[quarter, :, pl.ds((u - stacked) * features, features)]
        if u < staged:
            return wo_hbm.at[quarter]
        return shares.at[u - staged, quarter]

    reducer = Reducer(count, unit, staged, sums, reducer_scratch)

    def loads(at, slot, size):
        here, there = pl.ds(at, size), pl.ds(0, size)
        return [
            pltpu.make_async_copy(src.at[here], dst.at[slot, there], load_sem.at[slot, n])
            for n, (src, dst) in enumerate(((x_hbm, xbuf), (dk_hbm, kbuf), (dv_hbm, vbuf)))
        ]

    def far_loads(i, slot):
        return loads(near + ((me + i) % sources) * capacity, slot, capacity)

    def own_loads(n):
        half = blocks // 2
        return loads(n * half, n, half) + [
            pltpu.make_async_copy(dq_hbm.at[pl.ds(n * half, half)], qbuf.at[n], q_sem.at[n])
        ]

    def start(copies):
        for copy in copies:
            copy.start()

    def end(copies):
        for copy in copies:
            copy.wait()

    def gather_weights(rows, key_grad, value_grad):
        wk_sum[...] += tn(rows, key_grad)
        wv_sum[...] += tn(rows, value_grad)
        bias_sum[1:2] += jnp.sum(value_grad.astype(jnp.float32), axis=0, keepdims=True)

    start(far_loads(0, 0))
    greet(count, small.shape[0])
    for u in range(staged):
        reducer.begin(u)
    bias_sum[...] = jnp.zeros_like(bias_sum)
    wk_sum[...] = jnp.zeros_like(wk_sum)
    wv_sum[...] = jnp.zeros_like(wv_sum)

    for third in range(3):

        @pl.loop(third * sources // 3, (third + 1) * sources // 3)
        def _(i):
            slot = i % 2
            end(far_loads(i, slot))

            @pl.when(i + 1 < sources)
            def _():
                start(far_loads(i + 1, 1 - slot))

            key_grad = kbuf[slot].reshape(chunk, features)
            value_grad = vbuf[slot].reshape(chunk, features)
            row_grad = nt(key_grad, wk_ref[...]) + nt(value_grad, wv_ref[...])
            s = 1 + (me + i) % sources
            sending[pl.ds((s - 1) * capacity, capacity)] = row_grad.astype(sending.dtype).reshape(
                capacity, BLK, features
            )
            mover.send_random(s, range(EARLY))
            gather_weights(xbuf[slot].reshape(chunk, features), key_grad, value_grad)

        for u in range(third * staged // 3, (third + 1) * staged // 3):
            reducer.join_sib(u)
    mover.keep_own()

    rim_loads = loads(blocks, 0, EXTRA)
    start(rim_loads)
    end(rim_loads)
    rim_rows = EXTRA * BLK
    key_grad = kbuf[0, :EXTRA].reshape(rim_rows, features)
    value_grad = vbuf[0, :EXTRA].reshape(rim_rows, features)
    row_grad = nt(key_grad, wk_ref[...]) + nt(value_grad, wv_ref[...])
    rims[...] = row_grad.astype(rims.dtype).reshape(EXTRA, BLK, features)
    mover.send_rims()
    gather_weights(xbuf[0, :EXTRA].reshape(rim_rows, features), key_grad, value_grad)

    start(own_loads(0))
    start(own_loads(1))
    wq_sum[...] = jnp.zeros_like(wq_sum)
    half = length // 2

    def stage_load(n):
        return pltpu.make_async_copy(
            stream_hbm.at[pl.ds(n * half, half)], stage.at[n], stage_sem.at[0, n]
        )

    def stage_store(n):
        return pltpu.make_async_copy(
            stage.at[n], near_hbm.at[pl.ds(n * half, half)], stage_sem.at[1, n]
        )

    for n in range(2):
        stage_load(n).start()
        end(own_loads(n))

    @pl.loop(0, 2)
    def _(n):
        rows = xbuf[n].reshape(half, features)
        query_grad = qbuf[n].reshape(half, features)
        gather_weights(rows, kbuf[n].reshape(half, features), vbuf[n].reshape(half, features))
        wq_sum[...] += tn(rows, query_grad)
        bias_sum[0:1] += jnp.sum(query_grad.astype(jnp.float32), axis=0, keepdims=True)

    for u, total in ((0, wq_sum), (1, wk_sum), (2, wv_sum)):
        for quarter in range(4):
            shares[u, quarter] = total[quarter * part : (quarter + 1) * part].astype(shares.dtype)
        reducer.begin(staged + u)
    small[...] = small_in[...]
    for quarter in range(4):
        lanes = slice(quarter * part, (quarter + 1) * part)
        small[quarter, 0:2, :part] = bias_sum[0:2, lanes]
    mover.send_small()

    ticks = iter(range(reducer.steps()))
    waiting = list(range(EARLY * sources, capacity * sources))

    def advance():
        tick = next(ticks)
        reducer.step(tick)
        wave = PACE[tick] if tick < len(PACE) else 0
        for n in waiting[:wave]:
            mover.send_random(1 + (me + n % sources) % sources, (n // sources,))
        del waiting[:wave]
        return tick + 1

    advance()
    advance()
    for u in range(staged, reducer.units):
        reducer.join_sib(u)
    mover.pass_small()

    for n in range(2):
        stage_load(n).wait()
        stage[n] = (
            stage[n]
            + nt(qbuf[n].reshape(half, features), wq_ref[...])
            + nt(kbuf[n].reshape(half, features), wk_ref[...])
            + nt(vbuf[n].reshape(half, features), wv_ref[...])
        )
        stage_store(n).start()
        advance()
    while advance() < reducer.steps():
        pass
    for n in range(2):
        stage_store(n).wait()
    mover.end_small()
    reducer.finish()
    mover.finish()


def backward_tail(
    dq,
    dk,
    dv,
    ext_rows,
    stream_grad,
    outer_grad,
    inner_grad,
    output_grad,
    wq,
    wk,
    wv,
    small,
    count,
    capacity,
):
    blocks, block_rows, features = dq.shape
    tail = (block_rows, features)
    far_slots = (count - 2) * capacity
    part = features // 4
    outs, sems = returner_shapes(count, capacity, tail, small)
    units = outer_grad.shape[1] // part + inner_grad.shape[2] // features + 4
    sums, sum_scratch = reducer_shapes(units, part, features)
    kind = jnp.bfloat16
    dma = pltpu.SemaphoreType.DMA
    square = pltpu.VMEM((features, features), jnp.float32)
    some = pltpu.VMEM((2, capacity) + tail, kind)
    return pl.pallas_call(
        functools.partial(tail_kernel, count, capacity),
        out_shape=outs + [jax.ShapeDtypeStruct(stream_grad.shape, jnp.float32), sums],
        in_specs=[HBM_SPEC] * 8 + [VMEM_SPEC] * 4,
        out_specs=RETURN_SPECS + [HBM_SPEC, VMEM_SPEC],
        scratch_shapes=[some] * 4
        + [square] * 3
        + [
            pltpu.VMEM((3, 4, part, features), kind),
            pltpu.VMEM((far_slots,) + tail, kind),
            pltpu.VMEM((EXTRA,) + tail, kind),
            pltpu.VMEM((2, blocks * block_rows // 2, features), jnp.float32),
            pltpu.VMEM(small.shape, jnp.float32),
            pltpu.VMEM((8, features), jnp.float32),
            dma((2, 3)),
            dma((2,)),
            dma((2, 2)),
        ]
        + sems
        + sum_scratch,
        compiler_params=pltpu.CompilerParams(
            collective_id=1, has_side_effects=True, vmem_limit_bytes=58 * MIB
        ),
        cost_estimate=lasting(150),
        name="backward_tail",
    )(
        dq,
        dk,
        dv,
        ext_rows,
        stream_grad,
        outer_grad,
        inner_grad,
        output_grad,
        wq,
        wk,
        wv,
        small,
    )


def unpack_kernel(
    capacity, picked_ref, filled_ref, edge_ref, base_ref, back_ref, rim_ref, glob_ref, out_ref, acc
):
    step = pl.program_id(0)
    blocks = base_ref.shape[0]

    @pl.when(step == 0)
    def _():
        acc[...] = base_ref[...]

        @pl.when(edge_ref[0] == 0)
        def _():
            acc[0] += rim_ref[0].astype(jnp.float32)

        @pl.when(edge_ref[1] == 0)
        def _():
            acc[blocks - 1] += rim_ref[1].astype(jnp.float32)

    for k in range(capacity):
        slot = step * capacity + k

        @pl.when(filled_ref[slot] == 1)
        def _():
            acc[picked_ref[slot]] += back_ref[0, k].astype(jnp.float32)

    for which, block in ((0, 0), (1, blocks - 1)):

        @pl.when(edge_ref[which] == 1)
        def _():
            acc[block] += glob_ref[0].astype(jnp.float32)

    @pl.when(step == pl.num_programs(0) - 1)
    def _():
        out_ref[...] = acc[...].astype(out_ref.dtype)


def unpack_grads(base, back, rim, glob, picked, filled, edge):
    count, capacity = back.shape[:2]
    blocks, block_rows, features = base.shape
    return pl.pallas_call(
        functools.partial(unpack_kernel, capacity),
        out_shape=jax.ShapeDtypeStruct(base.shape, jnp.bfloat16),
        grid_spec=pltpu.PrefetchScalarGridSpec(
            num_scalar_prefetch=3,
            grid=(count,),
            in_specs=[
                pl.BlockSpec(base.shape, lambda i, *t: (0, 0, 0)),
                pl.BlockSpec((1,) + back.shape[1:], lambda i, *t: (i, 0, 0, 0)),
                pl.BlockSpec(rim.shape, lambda i, *t: (0, 0, 0)),
                pl.BlockSpec((1, block_rows, features), lambda i, *t: (i, 0, 0)),
            ],
            out_specs=pl.BlockSpec(base.shape, lambda i, *t: (0, 0, 0)),
            scratch_shapes=[pltpu.VMEM(base.shape, jnp.float32)],
        ),
        compiler_params=pltpu.CompilerParams(vmem_limit_bytes=58 * MIB),
        name="unpack_grads",
    )(picked, filled, edge, base, back, rim, glob)


def head_mask():
    rows = lax.broadcasted_iota(jnp.int32, (LANES, LANES), 0) // HD
    columns = lax.broadcasted_iota(jnp.int32, (LANES, LANES), 1) // HD
    return rows == columns


def spread_heads(block, mask):
    tiled = jnp.concatenate([block] * PACKED, axis=0)
    return jnp.where(mask, tiled, jnp.zeros_like(tiled))


def fold_heads(square, mask):
    kept = jnp.where(mask, square, 0.0)
    total = kept[:BLK]
    for i in range(1, PACKED):
        total = total + kept[i * BLK : (i + 1) * BLK]
    return total


def listed_rows(ref, index_ref, b):
    return jnp.concatenate([ref[index_ref[b * LISTED + j]] for j in range(LISTED)], axis=0)


def nt(left, right):
    return lax.dot_general(
        left, right, (((1,), (1,)), ((), ())), preferred_element_type=jnp.float32
    )


def nn(left, right):
    return jnp.dot(left, right, preferred_element_type=jnp.float32)


def tn(left, right):
    return lax.dot_general(
        left, right, (((0,), (0,)), ((), ())), preferred_element_type=jnp.float32
    )


def mask_edges(scores, edge_ref, b, blocks):
    low = jnp.logical_and(b == 0, edge_ref[0] == 1)
    high = jnp.logical_and(b == blocks - 1, edge_ref[1] == 1)
    first = jnp.where(low, NEG_FILL, scores[:BLK])
    third = jnp.where(high, NEG_FILL, scores[2 * BLK : 3 * BLK])
    return jnp.concatenate([first, scores[BLK : 2 * BLK], third, scores[3 * BLK :]], axis=0)


def forward_kernel(index_ref, edge_ref, q_ref, k_ref, v_ref, o_ref, log_ref):
    blocks = q_ref.shape[0]
    mask = head_mask()

    @pl.loop(0, blocks, unroll=True)
    def _(b):
        query = spread_heads(q_ref[b] * HD**-0.5, mask)
        scores = mask_edges(nt(listed_rows(k_ref, index_ref, b), query), edge_ref, b, blocks)
        top = jnp.max(scores, axis=0, keepdims=True)
        raised = jnp.exp(scores - top)
        total = jnp.sum(raised, axis=0, keepdims=True)
        probs = (raised * (1.0 / total)).astype(jnp.bfloat16)
        log_ref[b] = top + jnp.log(total)
        mixed = tn(probs, listed_rows(v_ref, index_ref, b))
        o_ref[b] = fold_heads(mixed, mask).astype(o_ref.dtype)


def attend(queries, keys, values, index, edge):
    blocks, block_rows, features = queries.shape
    slots = keys.shape[0]
    groups = features // LANES
    column = lambda g, *t: (0, 0, g)
    return pl.pallas_call(
        forward_kernel,
        out_shape=[
            jax.ShapeDtypeStruct(queries.shape, jnp.bfloat16),
            jax.ShapeDtypeStruct((blocks, 1, features), jnp.float32),
        ],
        grid_spec=pltpu.PrefetchScalarGridSpec(
            num_scalar_prefetch=2,
            grid=(groups,),
            in_specs=[
                pl.BlockSpec((blocks, block_rows, LANES), column),
                pl.BlockSpec((slots, block_rows, LANES), column),
                pl.BlockSpec((slots, block_rows, LANES), column),
            ],
            out_specs=[
                pl.BlockSpec((blocks, block_rows, LANES), column),
                pl.BlockSpec((blocks, 1, LANES), column),
            ],
        ),
        compiler_params=pltpu.CompilerParams(vmem_limit_bytes=58 * MIB),
        cost_estimate=lasting(37),
        name="attend",
    )(index, edge, queries, keys, values)


def backward_kernel(
    index_ref,
    edge_ref,
    q_ref,
    g_ref,
    k_ref,
    v_ref,
    log_ref,
    dq_ref,
    dk_ref,
    dv_ref,
    key_sum,
    value_sum,
):
    blocks = q_ref.shape[0]
    near = blocks + EXTRA
    mask = head_mask()
    key_sum[...] = jnp.zeros_like(key_sum)
    value_sum[...] = jnp.zeros_like(value_sum)
    dk_ref[...] = jnp.zeros_like(dk_ref)
    dv_ref[...] = jnp.zeros_like(dv_ref)

    @pl.loop(0, blocks, unroll=True)
    def _(b):
        query = spread_heads(q_ref[b] * HD**-0.5, mask)
        upstream = spread_heads(g_ref[b], mask)
        key_rows = listed_rows(k_ref, index_ref, b)
        scores = mask_edges(nt(key_rows, query), edge_ref, b, blocks)
        probs = jnp.exp(scores - log_ref[b])
        prob_grad = nt(listed_rows(v_ref, index_ref, b), upstream)
        delta = jnp.sum(probs * prob_grad, axis=0, keepdims=True)
        score_grad = (probs * (prob_grad - delta)).astype(jnp.bfloat16)
        value_grad = nn(probs.astype(jnp.bfloat16), upstream)
        key_grad = nn(score_grad, query)
        query_grad = fold_heads(tn(score_grad, key_rows), mask) * HD**-0.5
        dq_ref[b] = query_grad.astype(dq_ref.dtype)
        for j in range(LISTED):
            slot = index_ref[b * LISTED + j]
            piece = slice(j * BLK, (j + 1) * BLK)
            if j < 5:
                key_sum[slot] += key_grad[piece]
                value_sum[slot] += value_grad[piece]
            else:
                dk_ref[slot] = key_grad[piece].astype(dk_ref.dtype)
                dv_ref[slot] = value_grad[piece].astype(dv_ref.dtype)

    dk_ref[:near] = key_sum[...].astype(dk_ref.dtype)
    dv_ref[:near] = value_sum[...].astype(dv_ref.dtype)


def attend_back(queries, upstream, keys, values, log_total, index, edge):
    blocks, block_rows, features = queries.shape
    slots = keys.shape[0]
    groups = features // LANES
    column = lambda g, *t: (0, 0, g)
    few = pl.BlockSpec((blocks, block_rows, LANES), column)
    many = pl.BlockSpec((slots, block_rows, LANES), column)
    return pl.pallas_call(
        backward_kernel,
        out_shape=[
            jax.ShapeDtypeStruct(queries.shape, jnp.bfloat16),
            jax.ShapeDtypeStruct(keys.shape, jnp.bfloat16),
            jax.ShapeDtypeStruct(keys.shape, jnp.bfloat16),
        ],
        grid_spec=pltpu.PrefetchScalarGridSpec(
            num_scalar_prefetch=2,
            grid=(groups,),
            in_specs=[few, few, many, many, pl.BlockSpec((blocks, 1, LANES), column)],
            out_specs=[few, many, many],
            scratch_shapes=[
                pltpu.VMEM((blocks + EXTRA, block_rows, LANES), jnp.float32),
                pltpu.VMEM((blocks + EXTRA, block_rows, LANES), jnp.float32),
            ],
        ),
        compiler_params=pltpu.CompilerParams(vmem_limit_bytes=58 * MIB),
        cost_estimate=lasting(44),
        name="attend_back",
    )(index, edge, queries, upstream, keys, values, log_total)


def project_kernel(rows_ref, wk_ref, wv_ref, bias_ref, k_ref, v_ref):
    count, block_rows, features = rows_ref.shape
    rows = rows_ref[...].reshape(count * block_rows, features)
    k_ref[...] = nn(rows, wk_ref[...]).astype(k_ref.dtype).reshape(k_ref.shape)
    values = nn(rows, wv_ref[...]) + bias_ref[...]
    v_ref[...] = values.astype(v_ref.dtype).reshape(v_ref.shape)


def project(rows, wk, wv, bias):
    slots = rows.shape[0]
    step = max(n for n in range(1, 21) if slots % n == 0)
    by_row = pl.BlockSpec((step,) + rows.shape[1:], lambda i: (i, 0, 0))
    whole = pl.BlockSpec(wk.shape, lambda i: (0, 0))
    return pl.pallas_call(
        project_kernel,
        grid=(slots // step,),
        out_shape=[jax.ShapeDtypeStruct(rows.shape, jnp.bfloat16)] * 2,
        in_specs=[by_row, whole, whole, pl.BlockSpec(bias.shape, lambda i: (0, 0))],
        out_specs=[by_row, by_row],
        compiler_params=pltpu.CompilerParams(vmem_limit_bytes=58 * MIB),
        cost_estimate=lasting(13),
        name="project",
    )(rows, wk, wv, bias)


def layer_norm(hidden, gain, shift):
    center = hidden - jnp.mean(hidden, axis=-1, keepdims=True)
    inverse = lax.rsqrt(jnp.mean(center * center, axis=-1, keepdims=True) + EPSILON)
    normal = center * inverse
    return (normal * gain + shift, normal, inverse)


def norm_back(upstream, normal, inverse, gain):
    scaled = upstream * gain
    return inverse * (
        scaled
        - jnp.mean(scaled, axis=-1, keepdims=True)
        - normal * jnp.mean(scaled * normal, axis=-1, keepdims=True)
    )


def erf_f32(x):
    return lax.erf(x)


def mid_kernel(
    chunk,
    mixed_ref,
    rows_ref,
    cot_ref,
    vec_ref,
    inner_bias_ref,
    wo_ref,
    w1_ref,
    w2_ref,
    final_ref,
    stream_grad_ref,
    mixed_grad_ref,
    normed_ref,
    act_ref,
    outer_grad_ref,
    inner_grad_ref,
    att_grad_ref,
    sums_ref,
    inner_sums_ref,
    slope,
):
    @pl.when(pl.program_id(0) == 0)
    def _():
        sums_ref[...] = jnp.zeros_like(sums_ref)
        inner_sums_ref[...] = jnp.zeros_like(inner_sums_ref)

    def vector(i):
        return vec_ref[i : i + 1]

    def tally(i, value):
        sums_ref[i : i + 1] += jnp.sum(value, axis=0, keepdims=True)

    hidden = w1_ref.shape[1]
    pieces = [slice(at, at + chunk) for at in range(0, hidden, chunk)]
    attention = nn(mixed_ref[...], wo_ref[...]) + vector(2)
    stream = rows_ref[...].astype(jnp.float32) + attention
    tally(6, stream * stream)
    tally(7, attention * attention)
    first_gain = vector(3)
    normed, first_normal, first_inverse = layer_norm(stream, first_gain, vector(4))
    normed_bf = normed.astype(jnp.bfloat16)
    normed_ref[...] = normed_bf
    outer = jnp.zeros_like(normed)
    for piece in pieces:
        inner = nn(normed_bf, w1_ref[:, piece]) + inner_bias_ref[:, piece]
        cumulative = 0.5 * (1.0 + erf_f32(inner * (1.0 / math.sqrt(2.0))))
        density = jnp.exp(-0.5 * inner * inner) * (1.0 / math.sqrt(2.0 * math.pi))
        slope[:, piece] = cumulative + inner * density
        active = (inner * cumulative).astype(jnp.bfloat16)
        act_ref[:, piece] = active
        outer = outer + nn(active, w2_ref[piece])
    second_gain = vector(6)
    final, second_normal, second_inverse = layer_norm(
        normed + (outer + vector(5)), second_gain, vector(7)
    )
    final_ref[...] = final.astype(final_ref.dtype)
    upstream = cot_ref[...].astype(jnp.float32)
    tally(4, upstream * second_normal)
    tally(5, upstream)
    second_grad = norm_back(upstream, second_normal, second_inverse, second_gain)
    outer_grad = second_grad.astype(jnp.bfloat16)
    outer_grad_ref[...] = outer_grad
    tally(3, outer_grad.astype(jnp.float32))
    normed_grad = second_grad
    for piece in pieces:
        inner_grad = (nt(outer_grad, w2_ref[piece]) * slope[:, piece]).astype(jnp.bfloat16)
        inner_grad_ref[:, piece] = inner_grad
        inner_sums_ref[:, piece] += jnp.sum(
            inner_grad.astype(jnp.float32), axis=0, keepdims=True
        )
        normed_grad = normed_grad + nt(inner_grad, w1_ref[:, piece])
    tally(1, normed_grad * first_normal)
    tally(2, normed_grad)
    stream_grad = norm_back(normed_grad, first_normal, first_inverse, first_gain)
    stream_grad_ref[...] = stream_grad
    att_grad = stream_grad.astype(jnp.bfloat16)
    att_grad_ref[...] = att_grad
    tally(0, att_grad.astype(jnp.float32))
    mixed_grad = nt(att_grad, wo_ref[...]).astype(jnp.bfloat16)
    mixed_grad_ref[...] = mixed_grad


def middle(mixed, rows, cotangent, vectors, inner_bias, wo, w1, w2):
    length, features = rows.shape
    hidden = w1.shape[1]
    block = min(MID_ROWS, length)
    by_row = pl.BlockSpec((block, features), lambda i: (i, 0))
    wide = pl.BlockSpec((block, hidden), lambda i: (i, 0))

    def whole(array):
        return pl.BlockSpec(array.shape, lambda i: (0, 0), pipeline_mode=pl.Buffered(1))

    narrow_bf = jax.ShapeDtypeStruct((length, features), jnp.bfloat16)
    wide_bf = jax.ShapeDtypeStruct((length, hidden), jnp.bfloat16)
    return pl.pallas_call(
        functools.partial(mid_kernel, MID_CHUNK),
        grid=(length // block,),
        out_shape=[
            narrow_bf,
            jax.ShapeDtypeStruct((length, features), jnp.float32),
            narrow_bf,
            narrow_bf,
            wide_bf,
            narrow_bf,
            wide_bf,
            narrow_bf,
            jax.ShapeDtypeStruct((8, features), jnp.float32),
            jax.ShapeDtypeStruct((1, hidden), jnp.float32),
        ],
        in_specs=[
            by_row,
            by_row,
            by_row,
            whole(vectors),
            whole(inner_bias),
            whole(wo),
            whole(w1),
            whole(w2),
        ],
        out_specs=[
            by_row,
            by_row,
            by_row,
            by_row,
            wide,
            by_row,
            wide,
            by_row,
            pl.BlockSpec((8, features), lambda i: (0, 0)),
            pl.BlockSpec((1, hidden), lambda i: (0, 0)),
        ],
        scratch_shapes=[pltpu.VMEM((block, hidden), jnp.float32)],
        compiler_params=pltpu.CompilerParams(vmem_limit_bytes=56 * MIB),
        cost_estimate=lasting(50),
        name="middle",
    )(mixed, rows, cotangent, vectors, inner_bias, wo, w1, w2)


def outer_product(left, right):
    return jnp.einsum("ta,tb->ab", left, right, preferred_element_type=jnp.float32)


def back_product(upstream, weight):
    return jnp.einsum("tb,ab->ta", upstream, weight, preferred_element_type=jnp.float32)


def column_sum(upstream):
    return jnp.sum(upstream.astype(jnp.float32), axis=0)


def shards(
    tokens,
    cotangent,
    random_blocks,
    query_weight,
    query_bias,
    key_weight,
    value_weight,
    value_bias,
    output_weight,
    output_bias,
    first_gain,
    first_shift,
    inner_weight,
    inner_bias,
    outer_weight,
    outer_bias,
    second_gain,
    second_shift,
):
    token_rows = tokens[0]
    length, features = token_rows.shape
    blocks_here = length // BLK
    count = lax.axis_size("ctx")
    groups = lax.axis_size("wsh")
    own_index = lax.axis_index("ctx")
    capacity = (3 * blocks_here + count - 3) // (count - 2)
    part = features // groups
    inner_parts = inner_bias.shape[0] // part

    small = jnp.concatenate(
        (
            query_bias,
            value_bias,
            output_bias,
            first_gain,
            first_shift,
            outer_bias,
            second_gain,
            second_shift,
            inner_bias,
        )
    )
    small = jnp.pad(small, (0, (-small.shape[0]) % 2048)).reshape(-1, 128)

    source, within, ranking = request_tables(random_blocks[0], count, blocks_here)
    filled, picked = send_slots(source, within, ranking, own_index, capacity)
    filled, picked = filled.reshape(-1), picked.reshape(-1)
    own_source = lax.dynamic_index_in_dim(source, own_index, 0, keepdims=False)
    own_rank = lax.dynamic_index_in_dim(ranking, own_index, 0, keepdims=False)
    index = key_slots(own_source, own_rank, blocks_here, capacity).reshape(-1)
    edge = jnp.stack([own_index == 0, own_index == count - 1]).astype(jnp.int32)

    row_blocks = token_rows.reshape(blocks_here, BLK, features)
    pack = pack_blocks(row_blocks, picked).reshape(count, capacity, BLK, features)
    ext_rows, fulls = spread(
        pack,
        row_blocks,
        (
            query_weight,
            key_weight,
            value_weight,
            output_weight,
            inner_weight,
            outer_weight,
            small,
        ),
        count,
        capacity,
    )
    full_query, full_key, full_value, full_output, full_inner, full_outer = (
        full.reshape(-1, full.shape[-1]) for full in fulls[:6]
    )
    gathered = fulls[6].reshape(groups, -1).astype(jnp.float32)
    vectors = gathered[:, : 8 * part].reshape(groups, 8, part)
    vectors = jnp.transpose(vectors, (1, 0, 2)).reshape(8, features)
    full_inner_bias = gathered[:, 8 * part : (8 + inner_parts) * part].reshape(1, -1)

    slots = ext_rows.shape[0]
    ext_flat = ext_rows.reshape(slots * BLK, features)
    queries_bf = (
        jnp.dot(token_rows, full_query, preferred_element_type=jnp.float32) + vectors[0]
    ).astype(jnp.bfloat16)
    query_blocks = queries_bf.reshape(blocks_here, BLK, features)
    key_blocks, value_blocks = project(ext_rows, full_key, full_value, vectors[1:2])
    mixed_blocks, log_total = attend(query_blocks, key_blocks, value_blocks, index, edge)
    mixed_bf = mixed_blocks.reshape(length, features)

    (
        final,
        stream_grad,
        mixed_grad_bf,
        normed_bf,
        activated_bf,
        outer_grad_bf,
        inner_grad_bf,
        attention_grad_bf,
        middle_sums,
        inner_bias_grad,
    ) = middle(
        mixed_bf,
        token_rows,
        cotangent[0],
        vectors,
        full_inner_bias,
        full_output,
        full_inner,
        full_outer,
    )
    output_weight_grad = outer_product(mixed_bf, attention_grad_bf)
    inner_weight_grad = outer_product(normed_bf, inner_grad_bf)
    outer_weight_grad = outer_product(activated_bf, outer_grad_bf)
    square_sums = jnp.sum(middle_sums[6:8], axis=1)

    fused = count == 8 and 3 * blocks_here == capacity * (count - 2)

    def small_parts(query_row, value_row):
        rows = jnp.concatenate([query_row, value_row, middle_sums[:6]], axis=0)
        parts = jnp.concatenate(
            [
                jnp.transpose(rows.reshape(8, groups, part), (1, 0, 2)),
                inner_bias_grad.reshape(groups, inner_parts, part),
                jnp.broadcast_to(
                    jnp.pad(square_sums, (0, part - 2)).reshape(1, 1, part), (groups, 1, part)
                ),
            ],
            axis=1,
        )
        return jnp.pad(parts, ((0, 0), (0, (-parts.shape[1]) % 8), (0, (-part) % 128)))

    mixed_grad_blocks = mixed_grad_bf.reshape(blocks_here, BLK, features)
    dq_blocks, dk_blocks, dv_blocks = attend_back(
        query_blocks, mixed_grad_blocks, key_blocks, value_blocks, log_total, index, edge
    )
    if fused:
        empty = jnp.zeros((1, features), jnp.float32)
        back, rim, glob, small_sums, near_grad, unit_sums = backward_tail(
            dq_blocks,
            dk_blocks,
            dv_blocks,
            ext_rows,
            stream_grad,
            outer_weight_grad.astype(jnp.bfloat16).reshape(groups, -1, features),
            inner_weight_grad.astype(jnp.bfloat16).reshape(groups, part, -1),
            output_weight_grad.astype(jnp.bfloat16).reshape(groups, part, features),
            full_query,
            full_key,
            full_value,
            small_parts(empty, empty),
            count,
            capacity,
        )
        stacked = full_outer.shape[0] // features
        across = full_inner.shape[1] // features
        units = unit_sums.reshape(-1, part, features).astype(jnp.float32)
        sums = [units[stacked + across + i] for i in (1, 2, 3, 0)] + [
            jnp.concatenate([units[stacked + i] for i in range(across)], axis=1),
            units[:stacked].reshape(-1, features),
        ]
    else:
        dq = dq_blocks.reshape(length, features)
        dk = dk_blocks.reshape(slots * BLK, features)
        dv = dv_blocks.reshape(slots * BLK, features)
        far_grad = (
            (back_product(dk[length:], full_key) + back_product(dv[length:], full_value))
            .astype(jnp.bfloat16)
            .reshape(slots - blocks_here, BLK, features)
        )
        back, rim, glob, small_sums = return_grads(
            far_grad, small_parts(column_sum(dq)[None], column_sum(dv)[None]), count, capacity
        )
        near_grad = (
            stream_grad
            + back_product(dq, full_query)
            + back_product(dk[:length], full_key)
            + back_product(dv[:length], full_value)
        )
        sums = lax.psum(
            tuple(
                lax.psum_scatter(
                    grad.astype(jnp.bfloat16), "wsh", scatter_dimension=0, tiled=True
                )
                for grad in (
                    outer_product(token_rows, dq),
                    outer_product(ext_flat, dk),
                    outer_product(ext_flat, dv),
                    output_weight_grad,
                    inner_weight_grad,
                    outer_weight_grad,
                )
            ),
            "ctx",
        )
        sums = [total.astype(jnp.float32) for total in sums]
    tokens_grad = unpack_grads(
        near_grad.reshape(blocks_here, BLK, features), back, rim, glob, picked, filled, edge
    )
    element_count = count * groups * length * features
    stream_rms = jnp.sqrt(small_sums[8 + inner_parts, :2] / element_count)
    (
        query_bias_grad,
        value_bias_grad,
        output_bias_grad,
        first_gain_grad,
        first_shift_grad,
        outer_bias_grad,
        second_gain_grad,
        second_shift_grad,
    ) = (small_sums[i, :part] for i in range(8))
    inner_bias_grad = small_sums[8 : 8 + inner_parts, :part].reshape(-1)
    query_weight_sum, key_weight_sum, value_weight_sum, output_weight_sum = sums[:4]
    return (
        final[None],
        tokens_grad.reshape(1, length, features),
        query_weight_sum,
        query_bias_grad,
        key_weight_sum,
        value_weight_sum,
        value_bias_grad,
        output_weight_sum,
        output_bias_grad,
        first_gain_grad,
        first_shift_grad,
        sums[4],
        inner_bias_grad,
        sums[5],
        outer_bias_grad,
        second_gain_grad,
        second_shift_grad,
        stream_rms,
    )


def solution(mesh):
    in_specs = (
        P("wsh", "ctx", None),
        P("wsh", "ctx", None),
        P("wsh", None, None),
        P("wsh", None),
        P("wsh"),
        P("wsh", None),
        P("wsh", None),
        P("wsh"),
        P("wsh", None),
        P("wsh"),
        P("wsh"),
        P("wsh"),
        P("wsh", None),
        P("wsh"),
        P("wsh", None),
        P("wsh"),
        P("wsh"),
        P("wsh"),
    )
    out_specs = (
        P("wsh", "ctx", None),
        P("wsh", "ctx", None),
        P("wsh", None),
        P("wsh"),
        P("wsh", None),
        P("wsh", None),
        P("wsh"),
        P("wsh", None),
        P("wsh"),
        P("wsh"),
        P("wsh"),
        P("wsh", None),
        P("wsh"),
        P("wsh", None),
        P("wsh"),
        P("wsh"),
        P("wsh"),
        P(),
    )
    return jax.shard_map(shards, mesh=mesh, in_specs=in_specs, out_specs=out_specs, check_vma=False)
```
